32 devices in a mesh: vid: 4 (over y, x), tok: 8 (over z, core).
Axes of the slice: x: 2, y: 2, z: 4, core: 2. Of those that a mesh axis runs over, the one named last changes fastest.
Arguments:
- frames: bfloat16 [8, 16, 224, 768], P('vid', None, 'tok'), may hold values from -6 to 6
- messages: bfloat16 [8, 16, 768], P('vid', None, 'tok'), may hold values from -6 to 6
- frame_counts: int32 [8], P('vid'), may hold values from 8 to 16, as said below
- cotangent: bfloat16 [8, 16, 224, 768], P('vid', None, 'tok'), may hold values from -6 to 6
- msg_gain: bfloat16 [768], replicated, may hold values from 0.5 to 1.5
- msg_shift: bfloat16 [768], replicated, may hold values from -1.25 to 1.25
- msg_in_w: bfloat16 [768, 2304], replicated, may hold values from -0.21875 to 0.21875
- msg_in_b: bfloat16 [2, 768], replicated, may hold values from -1.25 to 1.25
- msg_out_w: bfloat16 [768, 768], replicated, may hold values from -0.625 to 0.625
- msg_out_b: bfloat16 [768], replicated, may hold values from -1.25 to 1.25
- ln1_gain: bfloat16 [768], replicated, may hold values from 0.5 to 1.5
- ln1_shift: bfloat16 [768], replicated, may hold values from -1.25 to 1.25
- attn_in_w: bfloat16 [768, 2304], replicated, may hold values from -0.21875 to 0.21875
- attn_in_b: bfloat16 [2, 768], replicated, may hold values from -1.25 to 1.25
- attn_out_w: bfloat16 [768, 768], replicated, may hold values from -1.25 to 1.25
- attn_out_b: bfloat16 [768], replicated, may hold values from -1.25 to 1.25
- ln2_gain: bfloat16 [768], replicated, may hold values from 0.5 to 1.5
- ln2_shift: bfloat16 [768], replicated, may hold values from -1.25 to 1.25
- fc_w: bfloat16 [768, 3072], replicated, may hold values from -0.21875 to 0.21875
- fc_b: bfloat16 [3072], replicated, may hold values from -1.25 to 1.25
- proj_w: bfloat16 [3072, 768], replicated, may hold values from -0.109375 to 0.109375
- proj_b: bfloat16 [768], replicated, may hold values from -1.25 to 1.25
Outputs:
- output: bfloat16 [8, 16, 224, 768], P('vid', None, 'tok')
- frames_grad: bfloat16 [8, 16, 224, 768], P('vid', None, 'tok')
- messages_grad: bfloat16 [8, 16, 768], P('vid', None, 'tok')
- msg_gain_grad: float32 [768], P(('vid', 'tok'))
- msg_shift_grad: float32 [768], P(('vid', 'tok'))
- msg_in_w_grad: float32 [768, 2304], P(('vid', 'tok'))
- msg_in_b_grad: float32 [2, 768], P(None, ('vid', 'tok'))
- msg_out_w_grad: float32 [768, 768], P(('vid', 'tok'))
- msg_out_b_grad: float32 [768], P(('vid', 'tok'))
- ln1_gain_grad: float32 [768], P(('vid', 'tok'))
- ln1_shift_grad: float32 [768], P(('vid', 'tok'))
- attn_in_w_grad: float32 [768, 2304], P(('vid', 'tok'))
- attn_in_b_grad: float32 [2, 768], P(None, ('vid', 'tok'))
- attn_out_w_grad: float32 [768, 768], P(('vid', 'tok'))
- attn_out_b_grad: float32 [768], P(('vid', 'tok'))
- ln2_gain_grad: float32 [768], P(('vid', 'tok'))
- ln2_shift_grad: float32 [768], P(('vid', 'tok'))
- fc_w_grad: float32 [768, 3072], P(('vid', 'tok'))
- fc_b_grad: float32 [3072], P(('vid', 'tok'))
- proj_w_grad: float32 [3072, 768], P(('vid', 'tok'))
- proj_b_grad: float32 [768], P(('vid', 'tok'))
The draws below stay inside these ranges and needn't reach their ends.
Inputs may be any that keep to these rules, and one draw needn't show every extreme that they name: `frame_counts`: every entry is 8 or 16.
All inputs are finite; a program needn't handle non-finite values.
Results may differ from the reference program's by a relative error of at most 0.022.
Values may be sent and summed in bfloat16 or wider, within the bound.
No kernel may reach another device: no remote copies, remote signals or barrier semaphores. Data moves between devices by JAX's collectives and lax.ppermute only.
A program may use at most 256 MiB of HBM per device.

```python
from functools import partial
import jax
import jax.numpy as jnp
from jax import lax

D = 768
HEADS = 12
HEAD = 64
FF = 3072
PATCHES = 197
SLOTS = 224
FRAMES = 16
VIDS = 8


def draw_frame_counts(key, part):
    base_key = jax.random.fold_in(jax.random.fold_in(key, 7013), part)
    halves_key, full_key, short_key = jax.random.split(base_key, 3)
    drawn_halves = jax.random.randint(halves_key, (VIDS,), 1, 3)
    counts = FRAMES // 2 * drawn_halves
    position = jnp.arange(VIDS, dtype=jnp.int32)
    full_place = jax.random.randint(full_key, (), 0, VIDS)
    step_away = jax.random.randint(short_key, (), 1, VIDS)
    short_place = (full_place + step_away) % VIDS
    counts = jnp.where(position == full_place, FRAMES, counts)
    counts = jnp.where(position == short_place, FRAMES // 2, counts)
    return counts.astype(jnp.int32)


def shard_levels(rng, shape, cuts, smallest, top_value):
    def one(dim, blocks):
        draws = jax.random.uniform(jax.random.fold_in(jax.random.fold_in(rng, 6), dim), (blocks,), jnp.float32, smallest / len(cuts), top_value / len(cuts))
        return jnp.repeat(jnp.exp(draws), shape[dim] // blocks).reshape((-1,) + (1,) * (len(shape) - dim - 1))

    factor_of = one(*cuts[0])
    for cut in cuts[1:]:
        factor_of = factor_of * one(*cut)
    return factor_of


def gaussian(own_key, extent, scale, limit, cuts=(), held_as=jnp.bfloat16):
    drawn = scale * jax.random.normal(own_key, extent, jnp.float32)
    if cuts:
        drawn = drawn * shard_levels(own_key, extent, cuts, -0.22, 0.18)
    return jnp.clip(drawn, -limit, limit).astype(held_as)


def setup_inputs(seed: int = 0) -> dict:
    splits = jax.random.split(jax.random.key(seed), 23)
    frames = gaussian(splits[0], (VIDS, FRAMES, SLOTS, D), 1.0, 6.0, ((0, 4), (2, 8)))
    messages = gaussian(splits[1], (VIDS, FRAMES, D), 1.0, 6.0, ((0, 4), (2, 8)))
    frame_counts = draw_frame_counts(jax.random.fold_in(splits[22], 71), 0)
    cotangent = gaussian(splits[3], (VIDS, FRAMES, SLOTS, D), 1.0, 6.0, ((0, 4), (2, 8)))
    msg_gain = jnp.clip(1.0 + 0.1 * jax.random.normal(splits[4], (D,), jnp.float32), 0.5, 1.5).astype(jnp.bfloat16)
    msg_shift = gaussian(splits[5], (D,), 0.2, 1.25)
    msg_in_w = gaussian(splits[6], (D, 3 * D), D ** -0.5, 0.21875)
    msg_in_b = gaussian(splits[7], (2, D), 0.2, 1.25)
    msg_out_w = gaussian(splits[8], (D, D), (D // 8) ** -0.5, 0.625)
    msg_out_b = gaussian(splits[9], (D,), 0.2, 1.25)
    ln1_gain = jnp.clip(1.0 + 0.1 * jax.random.normal(splits[10], (D,), jnp.float32), 0.5, 1.5).astype(jnp.bfloat16)
    ln1_shift = gaussian(splits[11], (D,), 0.2, 1.25)
    attn_in_w = gaussian(splits[12], (D, 3 * D), D ** -0.5, 0.21875)
    attn_in_b = gaussian(splits[13], (2, D), 0.2, 1.25)
    attn_out_w = gaussian(splits[14], (D, D), (D // 32) ** -0.5, 1.25)
    attn_out_b = gaussian(splits[15], (D,), 0.2, 1.25)
    ln2_gain = jnp.clip(1.0 + 0.1 * jax.random.normal(splits[16], (D,), jnp.float32), 0.5, 1.5).astype(jnp.bfloat16)
    ln2_shift = gaussian(splits[17], (D,), 0.2, 1.25)
    fc_w = gaussian(splits[18], (D, FF), D ** -0.5, 0.21875)
    fc_b = gaussian(splits[19], (FF,), 0.2, 1.25)
    proj_w = gaussian(splits[20], (FF, D), FF ** -0.5, 0.109375)
    proj_b = gaussian(splits[21], (D,), 0.2, 1.25)
    return {"frames": frames, "messages": messages, "frame_counts": frame_counts, "cotangent": cotangent, "msg_gain": msg_gain, "msg_shift": msg_shift, "msg_in_w": msg_in_w, "msg_in_b": msg_in_b, "msg_out_w": msg_out_w, "msg_out_b": msg_out_b, "ln1_gain": ln1_gain, "ln1_shift": ln1_shift, "attn_in_w": attn_in_w, "attn_in_b": attn_in_b, "attn_out_w": attn_out_w, "attn_out_b": attn_out_b, "ln2_gain": ln2_gain, "ln2_shift": ln2_shift, "fc_w": fc_w, "fc_b": fc_b, "proj_w": proj_w, "proj_b": proj_b}


@jax.custom_vjp
def low(v):
    return lax.optimization_barrier(v.astype(jnp.bfloat16)).astype(jnp.float32)

@jax.custom_vjp
def low_back(v):
    return v

def low_keep(v):
    return (low(v), None)

def low_pass(kept, grad):
    return (grad,)

def back_keep(v):
    return (v, None)

def back_low(kept, grad):
    return (low(grad),)
low.defvjp(low_keep, low_pass)
low_back.defvjp(back_keep, back_low)
highest = lax.Precision.HIGHEST

def product(left_rows, right_rows):
    return jnp.dot(left_rows, right_rows, precision=highest)

def layer_norm(tensor, gain, shift):
    row_mean = lax.optimization_barrier(jnp.mean(tensor, axis=-1, keepdims=True))
    centred = tensor - row_mean
    spread = lax.optimization_barrier(jnp.mean(centred * centred, axis=-1, keepdims=True))
    return centred * lax.rsqrt(spread + 1e-05) * gain + shift

def qkv_bias(bias_pair):
    return jnp.concatenate([bias_pair[0], jnp.zeros_like(bias_pair[0]), bias_pair[1]])

def attend(query_rows, key_rows, value_rows, allowed):
    batch_count, row_count, feature = query_rows.shape
    heads_q = query_rows.reshape(batch_count, row_count, HEADS, HEAD)
    heads_k = key_rows.reshape(batch_count, key_rows.shape[1], HEADS, HEAD)
    heads_v = value_rows.reshape(batch_count, value_rows.shape[1], HEADS, HEAD)
    raw_score = jnp.einsum('bqhe,bkhe->bhqk', heads_q, heads_k, precision=highest) * HEAD ** (-0.5)
    raw_score = low_back(raw_score)
    scores = jnp.where(allowed[:, None], raw_score, -1000000000.0)
    weights = low(jax.nn.softmax(scores, axis=-1))
    mixed_rows = jnp.einsum('bhqk,bkhe->bqhe', weights, heads_v, precision=highest)
    return mixed_rows.reshape(batch_count, row_count, feature)

def message_update(params, allowed, message_rows):
    gain, shift, in_weight, in_bias, out_weight, out_bias = params
    feature = message_rows.shape[-1]
    normed = low(layer_norm(message_rows, gain, shift))
    joined = low(low_back(product(normed, in_weight) + qkv_bias(in_bias)))
    mixed_rows = attend(joined[None, :, :feature], joined[None, :, feature:2 * feature], joined[None, :, 2 * feature:], allowed[None])[0]
    mixed_rows = low(low_back(mixed_rows))
    return message_rows + low_back(product(mixed_rows, out_weight) + out_bias)

def frame_block(params, allowed_keys, pieces):
    frame_rows, message_rows = pieces
    ln1_gain, ln1_shift, attn_in_w, attn_in_b, attn_out_w, attn_out_b, ln2_gain, ln2_shift, fc_w, fc_b, proj_w, proj_b = params
    feature = frame_rows.shape[-1]
    tokens = jnp.concatenate([frame_rows, message_rows[:, None, :]], axis=1)
    normed = low(layer_norm(tokens, ln1_gain, ln1_shift))
    joined = low(low_back(jnp.einsum('fsd,dn->fsn', normed, attn_in_w, precision=highest) + qkv_bias(attn_in_b)))
    query_rows = joined[:, :SLOTS, :feature]
    key_rows = joined[:, :, feature:2 * feature]
    value_rows = joined[:, :, 2 * feature:]
    mixed_rows = low(low_back(attend(query_rows, key_rows, value_rows, allowed_keys)))
    residual = frame_rows + low_back(jnp.einsum('fsd,dn->fsn', mixed_rows, attn_out_w, precision=highest) + attn_out_b)
    hidden = low(layer_norm(residual, ln2_gain, ln2_shift))
    pre_act = low_back(jnp.einsum('fsd,dn->fsn', hidden, fc_w, precision=highest) + fc_b)
    active = low(pre_act * jax.nn.sigmoid(1.702 * pre_act))
    return residual + jnp.einsum('fsn,nd->fsd', active, proj_w, precision=highest) + proj_b

def forward(allowed, allowed_keys, frames, messages, *params):
    flat_rows = messages.reshape(VIDS * FRAMES, -1)
    updated = message_update(params[:6], allowed, flat_rows)
    block_fn = jax.checkpoint(partial(frame_block, params[6:], allowed_keys))
    return lax.map(block_fn, (frames, updated.reshape(VIDS, FRAMES, -1)))

def reference(frames, messages, frame_counts, cotangent, msg_gain, msg_shift, msg_in_w, msg_in_b, msg_out_w, msg_out_b, ln1_gain, ln1_shift, attn_in_w, attn_in_b, attn_out_w, attn_out_b, ln2_gain, ln2_shift, fc_w, fc_b, proj_w, proj_b):
    params = tuple((element.astype(jnp.float32) for element in (msg_gain, msg_shift, msg_in_w, msg_in_b, msg_out_w, msg_out_b, ln1_gain, ln1_shift, attn_in_w, attn_in_b, attn_out_w, attn_out_b, ln2_gain, ln2_shift, fc_w, fc_b, proj_w, proj_b)))
    message_index = jnp.arange(VIDS * FRAMES, dtype=jnp.int32)
    video_index = message_index // FRAMES
    count_each = frame_counts[video_index]
    live = message_index % FRAMES < count_each
    allowed = (video_index[:, None] == video_index[None, :]) & live[None, :]
    key_index = jnp.arange(SLOTS + 1, dtype=jnp.int32)
    allowed_keys = ((key_index < PATCHES) | (key_index == SLOTS))[None, None, :]
    result, pullback = jax.vjp(partial(forward, allowed, allowed_keys), frames.astype(jnp.float32), messages.astype(jnp.float32), *params)
    slot_live = jnp.arange(SLOTS, dtype=jnp.int32) < PATCHES
    keep_mask = live.reshape(VIDS, FRAMES)[:, :, None, None] & slot_live[None, None, :, None]
    gradients = pullback(jnp.where(keep_mask, cotangent.astype(jnp.float32), 0.0))
    return (result.astype(jnp.bfloat16), gradients[0].astype(jnp.bfloat16), gradients[1].astype(jnp.bfloat16), gradients[2], gradients[3], gradients[4], gradients[5], gradients[6], gradients[7], gradients[8], gradients[9], gradients[10], gradients[11], gradients[12], gradients[13], gradients[14], gradients[15], gradients[16], gradients[17], gradients[18], gradients[19])
```

```python
from functools import partial

import jax
import jax.numpy as jnp
from jax import lax
from jax.experimental import pallas as pl
from jax.experimental.pallas import tpu as pltpu
from jax.sharding import PartitionSpec as P

HEADS = 12
HEAD = 64
PATCHES = 197
PAIR = 2 * HEAD
EPS = 1e-05
NEG = -1000000000.0
SLOPE = 1.702
F32 = jnp.float32
BF16 = jnp.bfloat16
VMEM_CAP = 60 * 2**20

KEY_ROWS = (PATCHES + 1 + 15) // 16 * 16


def norm_parts(tensor):
    row_mean = jnp.mean(tensor, axis=-1, keepdims=True)
    centred = tensor - row_mean
    spread = jnp.mean(centred * centred, axis=-1, keepdims=True)
    inverse = lax.rsqrt(spread + EPS)
    return centred * inverse, inverse


def norm_back(grad_in, normed, inverse, gain):
    scaled = grad_in * gain
    return inverse * (
        scaled
        - jnp.mean(scaled, axis=-1, keepdims=True)
        - normed * jnp.mean(scaled * normed, axis=-1, keepdims=True)
    )


def dot_nn(left, right):
    return lax.dot_general(left, right, (((1,), (0,)), ((), ())), preferred_element_type=F32)


def dot_nt(left, right):
    return lax.dot_general(left, right, (((1,), (1,)), ((), ())), preferred_element_type=F32)


def dot_tn(left, right):
    return lax.dot_general(left, right, (((0,), (0,)), ((), ())), preferred_element_type=F32)


def lane_masks(dtype=BF16):
    lane = lax.broadcasted_iota(jnp.int32, (1, PAIR), 1)
    first = jnp.where(lane < HEAD, 1.0, 0.0)
    return first.astype(dtype), (1.0 - first).astype(dtype)


def column_sum(rows):
    return jnp.sum(rows, axis=0, keepdims=True)


def message_forward_kernel(
    msg_ref, allow_ref, gain_ref, shift_ref, in_w_ref, in_b_ref, out_w_ref, out_b_ref,
    joined_ref, mixed_ref, new_ref,
):
    feature = msg_ref.shape[1]
    message = msg_ref[...].astype(F32)
    normed, _ = norm_parts(message)
    hidden = (normed * gain_ref[...].astype(F32) + shift_ref[...].astype(F32)).astype(BF16)
    in_b = in_b_ref[...].astype(F32)
    for block in range(3):
        cols = slice(block * feature, (block + 1) * feature)
        part = dot_nn(hidden, in_w_ref[:, cols])
        if block != 1:
            part = part + in_b[block // 2 : block // 2 + 1]
        joined_ref[:, cols] = part.astype(BF16)
    allowed = allow_ref[...] > 0.5
    masks = lane_masks()
    scale = jnp.asarray(HEAD**-0.5, BF16)
    for pair in range(HEADS // 2):
        cols = slice(pair * PAIR, (pair + 1) * PAIR)
        query = joined_ref[:, cols]
        keys = joined_ref[:, feature + pair * PAIR : feature + (pair + 1) * PAIR]
        values = joined_ref[:, 2 * feature + pair * PAIR : 2 * feature + (pair + 1) * PAIR]
        total = None
        for mask in masks:
            score = dot_nt(query * (mask * scale), keys)
            score = jnp.where(allowed, score, NEG)
            weight = jnp.exp(score - jnp.max(score, axis=-1, keepdims=True))
            weight = weight / jnp.sum(weight, axis=-1, keepdims=True)
            part = dot_nn(weight.astype(BF16), values * mask)
            total = part if total is None else total + part
        mixed_ref[:, cols] = total.astype(BF16)
    new_ref[...] = message + (dot_nn(mixed_ref[...], out_w_ref[...]) + out_b_ref[...].astype(F32))


def message_backward_kernel(
    place_ref, msg_ref, allow_ref, low_ref, joined_ref, mixed_ref,
    gain_ref, shift_ref, in_w_ref, out_w_ref,
    grad_ref, in_w_grad_ref, out_w_grad_ref, vec_ref,
    mixed_grad_s, joined_grad_s,
):
    feature = msg_ref.shape[1]
    share = in_w_grad_ref.shape[0]
    message = msg_ref[...].astype(F32)
    normed, inverse = norm_parts(message)
    gain = gain_ref[...].astype(F32)
    hidden = (normed * gain + shift_ref[...].astype(F32)).astype(BF16)
    low = low_ref[...]
    mixed_grad_s[...] = dot_nt(low, out_w_ref[...]).astype(BF16)
    allowed = allow_ref[...] > 0.5
    masks = lane_masks()
    scale = jnp.asarray(HEAD**-0.5, BF16)
    for pair in range(HEADS // 2):
        cols = slice(pair * PAIR, (pair + 1) * PAIR)
        key_cols = slice(feature + pair * PAIR, feature + (pair + 1) * PAIR)
        value_cols = slice(2 * feature + pair * PAIR, 2 * feature + (pair + 1) * PAIR)
        query = joined_ref[:, cols]
        keys = joined_ref[:, key_cols]
        values = joined_ref[:, value_cols]
        grad = mixed_grad_s[:, cols]
        grad_q = grad_k = grad_v = None
        for mask in masks:
            query_one = query * (mask * scale)
            grad_one = grad * mask
            score = jnp.where(allowed, dot_nt(query_one, keys), NEG)
            weight = jnp.exp(score - jnp.max(score, axis=-1, keepdims=True))
            weight = weight / jnp.sum(weight, axis=-1, keepdims=True)
            grad_weight = dot_nt(grad_one, values)
            inner = jnp.sum(weight * grad_weight, axis=-1, keepdims=True)
            grad_score = (weight * (grad_weight - inner)).astype(BF16)
            one_q = dot_nn(grad_score, keys * (mask * scale))
            one_k = dot_tn(grad_score, query_one)
            one_v = dot_tn(weight.astype(BF16), grad_one)
            grad_q = one_q if grad_q is None else grad_q + one_q
            grad_k = one_k if grad_k is None else grad_k + one_k
            grad_v = one_v if grad_v is None else grad_v + one_v
        joined_grad_s[:, cols] = grad_q.astype(BF16)
        joined_grad_s[:, key_cols] = grad_k.astype(BF16)
        joined_grad_s[:, value_cols] = grad_v.astype(BF16)
    joined_grad = joined_grad_s[...]
    hidden_grad = dot_nt(joined_grad, in_w_ref[...])
    low_wide = low.astype(F32)
    grad_ref[...] = (low_wide + norm_back(hidden_grad, normed, inverse, gain)).astype(BF16)
    width = (share + 127) // 128 * 128
    row = lax.broadcasted_iota(jnp.int32, (feature, width), 0)
    col = lax.broadcasted_iota(jnp.int32, (feature, width), 1)
    pick = jnp.where((row == col + place_ref[0]) & (col < share), 1.0, 0.0)
    pick_low = pick.astype(BF16)
    own_hidden = dot_nn(hidden, pick_low).astype(BF16)
    own_mixed = dot_nn(mixed_ref[...], pick_low).astype(BF16)
    in_w_grad_ref[...] = dot_tn(own_hidden, joined_grad)[:share]
    out_w_grad_ref[...] = dot_tn(own_mixed, low)[:share]
    sums = jnp.concatenate(
        [
            column_sum(hidden_grad * normed),
            column_sum(hidden_grad),
            column_sum(joined_grad[:, :feature].astype(F32)),
            column_sum(joined_grad[:, 2 * feature :].astype(F32)),
            column_sum(low_wide),
            jnp.zeros((3, feature), F32),
        ],
        axis=0,
    )
    vec_ref[...] = lax.dot_general(
        sums, pick, (((1,), (0,)), ((), ())), precision=lax.Precision.HIGHEST, preferred_element_type=F32
    )


def frame_rows(block_ref, scratch, frame=0):
    sources, _, slots, _ = block_ref.shape
    for source in range(sources):
        scratch[source * slots : (source + 1) * slots, :] = block_ref[source, frame].astype(F32)


def attention_forward_kernel(
    x_ref, new_ref, gain_ref, shift_ref, in_w_ref, in_b_ref, out_w_ref, out_b_ref,
    query_ref, keyval_ref, mixed_ref, lse_ref, resid_ref,
    rows_s,
):
    feature = x_ref.shape[3]
    slot_count = rows_s.shape[0]
    frame_rows(x_ref, rows_s)
    gain = gain_ref[...].astype(F32)
    shift = shift_ref[...].astype(F32)
    frame_in = rows_s[...]
    normed, _ = norm_parts(frame_in)
    hidden = normed * gain + shift
    msg_normed, _ = norm_parts(new_ref[0])
    msg_hidden = msg_normed * gain + shift
    key_row = lax.broadcasted_iota(jnp.int32, (KEY_ROWS, 1), 0)
    hidden_kv = jnp.where(key_row == PATCHES, msg_hidden, hidden[:KEY_ROWS]).astype(BF16)
    hidden = hidden.astype(BF16)
    in_b = in_b_ref[...].astype(F32)
    query_ref[0] = (dot_nn(hidden, in_w_ref[:, :feature]) + in_b[0:1]).astype(BF16)
    keyval_ref[0, :, :feature] = dot_nn(hidden_kv, in_w_ref[:, feature : 2 * feature]).astype(BF16)
    keyval_ref[0, :, feature:] = (
        dot_nn(hidden_kv, in_w_ref[:, 2 * feature :]) + in_b[1:2]
    ).astype(BF16)
    allowed = key_row <= PATCHES
    masks = lane_masks()
    scale = jnp.asarray(HEAD**-0.5, BF16)
    for pair in range(HEADS // 2):
        cols = slice(pair * PAIR, (pair + 1) * PAIR)
        query = query_ref[0, :, cols]
        keys = keyval_ref[0, :, cols]
        values = keyval_ref[0, :, feature + pair * PAIR : feature + (pair + 1) * PAIR]
        total = None
        for side, mask in enumerate(masks):
            score = dot_nt(keys, query * (mask * scale))
            score = jnp.where(allowed, score, NEG)
            peak = jnp.max(score, axis=0, keepdims=True)
            weight = jnp.exp(score - peak)
            norm = jnp.sum(weight, axis=0, keepdims=True)
            lse_ref[0, 2 * pair + side : 2 * pair + side + 1, :] = peak + jnp.log(norm)
            weight = (weight * (1.0 / norm)).astype(BF16)
            part = dot_tn(weight, values * mask)
            total = part if total is None else total + part
        mixed_ref[0, :, cols] = total.astype(BF16)
    resid_ref[0] = rows_s[...] + (
        dot_nn(mixed_ref[0], out_w_ref[...]) + out_b_ref[...].astype(F32)
    )


def store_share(value, keep_ref, send_ref, table_ref, vids, tail):
    depth = keep_ref.shape[1]
    share = keep_ref.shape[-2]
    low_core = table_ref[2 * vids] == 0
    for vid in range(vids):
        for level in range(depth):
            at = ((vid * depth + level) * 2) * share
            first = value[at : at + share].astype(BF16)
            second = value[at + share : at + 2 * share].astype(BF16)
            keep_ref[(table_ref[vid], level) + tail] = jnp.where(low_core, first, second)
            send_ref[(table_ref[vids + vid], level) + tail] = jnp.where(low_core, second, first)


def feed_forward_kernel(
    packed, vids, table_ref, live_ref,
    resid_ref, cot_ref, gain_ref, shift_ref, fc_w_ref, fc_b_ref, proj_w_ref, proj_b_ref,
    *refs,
):
    if packed:
        out_ref, resid_grad_ref, vec_ref, proj_keep, proj_send, fc_keep, fc_send = refs[:7]
    else:
        out_ref, resid_grad_ref, vec_ref, proj_grad_ref, fc_grad_ref = refs[:5]
    hidden_s, hidden_low_s, grad_s, act_s, pre_grad_s, out_s, hidden_grad_s, rows_s = refs[-8:]
    step = pl.program_id(0)
    frames, slot_count, feature = resid_ref.shape
    gain = gain_ref[...].astype(F32)

    @pl.when(step == 0)
    def _():
        vec_ref[...] = jnp.zeros_like(vec_ref)
        row = lax.broadcasted_iota(jnp.int32, (KEY_ROWS, 1), 0)
        for frame in range(frames):
            normed, _ = norm_parts(resid_ref[frame])
            hidden = (normed * gain + shift_ref[...].astype(F32)).astype(BF16)
            hidden_s[frame] = hidden
            hidden_low_s[frame * KEY_ROWS : (frame + 1) * KEY_ROWS, :] = hidden[:KEY_ROWS]
            frame_rows(cot_ref, rows_s, frame)
            keep = (row < PATCHES) & (live_ref[frame] > 0)
            grad = jnp.where(keep, rows_s[:KEY_ROWS, :], 0.0)
            grad_s[frame * KEY_ROWS : (frame + 1) * KEY_ROWS, :] = grad.astype(BF16)
            vec_ref[0:1, :] += column_sum(grad)

    fc_b = fc_b_ref[...].astype(F32)

    def one_frame(frame, carry):
        at = pl.multiple_of(frame * KEY_ROWS, 16)
        pre = dot_nn(hidden_s[frame], fc_w_ref[...]) + fc_b
        gate = 0.5 + 0.5 * jnp.tanh((0.5 * SLOPE) * pre)
        active = (pre * gate).astype(BF16)
        act_s[pl.ds(at, KEY_ROWS), :] = active[:KEY_ROWS]
        part = dot_nn(active, proj_w_ref[...])
        slope = (gate + SLOPE * pre * gate * (1.0 - gate))[:KEY_ROWS]
        grad_act = dot_nt(grad_s[pl.ds(at, KEY_ROWS), :], proj_w_ref[...])
        pre_grad = (grad_act * slope).astype(BF16)
        pre_grad_s[pl.ds(at, KEY_ROWS), :] = pre_grad
        back = dot_nt(pre_grad, fc_w_ref[...])

        @pl.when(step == 0)
        def _():
            out_s[frame] = part
            hidden_grad_s[frame] = back

        @pl.when(step > 0)
        def _():
            out_s[frame] += part
            hidden_grad_s[frame] += back

        return carry + column_sum(pre_grad.astype(F32))

    fc_b_grad = lax.fori_loop(0, frames, one_frame, jnp.zeros((1, feature), F32))
    vec_ref[pl.ds(1 + step, 1), :] = fc_b_grad

    proj_grad = dot_tn(act_s[...], grad_s[...])
    if packed:
        depth = proj_keep.shape[1]
        share = proj_keep.shape[2]
        low_core = table_ref[2 * vids] == 0
        for level in range(depth):
            first = proj_grad[2 * level * share : (2 * level + 1) * share].astype(BF16)
            second = proj_grad[(2 * level + 1) * share : (2 * level + 2) * share].astype(BF16)
            proj_keep[0, level] = jnp.where(low_core, first, second)
            proj_send[0, level] = jnp.where(low_core, second, first)
    else:
        proj_grad_ref[...] = proj_grad
    fc_grad = dot_tn(hidden_low_s[...], pre_grad_s[...])
    if packed:
        store_share(fc_grad, fc_keep, fc_send, table_ref, vids, (0,))
    else:
        fc_grad_ref[...] = fc_grad

    @pl.when(step == pl.num_programs(0) - 1)
    def _():
        sources, _, slots, _ = out_ref.shape
        proj_b = proj_b_ref[...].astype(F32)
        gain_grad = jnp.zeros((1, feature), F32)
        shift_grad = jnp.zeros((1, feature), F32)
        bias_grad = jnp.zeros((1, feature), F32)
        for frame in range(frames):
            rows_s[...] = resid_ref[frame] + (out_s[frame] + proj_b)
            for source in range(sources):
                out_ref[source, frame] = rows_s[source * slots : (source + 1) * slots, :].astype(BF16)
            normed, inverse = norm_parts(resid_ref[frame, :KEY_ROWS, :])
            hidden_grad = hidden_grad_s[frame]
            gain_grad += column_sum(hidden_grad * normed)
            shift_grad += column_sum(hidden_grad)
            grad = grad_s[frame * KEY_ROWS : (frame + 1) * KEY_ROWS, :].astype(F32)
            resid_grad = grad + norm_back(hidden_grad, normed, inverse, gain)
            resid_grad_ref[frame] = resid_grad
            bias_grad += column_sum(resid_grad.astype(BF16).astype(F32))
        spare = vec_ref.shape[0] - 3
        vec_ref[spare : spare + 1, :] = gain_grad
        vec_ref[spare + 1 : spare + 2, :] = shift_grad
        vec_ref[spare + 2 : spare + 3, :] = bias_grad


def attention_backward_kernel(
    x_ref, new_ref, query_ref, keyval_ref, lse_ref, resid_grad_ref,
    gain_ref, shift_ref, in_w_ref, out_w_ref,
    frame_grad_ref, new_grad_ref, hidden_ref, joined_grad_ref, low_ref, vec_ref,
    rows_s, mixed_grad_s,
):
    feature = x_ref.shape[3]
    sources, _, slots, _ = x_ref.shape
    frame_rows(x_ref, rows_s)
    gain = gain_ref[...].astype(F32)
    key_row = lax.broadcasted_iota(jnp.int32, (KEY_ROWS, 1), 0)
    tokens = jnp.where(key_row == PATCHES, new_ref[0], rows_s[:KEY_ROWS, :])
    normed, inverse = norm_parts(tokens)
    hidden_ref[0] = (normed * gain + shift_ref[...].astype(F32)).astype(BF16)
    resid_low = resid_grad_ref[0].astype(BF16)
    low_ref[0] = resid_low
    mixed_grad_s[...] = dot_nt(resid_low, out_w_ref[...]).astype(BF16)
    allowed = key_row <= PATCHES
    masks = lane_masks()
    scale = jnp.asarray(HEAD**-0.5, BF16)
    for pair in range(HEADS // 2):
        cols = slice(pair * PAIR, (pair + 1) * PAIR)
        key_cols = slice(feature + pair * PAIR, feature + (pair + 1) * PAIR)
        value_cols = slice(2 * feature + pair * PAIR, 2 * feature + (pair + 1) * PAIR)
        query = query_ref[0, :KEY_ROWS, cols]
        keys = keyval_ref[0, :, cols]
        values = keyval_ref[0, :, feature + pair * PAIR : feature + (pair + 1) * PAIR]
        grad = mixed_grad_s[:, cols]
        grad_q = grad_k = grad_v = None
        for side, mask in enumerate(masks):
            query_one = query * (mask * scale)
            grad_one = grad * mask
            lse = lse_ref[0, 2 * pair + side : 2 * pair + side + 1, :KEY_ROWS]
            score = dot_nt(keys, query_one)
            weight = jnp.where(allowed, jnp.exp(score - lse), 0.0)
            grad_weight = dot_nt(values, grad_one)
            inner = jnp.sum(weight * grad_weight, axis=0, keepdims=True)
            grad_score = (weight * (grad_weight - inner)).astype(BF16)
            one_v = dot_nn(weight.astype(BF16), grad_one)
            one_k = dot_nn(grad_score, query_one)
            one_q = dot_tn(grad_score, keys * (mask * scale))
            grad_q = one_q if grad_q is None else grad_q + one_q
            grad_k = one_k if grad_k is None else grad_k + one_k
            grad_v = one_v if grad_v is None else grad_v + one_v
        joined_grad_ref[0, :, cols] = grad_q.astype(BF16)
        joined_grad_ref[0, :, key_cols] = grad_k.astype(BF16)
        joined_grad_ref[0, :, value_cols] = grad_v.astype(BF16)
    joined_grad = joined_grad_ref[0]
    hidden_grad = dot_nt(joined_grad, in_w_ref[...])
    tokens_grad = norm_back(hidden_grad, normed, inverse, gain)
    new_grad_ref[0] = tokens_grad[PATCHES : PATCHES + 1].astype(BF16)
    rows_s[:KEY_ROWS, :] = jnp.where(key_row < PATCHES, resid_grad_ref[0] + tokens_grad, 0.0)
    rows_s[KEY_ROWS:, :] = jnp.zeros((rows_s.shape[0] - KEY_ROWS, feature), F32)
    for source in range(sources):
        frame_grad_ref[source, 0] = rows_s[source * slots : (source + 1) * slots, :].astype(BF16)

    @pl.when(pl.program_id(0) == 0)
    def _():
        vec_ref[...] = jnp.zeros_like(vec_ref)

    vec_ref[0:1, :] += column_sum(joined_grad[:, :feature].astype(F32))
    vec_ref[1:2, :] += column_sum(joined_grad[:, 2 * feature :].astype(F32))
    vec_ref[2:3, :] += column_sum(hidden_grad * normed)
    vec_ref[3:4, :] += column_sum(hidden_grad)


def attention_weights_kernel(packed, vids, table_ref, hidden_ref, joined_grad_ref, mixed_ref, low_ref, *refs):
    step = pl.program_id(0)
    last = pl.num_programs(0) - 1

    def finish(grad):
        if packed:
            store_share(grad, refs[0], refs[1], table_ref, vids, (0,))
        else:
            refs[0][0] = grad

    @pl.when(step < last)
    def _():
        finish(dot_tn(hidden_ref[...], joined_grad_ref[...]))

    @pl.when(step == last)
    def _():
        frames = mixed_ref.shape[0]
        total = None
        for frame in range(frames):
            part = dot_tn(mixed_ref[frame, :KEY_ROWS, :], low_ref[frame * KEY_ROWS : (frame + 1) * KEY_ROWS, :])
            total = part if total is None else total + part
        finish(total)


def whole(shape):
    return pl.BlockSpec(shape, lambda *_: (0,) * len(shape), pipeline_mode=pl.Buffered(1))


def params():
    return pltpu.CompilerParams(vmem_limit_bytes=VMEM_CAP)


def cost(flops, nbytes, transcendentals=0):
    return pl.CostEstimate(flops=int(flops), bytes_accessed=int(nbytes), transcendentals=int(transcendentals))


def shards(
    vids, toks,
    frames, messages, frame_counts, cotangent,
    msg_gain, msg_shift, msg_in_w, msg_in_b, msg_out_w, msg_out_b,
    ln1_gain, ln1_shift, attn_in_w, attn_in_b, attn_out_w, attn_out_b,
    ln2_gain, ln2_shift, fc_w, fc_b, proj_w, proj_b,
):
    video_count, frame_slots, slots, feature = frames.shape
    devices = vids * toks
    group_frames = video_count * frame_slots
    owned = group_frames // toks
    slot_count = slots * toks
    hidden_units = fc_w.shape[1]
    chunks = hidden_units // feature
    share = feature // devices
    vid = lax.axis_index("vid")
    tok = lax.axis_index("tok")
    core = tok % 2
    both = ("vid", "tok")
    packed = vids == 4 and toks % 2 == 0 and share % 8 == 0

    def row_of(vector):
        return vector.reshape(1, -1)

    def exchange(blocks, axis):
        return lax.all_to_all(blocks, axis, split_axis=0, concat_axis=0, tiled=True)

    def to_all(rows):
        return exchange(jnp.broadcast_to(rows[None], (devices,) + rows.shape), both)

    group_index = jnp.arange(group_frames, dtype=jnp.int32)
    live_group = group_index % frame_slots < jnp.repeat(frame_counts, frame_slots)
    piece = messages.shape[-1]
    width = (piece + 1 + 127) // 128 * 128
    payload = jnp.concatenate(
        [
            messages.reshape(group_frames, piece),
            live_group.astype(BF16)[:, None],
            jnp.zeros((group_frames, width - piece - 1), BF16),
        ],
        axis=1,
    )
    gathered = to_all(payload).reshape(vids, toks, group_frames, width)
    message_rows = vids * group_frames
    message_all = (
        gathered[..., :piece].transpose(0, 2, 1, 3).reshape(message_rows, feature)
    )
    live_all = gathered[:, 0, :, piece].reshape(message_rows) > 0.5
    row_video = jnp.arange(message_rows, dtype=jnp.int32) // frame_slots
    allowed = ((row_video[:, None] == row_video[None, :]) & live_all[None, :]).astype(F32)

    x_blocks = exchange(frames.reshape(toks, owned, slots, feature), "tok")
    cot_blocks = exchange(cotangent.reshape(toks, owned, slots, feature), "tok")

    joined, mixed, message_new = pl.pallas_call(
        message_forward_kernel,
        out_shape=(
            jax.ShapeDtypeStruct((message_rows, 3 * feature), BF16),
            jax.ShapeDtypeStruct((message_rows, feature), BF16),
            jax.ShapeDtypeStruct((message_rows, feature), F32),
        ),
        compiler_params=params(),
        cost_estimate=cost(8 * message_rows * feature * feature, 8 * feature * feature),
        name="message_forward",
    )(
        message_all, allowed, row_of(msg_gain), row_of(msg_shift), msg_in_w, msg_in_b,
        msg_out_w, row_of(msg_out_b),
    )
    first_row = vid * group_frames + tok * owned
    own_new = lax.dynamic_slice(message_new, (first_row, 0), (owned, feature)).reshape(
        owned, 1, feature
    )

    rows = owned * slot_count
    by_frame = lambda *tail: pl.BlockSpec((1,) + tail, lambda f: (f,) + (0,) * len(tail))
    block_spec = pl.BlockSpec((toks, 1, slots, feature), lambda f: (0, f, 0, 0))
    query, keyval, attended, lse, resid = pl.pallas_call(
        attention_forward_kernel,
        grid=(owned,),
        in_specs=[
            block_spec,
            by_frame(1, feature),
            whole((1, feature)),
            whole((1, feature)),
            whole((feature, 3 * feature)),
            whole((2, feature)),
            whole((feature, feature)),
            whole((1, feature)),
        ],
        out_specs=[
            by_frame(slot_count, feature),
            by_frame(KEY_ROWS, 2 * feature),
            by_frame(slot_count, feature),
            by_frame(HEADS, slot_count),
            by_frame(slot_count, feature),
        ],
        out_shape=(
            jax.ShapeDtypeStruct((owned, slot_count, feature), BF16),
            jax.ShapeDtypeStruct((owned, KEY_ROWS, 2 * feature), BF16),
            jax.ShapeDtypeStruct((owned, slot_count, feature), BF16),
            jax.ShapeDtypeStruct((owned, HEADS, slot_count), F32),
            jax.ShapeDtypeStruct((owned, slot_count, feature), F32),
        ),
        scratch_shapes=[pltpu.VMEM((slot_count, feature), F32)],
        compiler_params=params(),
        cost_estimate=cost(10 * rows * feature * feature, 12 * rows * feature, rows * slot_count * HEADS),
        name="attention_forward",
    )(
        x_blocks, own_new, row_of(ln1_gain), row_of(ln1_shift), attn_in_w, attn_in_b,
        attn_out_w, row_of(attn_out_b),
    )

    own_index = tok * owned + jnp.arange(owned, dtype=jnp.int32)
    own_count = jnp.sum(
        jnp.where(
            (own_index // frame_slots)[:, None] == jnp.arange(video_count, dtype=jnp.int32)[None, :],
            frame_counts[None, :],
            0,
        ),
        axis=1,
    )
    own_live = (own_index % frame_slots < own_count).astype(jnp.int32)

    depth = toks // 2
    dest = jnp.arange(vids, dtype=jnp.int32)

    def slot_table(for_core):
        low_bit, high_bit = dest % 2 ^ vid % 2, dest // 2 ^ vid // 2
        return jnp.where(for_core == 0, 2 * low_bit + high_bit, 2 * high_bit + low_bit)

    table = jnp.concatenate([slot_table(core), slot_table(1 - core), core[None]]).astype(jnp.int32)

    half = (vids, depth)
    if packed:
        grad_specs = [
            pl.BlockSpec(
                (1, depth, chunks * share, feature),
                lambda j, table, live, base=base: (table[base + j], 0, 0, 0),
            )
            for base in (0, vids)
        ] + [
            pl.BlockSpec((vids, depth, 1, share, feature), lambda j, *_: (0, 0, j, 0, 0)) for _ in range(2)
        ]
        grad_shapes = [jax.ShapeDtypeStruct(half + (chunks * share, feature), BF16)] * 2 + [
            jax.ShapeDtypeStruct(half + (chunks, share, feature), BF16)
        ] * 2
    else:
        grad_specs = [
            pl.BlockSpec((feature, feature), lambda j, *_: (j, 0)),
            pl.BlockSpec((feature, feature), lambda j, *_: (0, j)),
        ]
        grad_shapes = [
            jax.ShapeDtypeStruct((hidden_units, feature), F32),
            jax.ShapeDtypeStruct((feature, hidden_units), F32),
        ]
    out_blocks_shape = (toks, owned, slots, feature)
    vec_rows = chunks + 4
    results = pl.pallas_call(
        partial(feed_forward_kernel, packed, vids),
        grid_spec=pltpu.PrefetchScalarGridSpec(
            num_scalar_prefetch=2,
            grid=(chunks,),
            in_specs=[
                whole((owned, slot_count, feature)),
                whole(out_blocks_shape),
                whole((1, feature)),
                whole((1, feature)),
                pl.BlockSpec((feature, feature), lambda j, *_: (0, j)),
                pl.BlockSpec((1, feature), lambda j, *_: (0, j)),
                pl.BlockSpec((feature, feature), lambda j, *_: (j, 0)),
                whole((1, feature)),
            ],
            out_specs=[
                whole(out_blocks_shape),
                whole((owned, KEY_ROWS, feature)),
                whole((vec_rows, feature)),
            ]
            + grad_specs,
            scratch_shapes=[
                pltpu.VMEM((owned, slot_count, feature), BF16),
                pltpu.VMEM((owned * KEY_ROWS, feature), BF16),
                pltpu.VMEM((owned * KEY_ROWS, feature), BF16),
                pltpu.VMEM((owned * KEY_ROWS, feature), BF16),
                pltpu.VMEM((owned * KEY_ROWS, feature), BF16),
                pltpu.VMEM((owned, slot_count, feature), F32),
                pltpu.VMEM((owned, KEY_ROWS, feature), F32),
                pltpu.VMEM((slot_count, feature), F32),
            ],
        ),
        out_shape=[
            jax.ShapeDtypeStruct(out_blocks_shape, BF16),
            jax.ShapeDtypeStruct((owned, KEY_ROWS, feature), F32),
            jax.ShapeDtypeStruct((vec_rows, feature), F32),
        ]
        + grad_shapes,
        compiler_params=params(),
        cost_estimate=cost(12 * rows * feature * hidden_units, 12 * feature * hidden_units, rows * hidden_units),
        name="feed_forward",
    )(
        table, own_live, resid, cot_blocks, row_of(ln2_gain), row_of(ln2_shift),
        fc_w, row_of(fc_b), proj_w, row_of(proj_b),
    )
    out_blocks, resid_grad, ff_vec = results[:3]
    output = exchange(out_blocks, "tok").reshape(frames.shape)

    frame_blocks, own_new_grad, hidden, joined_grad, resid_low, attn_vec = pl.pallas_call(
        attention_backward_kernel,
        grid=(owned,),
        in_specs=[
            block_spec,
            by_frame(1, feature),
            by_frame(slot_count, feature),
            by_frame(KEY_ROWS, 2 * feature),
            by_frame(HEADS, slot_count),
            by_frame(KEY_ROWS, feature),
            whole((1, feature)),
            whole((1, feature)),
            whole((feature, 3 * feature)),
            whole((feature, feature)),
        ],
        out_specs=[
            block_spec,
            by_frame(1, feature),
            by_frame(KEY_ROWS, feature),
            by_frame(KEY_ROWS, 3 * feature),
            by_frame(KEY_ROWS, feature),
            whole((8, feature)),
        ],
        out_shape=(
            jax.ShapeDtypeStruct(out_blocks_shape, BF16),
            jax.ShapeDtypeStruct((owned, 1, feature), BF16),
            jax.ShapeDtypeStruct((owned, KEY_ROWS, feature), BF16),
            jax.ShapeDtypeStruct((owned, KEY_ROWS, 3 * feature), BF16),
            jax.ShapeDtypeStruct((owned, KEY_ROWS, feature), BF16),
            jax.ShapeDtypeStruct((8, feature), F32),
        ),
        scratch_shapes=[pltpu.VMEM((slot_count, feature), F32), pltpu.VMEM((KEY_ROWS, feature), BF16)],
        compiler_params=params(),
        cost_estimate=cost(16 * rows * feature * feature, 20 * rows * feature, rows * slot_count * HEADS),
        name="attention_backward",
    )(
        x_blocks, own_new, query, keyval, lse, resid_grad, row_of(ln1_gain), row_of(ln1_shift),
        attn_in_w, attn_out_w,
    )
    frames_grad = exchange(frame_blocks, "tok").reshape(frames.shape)

    message_low = to_all(own_new_grad.reshape(owned, feature)).reshape(message_rows, feature)

    live_rows = owned * KEY_ROWS
    if packed:
        attn_specs = [pl.BlockSpec((vids, depth, 1, share, feature), lambda j, *_: (0, 0, j, 0, 0)) for _ in range(2)]
        attn_shapes = [jax.ShapeDtypeStruct(half + (4, share, feature), BF16)] * 2
    else:
        attn_specs = [pl.BlockSpec((1, feature, feature), lambda j, *_: (j, 0, 0))]
        attn_shapes = [jax.ShapeDtypeStruct((4, feature, feature), F32)]
    attn_grads = pl.pallas_call(
        partial(attention_weights_kernel, packed, vids),
        grid_spec=pltpu.PrefetchScalarGridSpec(
            num_scalar_prefetch=1,
            grid=(4,),
            in_specs=[
                whole((live_rows, feature)),
                pl.BlockSpec((live_rows, feature), lambda j, *_: (0, jnp.minimum(j, 2))),
                whole((owned, slot_count, feature)),
                whole((live_rows, feature)),
            ],
            out_specs=attn_specs,
        ),
        out_shape=attn_shapes,
        compiler_params=params(),
        cost_estimate=cost(8 * rows * feature * feature, 12 * rows * feature),
        name="attention_weights",
    )(
        table,
        hidden.reshape(live_rows, feature),
        joined_grad.reshape(live_rows, 3 * feature),
        attended,
        resid_low.reshape(live_rows, feature),
    )

    place = (vid * toks + tok) * share
    message_grad, msg_in_w_grad, msg_out_w_grad, msg_vec = pl.pallas_call(
        message_backward_kernel,
        grid_spec=pltpu.PrefetchScalarGridSpec(
            num_scalar_prefetch=1,
            grid=(1,),
            in_specs=[
                whole((message_rows, feature)),
                whole((message_rows, message_rows)),
                whole((message_rows, feature)),
                whole((message_rows, 3 * feature)),
                whole((message_rows, feature)),
                whole((1, feature)),
                whole((1, feature)),
                whole((feature, 3 * feature)),
                whole((feature, feature)),
            ],
            out_specs=[
                whole((message_rows, feature)),
                whole((share, 3 * feature)),
                whole((share, feature)),
                whole((8, (share + 127) // 128 * 128)),
            ],
            scratch_shapes=[
                pltpu.VMEM((message_rows, feature), BF16),
                pltpu.VMEM((message_rows, 3 * feature), BF16),
            ],
        ),
        out_shape=(
            jax.ShapeDtypeStruct((message_rows, feature), BF16),
            jax.ShapeDtypeStruct((share, 3 * feature), F32),
            jax.ShapeDtypeStruct((share, feature), F32),
            jax.ShapeDtypeStruct((8, (share + 127) // 128 * 128), F32),
        ),
        compiler_params=params(),
        cost_estimate=cost(20 * message_rows * feature * feature, 10 * feature * feature),
        name="message_backward",
    )(
        place[None].astype(jnp.int32), message_all, allowed, message_low, joined, mixed,
        row_of(msg_gain), row_of(msg_shift), msg_in_w, msg_out_w,
    )
    messages_grad = lax.dynamic_slice(
        message_grad, (vid * group_frames, tok * piece), (group_frames, piece)
    ).reshape(messages.shape)
    msg_vec = msg_vec[:, :share]

    def by_device(vector):
        return vector.reshape(devices, -1)

    spare = chunks + 1
    vectors = [
        by_device(ff_vec[0]),
        by_device(ff_vec[1 : 1 + chunks]),
        by_device(ff_vec[spare]),
        by_device(ff_vec[spare + 1]),
        by_device(ff_vec[spare + 2]),
        by_device(attn_vec[0]),
        by_device(attn_vec[1]),
        by_device(attn_vec[2]),
        by_device(attn_vec[3]),
    ]
    sizes = [v.shape[1] for v in vectors]
    total = sum(sizes)
    lanes = (total + 127) // 128 * 128
    stacked = jnp.concatenate(vectors + [jnp.zeros((devices, lanes - total), F32)], axis=1)
    small = jnp.sum(exchange(stacked.reshape(devices, lanes // 128, 128), both), axis=0).reshape(lanes)
    pieces, at = [], 0
    for size in sizes:
        pieces.append(small[at : at + size])
        at += size
    (
        proj_b_grad, fc_b_grad, ln2_gain_grad, ln2_shift_grad, attn_out_b_grad,
        in_b_first, in_b_second, ln1_gain_grad, ln1_shift_grad,
    ) = pieces

    def cross(bit_of_core):
        return [
            (v * toks + t, (v ^ bit_of_core[t % 2]) * toks + t) for v in range(vids) for t in range(toks)
        ]

    def reduce_packed(keep, send):
        def add(left, right):
            return (left.astype(F32) + right.astype(F32)).astype(BF16)

        got = lax.ppermute(send, "tok", [(t, t ^ 1) for t in range(toks)])
        send = add(keep[2:], got[2:])
        keep = add(keep[:2], got[:2])
        got = lax.ppermute(send, both, cross((1, 2)))
        send = add(keep[1], got[1])
        keep = add(keep[0], got[0])
        got = lax.ppermute(send, both, cross((2, 1)))
        blocks = add(keep, got)
        blocks = lax.all_to_all(
            blocks,
            "tok",
            split_axis=0,
            concat_axis=0,
            tiled=True,
            axis_index_groups=[[2 * z + c for z in range(depth)] for c in range(2)],
        )
        return jnp.sum(blocks.astype(F32), axis=0)

    def scatter(grad):
        return lax.psum_scatter(grad, both, scatter_dimension=0, tiled=True)

    if packed:
        proj_keep, proj_send, fc_keep, fc_send = results[3:]
        proj_w_grad = reduce_packed(proj_keep, proj_send)
        fc_w_grad = reduce_packed(fc_keep, fc_send).transpose(1, 0, 2).reshape(share, hidden_units)
        attn = reduce_packed(*attn_grads)
        attn_in_w_grad = attn[:3].transpose(1, 0, 2).reshape(share, 3 * feature)
        attn_out_w_grad = attn[3]
    else:
        proj_w_grad = scatter(results[3])
        fc_w_grad = scatter(results[4])
        attn_in_w_grad = scatter(attn_grads[0][:3].transpose(1, 0, 2).reshape(feature, 3 * feature))
        attn_out_w_grad = scatter(attn_grads[0][3])

    return (
        output,
        frames_grad,
        messages_grad,
        msg_vec[0],
        msg_vec[1],
        msg_in_w_grad,
        msg_vec[2:4],
        msg_out_w_grad,
        msg_vec[4],
        ln1_gain_grad,
        ln1_shift_grad,
        attn_in_w_grad,
        jnp.stack([in_b_first, in_b_second]),
        attn_out_w_grad,
        attn_out_b_grad,
        ln2_gain_grad,
        ln2_shift_grad,
        fc_w_grad,
        fc_b_grad,
        proj_w_grad,
        proj_b_grad,
    )


def solution(mesh):
    tokens = P("vid", None, "tok", None)
    rows, columns, one = P(("vid", "tok"), None), P(None, ("vid", "tok")), P(("vid", "tok"))
    in_specs = (tokens, P("vid", None, "tok"), P("vid"), tokens) + (P(),) * 18
    out_specs = (
        tokens, tokens, P("vid", None, "tok"),
        one, one, rows, columns, rows, one,
        one, one, rows, columns, rows, one,
        one, one, rows, one, rows, one,
    )
    return jax.shard_map(
        partial(shards, mesh.shape["vid"], mesh.shape["tok"]),
        mesh=mesh,
        in_specs=in_specs,
        out_specs=out_specs,
        check_vma=False,
    )
```

```python
from functools import partial

import jax
import jax.numpy as jnp
from jax import lax
from jax.experimental import pallas as pl
from jax.experimental.pallas import tpu as pltpu
from jax.sharding import PartitionSpec as P

HEADS = 12
HEAD = 64
PATCHES = 197
PAIR = 2 * HEAD
EPS = 1e-05
NEG = -1000000000.0
SLOPE = 1.702
F32 = jnp.float32
BF16 = jnp.bfloat16
MIB = 2**20

KEY_ROWS = (PATCHES + 1 + 15) // 16 * 16


def norm_parts(tensor):
    row_mean = jnp.mean(tensor, axis=-1, keepdims=True)
    centred = tensor - row_mean
    spread = jnp.mean(centred * centred, axis=-1, keepdims=True)
    inverse = lax.rsqrt(spread + EPS)
    return centred * inverse, inverse


def norm_back(grad_in, normed, inverse, gain):
    scaled = grad_in * gain
    return inverse * (
        scaled
        - jnp.mean(scaled, axis=-1, keepdims=True)
        - normed * jnp.mean(scaled * normed, axis=-1, keepdims=True)
    )


def dot_nn(left, right):
    return lax.dot_general(left, right, (((1,), (0,)), ((), ())), preferred_element_type=F32)


def dot_nt(left, right):
    return lax.dot_general(left, right, (((1,), (1,)), ((), ())), preferred_element_type=F32)


def dot_tn(left, right):
    return lax.dot_general(left, right, (((0,), (0,)), ((), ())), preferred_element_type=F32)


def lane_masks(dtype=BF16):
    lane = lax.broadcasted_iota(jnp.int32, (1, PAIR), 1)
    first = jnp.where(lane < HEAD, 1.0, 0.0)
    return first.astype(dtype), (1.0 - first).astype(dtype)


def column_sum(rows):
    return jnp.sum(rows, axis=0, keepdims=True)


def message_forward_kernel(
    msg_ref, allow_ref, gain_ref, shift_ref, in_w_ref, in_b_ref, out_w_ref, out_b_ref,
    joined_ref, mixed_ref, new_ref,
):
    feature = msg_ref.shape[1]
    message = msg_ref[...].astype(F32)
    normed, _ = norm_parts(message)
    hidden = (normed * gain_ref[...] + shift_ref[...]).astype(BF16)
    in_b = in_b_ref[...].astype(F32)
    for block in range(3):
        cols = slice(block * feature, (block + 1) * feature)
        part = dot_nn(hidden, in_w_ref[:, cols])
        if block != 1:
            part = part + in_b[block // 2 : block // 2 + 1]
        joined_ref[:, cols] = part.astype(BF16)
    allowed = allow_ref[...] > 0.5
    masks = lane_masks()
    scale = jnp.asarray(HEAD**-0.5, BF16)
    for pair in range(HEADS // 2):
        cols = slice(pair * PAIR, (pair + 1) * PAIR)
        query = joined_ref[:, cols]
        keys = joined_ref[:, feature + pair * PAIR : feature + (pair + 1) * PAIR]
        values = joined_ref[:, 2 * feature + pair * PAIR : 2 * feature + (pair + 1) * PAIR]
        total = None
        for mask in masks:
            score = dot_nt(query * (mask * scale), keys)
            score = jnp.where(allowed, score, NEG)
            weight = jnp.exp(score - jnp.max(score, axis=-1, keepdims=True))
            weight = weight / jnp.sum(weight, axis=-1, keepdims=True)
            part = dot_nn(weight.astype(BF16), values * mask)
            total = part if total is None else total + part
        mixed_ref[:, cols] = total.astype(BF16)
    new_ref[...] = message + (dot_nn(mixed_ref[...], out_w_ref[...]) + out_b_ref[...])


def message_backward_kernel(
    place_ref, msg_ref, allow_ref, low_ref, joined_ref, mixed_ref,
    gain_ref, shift_ref, in_w_ref, out_w_ref,
    grad_ref, in_w_grad_ref, out_w_grad_ref, vec_ref,
    mixed_grad_s, joined_grad_s,
):
    feature = msg_ref.shape[1]
    share = in_w_grad_ref.shape[0]
    message = msg_ref[...].astype(F32)
    normed, inverse = norm_parts(message)
    gain = gain_ref[...]
    hidden = (normed * gain + shift_ref[...]).astype(BF16)
    low = low_ref[...]
    low_wide = low.astype(F32)
    mixed_grad_s[...] = dot_nt(low, out_w_ref[...]).astype(BF16)
    allowed = allow_ref[...] > 0.5
    masks = lane_masks()
    scale = jnp.asarray(HEAD**-0.5, BF16)
    for pair in range(HEADS // 2):
        cols = slice(pair * PAIR, (pair + 1) * PAIR)
        key_cols = slice(feature + pair * PAIR, feature + (pair + 1) * PAIR)
        value_cols = slice(2 * feature + pair * PAIR, 2 * feature + (pair + 1) * PAIR)
        query = joined_ref[:, cols]
        keys = joined_ref[:, key_cols]
        values = joined_ref[:, value_cols]
        grad = mixed_grad_s[:, cols]
        grad_q = grad_k = grad_v = None
        for mask in masks:
            query_one = query * (mask * scale)
            grad_one = grad * mask
            score = jnp.where(allowed, dot_nt(query_one, keys), NEG)
            weight = jnp.exp(score - jnp.max(score, axis=-1, keepdims=True))
            weight = weight / jnp.sum(weight, axis=-1, keepdims=True)
            grad_weight = dot_nt(grad_one, values)
            inner = jnp.sum(weight * grad_weight, axis=-1, keepdims=True)
            grad_score = (weight * (grad_weight - inner)).astype(BF16)
            one_q = dot_nn(grad_score, keys * (mask * scale))
            one_k = dot_tn(grad_score, query_one)
            one_v = dot_tn(weight.astype(BF16), grad_one)
            grad_q = one_q if grad_q is None else grad_q + one_q
            grad_k = one_k if grad_k is None else grad_k + one_k
            grad_v = one_v if grad_v is None else grad_v + one_v
        joined_grad_s[:, cols] = grad_q.astype(BF16)
        joined_grad_s[:, key_cols] = grad_k.astype(BF16)
        joined_grad_s[:, value_cols] = grad_v.astype(BF16)
    joined_grad = joined_grad_s[...]
    hidden_grad = dot_nt(joined_grad, in_w_ref[...])
    grad_ref[...] = (low_wide + norm_back(hidden_grad, normed, inverse, gain)).astype(BF16)
    width = (share + 127) // 128 * 128
    row = lax.broadcasted_iota(jnp.int32, (feature, width), 0)
    col = lax.broadcasted_iota(jnp.int32, (feature, width), 1)
    pick = jnp.where((row == col + place_ref[0]) & (col < share), 1.0, 0.0)
    pick_low = pick.astype(BF16)
    own_hidden = dot_nn(hidden, pick_low).astype(BF16)
    own_mixed = dot_nn(mixed_ref[...], pick_low).astype(BF16)
    in_w_grad_ref[...] = dot_tn(own_hidden, joined_grad)[:share]
    out_w_grad_ref[...] = dot_tn(own_mixed, low)[:share]
    sums = jnp.concatenate(
        [
            column_sum(hidden_grad * normed),
            column_sum(hidden_grad),
            column_sum(joined_grad[:, :feature].astype(F32)),
            column_sum(joined_grad[:, 2 * feature :].astype(F32)),
            column_sum(low_wide),
            jnp.zeros((3, feature), F32),
        ],
        axis=0,
    )
    vec_ref[...] = lax.dot_general(
        sums, pick, (((1,), (0,)), ((), ())), precision=lax.Precision.HIGHEST, preferred_element_type=F32
    )


LANES = 128


def spread_rows(block_ref, scratch):
    sources, rows, _ = block_ref.shape
    for source in range(sources):
        for col in range(scratch.shape[0]):
            scratch[col, source * rows : (source + 1) * rows, :] = block_ref[
                source, :, col * LANES : (col + 1) * LANES
            ].astype(F32)


def gather_rows(scratch, block_ref):
    sources, rows, _ = block_ref.shape
    for source in range(sources):
        for col in range(scratch.shape[0]):
            block_ref[source, :, col * LANES : (col + 1) * LANES] = scratch[
                col, source * rows : (source + 1) * rows, :
            ].astype(BF16)


def take_frame(scratch, frame, count, stride):
    return jnp.concatenate(
        [scratch[col, pl.ds(frame, count, stride=stride), :] for col in range(scratch.shape[0])], axis=1
    )


def put_frame(scratch, frame, value, stride):
    for col in range(scratch.shape[0]):
        scratch[col, pl.ds(frame, value.shape[0], stride=stride), :] = value[:, col * LANES : (col + 1) * LANES]


def frame_places(slots, frame_slots, owned):
    for owner in range(frame_slots // owned):
        for frame in range(owned):
            yield owner, frame, owner * owned + frame


def to_owners_kernel(in_ref, out_ref, by_slot_s, by_owner_s):
    videos, slots, frame_slots, _ = in_ref.shape
    owners = out_ref.shape[0] // videos
    owned = frame_slots // owners
    for video in range(videos):
        for slot in range(slots):
            at = (video * slots + slot) * frame_slots
            for col in range(by_slot_s.shape[0]):
                by_slot_s[col, at : at + frame_slots, :] = in_ref[
                    video, slot, :, col * LANES : (col + 1) * LANES
                ].astype(F32)
        for owner, frame, place in frame_places(slots, frame_slots, owned):
            for col in range(by_slot_s.shape[0]):
                rows = by_slot_s[col, pl.ds(video * slots * frame_slots + place, slots, stride=frame_slots), :]
                first = (video * owners + owner) * slots * owned + frame
                by_owner_s[col, pl.ds(first, slots, stride=owned), :] = rows
    gather_rows(by_owner_s, out_ref)


def from_owners_kernel(parts, *refs):
    in_refs, out_ref, by_owner_s, by_slot_s = refs[:parts], refs[parts], refs[parts + 1], refs[parts + 2]
    videos, slots, frame_slots, _ = out_ref.shape
    owners = in_refs[0].shape[0] // videos
    owned = frame_slots // owners
    count = owned // parts
    for part, in_ref in enumerate(in_refs):
        spread_rows(in_ref, by_owner_s)
        for video in range(videos):
            for owner, frame, _ in frame_places(slots, frame_slots, owned):
                if frame >= count:
                    continue
                place = owner * owned + part * count + frame
                for col in range(by_slot_s.shape[0]):
                    first = (video * owners + owner) * slots * count + frame
                    rows = by_owner_s[col, pl.ds(first, slots, stride=count), :]
                    by_slot_s[col, pl.ds(video * slots * frame_slots + place, slots, stride=frame_slots), :] = rows
    for video in range(videos):
        for slot in range(slots):
            at = (video * slots + slot) * frame_slots
            for col in range(by_slot_s.shape[0]):
                out_ref[video, slot, :, col * LANES : (col + 1) * LANES] = by_slot_s[
                    col, at : at + frame_slots, :
                ].astype(BF16)


def attention_forward_kernel(
    owned, x_ref, new_ref, gain_ref, shift_ref, in_w_ref, in_b_ref, out_w_ref, out_b_ref,
    query_ref, keyval_ref, mixed_ref, lse_ref, resid_ref, tokens_ref, hidden_ref,
    rows_s,
):
    feature = x_ref.shape[2]
    slot_count = query_ref.shape[1]
    frame = pl.program_id(0)

    @pl.when(frame == 0)
    def _():
        spread_rows(x_ref, rows_s)

    gain = gain_ref[...]
    shift = shift_ref[...]
    frame_in = take_frame(rows_s, frame, slot_count, owned)
    normed, _ = norm_parts(frame_in)
    hidden = normed * gain + shift
    msg_normed, _ = norm_parts(new_ref[0])
    msg_hidden = msg_normed * gain + shift
    key_row = lax.broadcasted_iota(jnp.int32, (KEY_ROWS, 1), 0)
    tokens_ref[0] = jnp.where(key_row == PATCHES, new_ref[0], frame_in[:KEY_ROWS])
    hidden_kv = jnp.where(key_row == PATCHES, msg_hidden, hidden[:KEY_ROWS]).astype(BF16)
    hidden_ref[0] = hidden_kv
    hidden = hidden.astype(BF16)
    in_b = in_b_ref[...].astype(F32)
    query_ref[0] = (dot_nn(hidden, in_w_ref[:, :feature]) + in_b[0:1]).astype(BF16)
    keyval_ref[0, :, :feature] = dot_nn(hidden_kv, in_w_ref[:, feature : 2 * feature]).astype(BF16)
    keyval_ref[0, :, feature:] = (
        dot_nn(hidden_kv, in_w_ref[:, 2 * feature :]) + in_b[1:2]
    ).astype(BF16)
    allowed = key_row <= PATCHES
    masks = lane_masks()
    scale = jnp.asarray(HEAD**-0.5, BF16)
    for pair in range(HEADS // 2):
        cols = slice(pair * PAIR, (pair + 1) * PAIR)
        query = query_ref[0, :, cols]
        keys = keyval_ref[0, :, cols]
        values = keyval_ref[0, :, feature + pair * PAIR : feature + (pair + 1) * PAIR]
        total = None
        for side, mask in enumerate(masks):
            score = dot_nt(keys, query * (mask * scale))
            score = jnp.where(allowed, score, NEG)
            peak = jnp.max(score, axis=0, keepdims=True)
            weight = jnp.exp(score - peak)
            norm = jnp.sum(weight, axis=0, keepdims=True)
            lse_ref[0, 2 * pair + side : 2 * pair + side + 1, :] = peak + jnp.log(norm)
            weight = (weight * (1.0 / norm)).astype(BF16)
            part = dot_tn(weight, values * mask)
            total = part if total is None else total + part
        mixed_ref[0, :, cols] = total.astype(BF16)
    resid_ref[0] = take_frame(rows_s, frame, slot_count, owned) + (
        dot_nn(mixed_ref[0], out_w_ref[...]) + out_b_ref[...]
    )


def feed_forward_kernel(
    resid_ref, gain_ref, shift_ref, fc_w_ref, fc_b_ref, proj_w_ref, proj_b_ref,
    out_ref, hidden_low_ref, act_ref, slope_ref,
    hidden_s, out_s, rows_s,
):
    step = pl.program_id(0)
    frames, slot_count, feature = resid_ref.shape

    @pl.when(step == 0)
    def _():
        gain = gain_ref[...]
        shift = shift_ref[...]
        for frame in range(frames):
            normed, _ = norm_parts(resid_ref[frame])
            hidden = (normed * gain + shift).astype(BF16)
            hidden_s[frame * slot_count : (frame + 1) * slot_count, :] = hidden
            hidden_low_ref[frame * KEY_ROWS : (frame + 1) * KEY_ROWS, :] = hidden[:KEY_ROWS]
        out_s[...] = jnp.zeros_like(out_s)

    fc_b = fc_b_ref[...]
    batch = 2 if frames % 2 == 0 else 1
    batches = frames // batch
    size = batch * slot_count

    def pre_of(index):
        return dot_nn(hidden_s[index * size : (index + 1) * size, :], fc_w_ref[...]) + fc_b

    pre = pre_of(0)
    for index in range(batches):
        later = pre_of(index + 1) if index + 1 < batches else None
        gate = 0.5 + 0.5 * jnp.tanh((0.5 * SLOPE) * pre)
        active = pre * gate
        slope = (gate + SLOPE * active * (1.0 - gate)).astype(BF16)
        active = active.astype(BF16)
        for frame in range(batch):
            at = (index * batch + frame) * KEY_ROWS
            rows = slice(frame * slot_count, frame * slot_count + KEY_ROWS)
            slope_ref[at : at + KEY_ROWS, :] = slope[rows]
            act_ref[at : at + KEY_ROWS, :] = active[rows]
        out_s[index * size : (index + 1) * size, :] += dot_nn(active, proj_w_ref[...])
        pre = later

    @pl.when(step == pl.num_programs(0) - 1)
    def _():
        proj_b = proj_b_ref[...]
        for frame in range(frames):
            rows = out_s[frame * slot_count : (frame + 1) * slot_count, :]
            put_frame(rows_s, frame, resid_ref[frame] + (rows + proj_b), frames)
        gather_rows(rows_s, out_ref)


def owner_slots(table_ref, vids, depth, for_send):
    base = vids if for_send else 0
    for vid in range(vids):
        for level in range(depth):
            swapped = (level % 2) * (depth // 2) + level // 2
            yield vid, level, (table_ref[base + vid], swapped ^ table_ref[2 * vids + 1])


def store_share(value, keep_ref, send_ref, table_ref, vids, chunk=0):
    depth = keep_ref.shape[1]
    share, width = keep_ref.shape[-2:]
    low_core = table_ref[2 * vids] == 0
    slots = zip(owner_slots(table_ref, vids, depth, False), owner_slots(table_ref, vids, depth, True))
    for (vid, level, kept), (_, _, sent) in slots:
        at = ((vid * depth + level) * 2) * share
        for part in range(value.shape[1] // width):
            cols = slice(part * width, (part + 1) * width)
            first = value[at : at + share, cols].astype(BF16)
            second = value[at + share : at + 2 * share, cols].astype(BF16)
            keep_ref[kept + (chunk + part,)] = jnp.where(low_core, first, second)
            send_ref[sent + (chunk + part,)] = jnp.where(low_core, second, first)


def store_rows(value, keep_ref, send_ref, table_ref, vids):
    _, depth, count, share, width = keep_ref.shape
    across = value.shape[1] // width
    low_core = table_ref[2 * vids] == 0
    for level in range(depth):
        place = ((level % 2) * (depth // 2) + level // 2) ^ table_ref[2 * vids + 1]
        for part in range(count):
            cols = slice(part % across * width, (part % across + 1) * width)
            at = (2 * level * (count // across) + part // across) * share
            first = value[at : at + share, cols].astype(BF16)
            at += count // across * share
            second = value[at : at + share, cols].astype(BF16)
            keep_ref[0, place, part] = jnp.where(low_core, first, second)
            send_ref[0, place, part] = jnp.where(low_core, second, first)


def feed_backward_kernel(
    packed, vids, table_ref, live_ref,
    cot_ref, resid_ref, hidden_low_ref, act_ref, slope_ref, mixed_ref, gain_ref, fc_w_ref, proj_w_ref, out_w_ref,
    *refs,
):
    resid_grad_ref, mixed_grad_ref, vec_ref, fc_b_ref = refs[:4]
    grads = refs[4:-7]
    grad_s, pre_grad_s, hidden_grad_s, low_s, resid_s, mixed_s, rows_s = refs[-7:]
    step = pl.program_id(0)
    last = pl.num_programs(0) - 1
    frames, _, feature = resid_grad_ref.shape

    def finish(grad):
        if packed:
            store_share(grad, grads[2], grads[3], table_ref, vids)
        else:
            grads[1][0] = grad

    @pl.when(step == 0)
    def _():
        hidden_grad_s[...] = jnp.zeros_like(hidden_grad_s)
        spread_rows(cot_ref, rows_s)
        row = lax.broadcasted_iota(jnp.int32, (KEY_ROWS, 1), 0)
        total = None
        for frame in range(frames):
            keep = (row < PATCHES) & (live_ref[frame] > 0)
            grad = jnp.where(keep, take_frame(rows_s, frame, KEY_ROWS, frames), 0.0)
            grad_s[frame * KEY_ROWS : (frame + 1) * KEY_ROWS, :] = grad.astype(BF16)
            total = column_sum(grad) if total is None else total + column_sum(grad)
        spare = vec_ref.shape[0] - 1
        vec_ref[:spare, :] = jnp.zeros((spare, feature), F32)
        vec_ref[spare:, :] = total

    @pl.when(step < frames)
    def _():
        at = pl.multiple_of(step * KEY_ROWS, 16)
        resid_s[pl.ds(at, KEY_ROWS), :] = resid_ref[0, :KEY_ROWS, :]
        mixed_s[pl.ds(at, KEY_ROWS), :] = mixed_ref[0, :KEY_ROWS, :]

    @pl.when(step < last)
    def _():
        grad_act = dot_nt(grad_s[...], proj_w_ref[...])
        proj_grad = dot_tn(act_ref[...], grad_s[...])
        pre_grad = (grad_act * slope_ref[...].astype(F32)).astype(BF16)
        pre_grad_s[...] = pre_grad
        fc_b_ref[pl.ds(step, 1), :] = column_sum(pre_grad.astype(F32))
        if packed:
            store_rows(proj_grad, grads[0], grads[1], table_ref, vids)
        else:
            grads[0][...] = proj_grad
        hidden_grad_s[...] += dot_nt(pre_grad, fc_w_ref[...])
        finish(dot_tn(hidden_low_ref[...], pre_grad_s[...]))

    @pl.when(step == last)
    def _():
        gain = gain_ref[...]
        gain_grad = jnp.zeros((1, feature), F32)
        shift_grad = jnp.zeros((1, feature), F32)
        bias_grad = jnp.zeros((1, feature), F32)
        for frame in range(frames):
            rows = slice(frame * KEY_ROWS, (frame + 1) * KEY_ROWS)
            normed, inverse = norm_parts(resid_s[rows, :])
            hidden_grad = hidden_grad_s[rows, :]
            gain_grad += column_sum(hidden_grad * normed)
            shift_grad += column_sum(hidden_grad)
            resid_grad = grad_s[rows, :].astype(F32) + norm_back(hidden_grad, normed, inverse, gain)
            resid_grad_ref[frame] = resid_grad
            low = resid_grad.astype(BF16)
            low_s[rows, :] = low
            bias_grad += column_sum(low.astype(F32))
        spare = vec_ref.shape[0] - 4
        vec_ref[spare : spare + 1, :] = gain_grad
        vec_ref[spare + 1 : spare + 2, :] = shift_grad
        vec_ref[spare + 2 : spare + 3, :] = bias_grad
        mixed_grad = dot_nt(low_s[...], out_w_ref[...]).astype(BF16)
        for frame in range(frames):
            mixed_grad_ref[frame] = mixed_grad[frame * KEY_ROWS : (frame + 1) * KEY_ROWS]
        finish(dot_tn(mixed_s[...], low_s[...]))


def pair_backward(query, keys, values, grad, lse_of, allowed, masks, scale):
    grad_q = grad_k = grad_v = None
    for side, mask in enumerate(masks):
        query_one = query * (mask * scale)
        grad_one = grad * mask
        score = dot_nt(keys, query_one)
        weight = jnp.where(allowed, jnp.exp(score - lse_of(side)), 0.0)
        grad_weight = dot_nt(values, grad_one)
        inner = jnp.sum(weight * grad_weight, axis=0, keepdims=True)
        grad_score = (weight * (grad_weight - inner)).astype(BF16)
        one_v = dot_nn(weight.astype(BF16), grad_one)
        one_k = dot_nn(grad_score, query_one)
        one_q = dot_tn(grad_score, keys * (mask * scale))
        grad_q = one_q if grad_q is None else grad_q + one_q
        grad_k = one_k if grad_k is None else grad_k + one_k
        grad_v = one_v if grad_v is None else grad_v + one_v
    return grad_q.astype(BF16), grad_k.astype(BF16), grad_v.astype(BF16)


def attention_backward_kernel(
    packed, vids, first, count, final, table_ref,
    tokens_ref, query_ref, keyval_ref, lse_ref, mixed_grad_ref, resid_grad_ref, gain_ref, in_w_ref, earlier_ref, *refs,
):
    if final:
        hidden_ref, fc_b_ref, *others = refs[: -7 if packed else -6]
        refs = refs[len(others) + 2 :]
    frame_grad_ref, joined_ref, small_ref = refs[:3]
    rows_s = refs[-1] if not final else refs[-2]
    step = pl.program_id(0)
    feature = tokens_ref.shape[2]

    @pl.when(step < count)
    def _():
        gain = gain_ref[...]
        key_row = lax.broadcasted_iota(jnp.int32, (KEY_ROWS, 1), 0)
        allowed = key_row <= PATCHES
        masks = lane_masks()
        scale = jnp.asarray(HEAD**-0.5, BF16)
        for pair in range(HEADS // 2):
            cols = slice(pair * PAIR, (pair + 1) * PAIR)
            value_cols = slice(feature + pair * PAIR, feature + (pair + 1) * PAIR)

            def lse_of(side, head=2 * pair):
                return lse_ref[0, head + side : head + side + 1, :KEY_ROWS]

            grads = pair_backward(
                query_ref[0, :KEY_ROWS, cols], keyval_ref[0, :, cols], keyval_ref[0, :, value_cols],
                mixed_grad_ref[0, :, cols], lse_of, allowed, masks, scale,
            )
            for block, value in enumerate(grads):
                joined_ref[0, :, block * feature + pair * PAIR : block * feature + (pair + 1) * PAIR] = value
        joined = joined_ref[0]
        hidden_grad = dot_nt(joined, in_w_ref[...])
        normed, inverse = norm_parts(tokens_ref[0])
        tokens_grad = norm_back(hidden_grad, normed, inverse, gain)
        frame_grad = jnp.where(key_row < PATCHES, resid_grad_ref[0] + tokens_grad, 0.0)
        put_frame(rows_s, step, frame_grad, count)

        @pl.when(step == 0)
        def _():
            small_ref[...] = earlier_ref[...]

        sums = small_ref.shape[0] - 8
        small_ref[pl.ds(first + step, 1), :] = tokens_grad[PATCHES : PATCHES + 1]
        small_ref[sums : sums + 1, :] += column_sum(joined[:, :feature].astype(F32))
        small_ref[sums + 1 : sums + 2, :] += column_sum(joined[:, 2 * feature :].astype(F32))
        small_ref[sums + 2 : sums + 3, :] += column_sum(hidden_grad * normed)
        small_ref[sums + 3 : sums + 4, :] += column_sum(hidden_grad)
        if final:
            joined_s = refs[-1]
            joined_s[pl.ds(pl.multiple_of(step * KEY_ROWS, 16), KEY_ROWS), :] = joined

        @pl.when(step == count - 1)
        def _():
            live = count * KEY_ROWS
            rows_s[:, live:, :] = jnp.zeros((rows_s.shape[0], rows_s.shape[1] - live, LANES), F32)
            gather_rows(rows_s, frame_grad_ref)

    if not final:
        return
    outs = refs[3:-2]
    joined_s = refs[-1]
    across = feature // LANES

    for block in range(3):

        @pl.when(step == count + block)
        def _(block=block):
            cols = slice(block * feature, (block + 1) * feature)
            split = len(others) * count * KEY_ROWS
            grad = dot_tn(hidden_ref[split:, :], joined_s[:, cols])
            for part, other in enumerate(others):
                size = count * KEY_ROWS
                grad = grad + dot_tn(hidden_ref[part * size : (part + 1) * size, :], other[:, cols])
            if packed:
                store_share(grad, outs[0], outs[1], table_ref, vids, block * across)
            else:
                outs[0][block] = grad

    @pl.when(step == count + 3)
    def _():
        sums = jnp.concatenate([small_ref[small_ref.shape[0] - 8 :, :], fc_b_ref[...]])
        row = lax.broadcasted_iota(jnp.int32, (sums.shape[0], LANES), 0)
        col = lax.broadcasted_iota(jnp.int32, (sums.shape[0], LANES), 1)
        turned = lax.dot_general(
            sums, jnp.where(row == col, 1.0, 0.0), (((0,), (0,)), ((), ())),
            precision=lax.Precision.HIGHEST, preferred_element_type=F32,
        )
        if packed:
            store_share(turned, outs[0], outs[1], table_ref, vids, 3 * across)
        else:
            outs[0][3] = jnp.concatenate([turned] * across, axis=1)


def resident(shape):
    return pl.BlockSpec(shape, lambda *_: (0,) * len(shape), pipeline_mode=pl.Buffered(1))


def params(mebibytes):
    return pltpu.CompilerParams(vmem_limit_bytes=60 * MIB)


def cost(flops, nbytes, transcendentals=0):
    return pl.CostEstimate(
        flops=10 * int(flops), bytes_accessed=10 * int(nbytes), transcendentals=10 * int(transcendentals)
    )


def after(value, ready):
    return lax.optimization_barrier((value, ready))[0]


def add(left, right):
    return (left.astype(F32) + right.astype(F32)).astype(BF16)


def shards(
    vids, toks,
    frames, messages, frame_counts, cotangent,
    msg_gain, msg_shift, msg_in_w, msg_in_b, msg_out_w, msg_out_b,
    ln1_gain, ln1_shift, attn_in_w, attn_in_b, attn_out_w, attn_out_b,
    ln2_gain, ln2_shift, fc_w, fc_b, proj_w, proj_b,
):
    video_count, frame_slots, slots, feature = frames.shape
    devices = vids * toks
    group_frames = video_count * frame_slots
    owned = group_frames // toks
    owners = toks // video_count
    slot_count = slots * toks
    hidden_units = fc_w.shape[1]
    chunks = hidden_units // feature
    share = feature // devices
    vid = lax.axis_index("vid")
    tok = lax.axis_index("tok")
    core = tok % 2
    both = ("vid", "tok")
    depth = toks // 2
    packed = vids == 4 and toks == 8 and share % 8 == 0

    vectors = [msg_gain, msg_shift, msg_out_b, ln1_gain, ln1_shift, attn_out_b, ln2_gain, ln2_shift, proj_b]
    stacked = jnp.stack(vectors + [fc_b[at : at + feature] for at in range(0, hidden_units, feature)])
    stacked = stacked.astype(F32).reshape(-1, 1, feature)

    def row(index):
        return pl.BlockSpec((None, 1, feature), lambda *_: (index, 0, 0))

    def exchange(blocks):
        return lax.all_to_all(blocks, "tok", split_axis=0, concat_axis=0, tiled=True)

    slot_shape = (video_count, slots, frame_slots, feature)
    slot_scratch = pltpu.VMEM((feature // LANES, group_frames * slots, LANES), F32)

    def by_owner(tokens):
        return pl.pallas_call(
            to_owners_kernel,
            grid=(1,),
            in_specs=[resident(slot_shape)],
            out_specs=resident((toks, slots * owned, feature)),
            out_shape=jax.ShapeDtypeStruct((toks, slots * owned, feature), BF16),
            scratch_shapes=[slot_scratch, slot_scratch],
            compiler_params=params(40),
            cost_estimate=cost(0, 4 * group_frames * slots * feature),
            name="to_owners",
        )(tokens.transpose(0, 2, 1, 3))

    def from_owners(blocks):
        by_slot = pl.pallas_call(
            partial(from_owners_kernel, len(blocks)),
            grid=(1,),
            in_specs=[resident(block.shape) for block in blocks],
            out_specs=resident(slot_shape),
            out_shape=jax.ShapeDtypeStruct(slot_shape, BF16),
            scratch_shapes=[
                pltpu.VMEM((feature // LANES, group_frames * slots // len(blocks), LANES), F32),
                slot_scratch,
            ],
            compiler_params=params(40),
            cost_estimate=cost(0, 4 * group_frames * slots * feature),
            name="from_owners",
        )(*blocks)
        return by_slot.transpose(0, 2, 1, 3)

    def swap(rows, axis, size, bit):
        return lax.ppermute(rows, axis, [(i, i ^ bit) for i in range(size)])

    def over_levels(rows):
        return [rows] + [swap(rows, "tok", toks, 2 * step) for step in range(1, depth)]

    def by_difference(rows):
        bit = 1
        while bit < vids:
            pairs = rows.reshape((vids // (2 * bit), 2, bit) + rows.shape[1:])
            turned = jnp.where((vid // bit) % 2 == 1, pairs[:, ::-1], pairs)
            rows = turned.reshape(rows.shape)
            bit *= 2
        return rows

    def in_order(rows):
        rows = rows.reshape((2, depth) + rows.shape[2:]).swapaxes(0, 1)
        rows = rows.reshape((toks,) + rows.shape[2:])
        bit = 1
        while bit < toks:
            pairs = rows.reshape((toks // (2 * bit), 2, bit) + rows.shape[1:])
            turned = jnp.where((tok // bit) % 2 == 1, pairs[:, ::-1], pairs)
            rows = turned.reshape(rows.shape)
            bit *= 2
        return rows

    group_index = jnp.arange(group_frames, dtype=jnp.int32)
    live_group = group_index % frame_slots < jnp.repeat(frame_counts, frame_slots)
    piece = messages.shape[-1]
    width = (piece + 1 + 127) // 128 * 128
    payload = jnp.concatenate(
        [
            messages.reshape(group_frames, piece),
            live_group.astype(BF16)[:, None],
            jnp.zeros((group_frames, width - piece - 1), BF16),
        ],
        axis=1,
    )
    x_blocks = exchange(by_owner(frames))
    gathered = payload[None]
    bit = 1
    while bit < vids:
        gathered = jnp.concatenate([gathered, swap(gathered, "vid", vids, bit)])
        bit *= 2
    gathered = jnp.stack([gathered, swap(gathered, "tok", toks, 1)])
    gathered_first = gathered
    gathered = in_order(jnp.stack(over_levels(gathered), axis=1)).swapaxes(0, 1)
    message_rows = vids * group_frames
    message_all = gathered[..., :piece].transpose(0, 2, 1, 3).reshape(message_rows, feature)
    live_all = gathered[:, 0, :, piece].reshape(message_rows) > 0.5
    row_video = jnp.arange(message_rows, dtype=jnp.int32) // frame_slots
    allowed = ((row_video[:, None] == row_video[None, :]) & live_all[None, :]).astype(F32)

    joined, mixed, message_new = pl.pallas_call(
        message_forward_kernel,
        grid=(1,),
        in_specs=[
            resident((message_rows, feature)),
            resident((message_rows, message_rows)),
            row(0),
            row(1),
            resident((feature, 3 * feature)),
            resident((2, feature)),
            resident((feature, feature)),
            row(2),
        ],
        out_specs=[
            resident((message_rows, 3 * feature)),
            resident((message_rows, feature)),
            resident((message_rows, feature)),
        ],
        out_shape=(
            jax.ShapeDtypeStruct((message_rows, 3 * feature), BF16),
            jax.ShapeDtypeStruct((message_rows, feature), BF16),
            jax.ShapeDtypeStruct((message_rows, feature), F32),
        ),
        compiler_params=params(40),
        cost_estimate=cost(8 * message_rows * feature * feature, 8 * feature * feature),
        name="message_forward",
    )(
        message_all, allowed, stacked, stacked, msg_in_w, msg_in_b, msg_out_w, stacked,
    )
    cot_blocks = exchange(after(by_owner(cotangent), (x_blocks, gathered_first)))
    own_new = lax.dynamic_slice(message_new, (tok * owned, 0), (owned, feature)).reshape(owned, 1, feature)

    rows = owned * slot_count
    live_rows = owned * KEY_ROWS
    blocks_shape = (toks, slots * owned, feature)
    columns_shape = (feature // LANES, rows, LANES)

    def by_frame(*tail):
        return pl.BlockSpec((1,) + tail, lambda f, *_: (f,) + (0,) * len(tail))

    query, keyval, attended, lse, resid, tokens, hidden_kv = pl.pallas_call(
        partial(attention_forward_kernel, owned),
        grid=(owned,),
        in_specs=[
            resident(blocks_shape),
            by_frame(1, feature),
            row(3),
            row(4),
            resident((feature, 3 * feature)),
            resident((2, feature)),
            resident((feature, feature)),
            row(5),
        ],
        out_specs=[
            by_frame(slot_count, feature),
            by_frame(KEY_ROWS, 2 * feature),
            by_frame(slot_count, feature),
            by_frame(HEADS, slot_count),
            by_frame(slot_count, feature),
            by_frame(KEY_ROWS, feature),
            by_frame(KEY_ROWS, feature),
        ],
        out_shape=(
            jax.ShapeDtypeStruct((owned, slot_count, feature), BF16),
            jax.ShapeDtypeStruct((owned, KEY_ROWS, 2 * feature), BF16),
            jax.ShapeDtypeStruct((owned, slot_count, feature), BF16),
            jax.ShapeDtypeStruct((owned, HEADS, slot_count), F32),
            jax.ShapeDtypeStruct((owned, slot_count, feature), F32),
            jax.ShapeDtypeStruct((owned, KEY_ROWS, feature), F32),
            jax.ShapeDtypeStruct((owned, KEY_ROWS, feature), BF16),
        ),
        scratch_shapes=[pltpu.VMEM(columns_shape, F32)],
        compiler_params=params(40),
        cost_estimate=cost(10 * rows * feature * feature, 12 * rows * feature, rows * slot_count * HEADS),
        name="attention_forward",
    )(
        x_blocks, own_new, stacked, stacked, attn_in_w, attn_in_b, attn_out_w, stacked,
    )

    out_blocks, hidden_low, act, slope = pl.pallas_call(
        feed_forward_kernel,
        grid=(chunks,),
        in_specs=[
            resident((owned, slot_count, feature)),
            row(6),
            row(7),
            pl.BlockSpec((feature, feature), lambda j: (0, j)),
            pl.BlockSpec((None, 1, feature), lambda j: (9 + j, 0, 0)),
            pl.BlockSpec((feature, feature), lambda j: (j, 0)),
            row(8),
        ],
        out_specs=[
            resident(blocks_shape),
            resident((live_rows, feature)),
            pl.BlockSpec((live_rows, feature), lambda j: (0, j)),
            pl.BlockSpec((live_rows, feature), lambda j: (0, j)),
        ],
        out_shape=(
            jax.ShapeDtypeStruct(blocks_shape, BF16),
            jax.ShapeDtypeStruct((live_rows, feature), BF16),
            jax.ShapeDtypeStruct((live_rows, hidden_units), BF16),
            jax.ShapeDtypeStruct((live_rows, hidden_units), BF16),
        ),
        scratch_shapes=[
            pltpu.VMEM((rows, feature), BF16),
            pltpu.VMEM((rows, feature), F32),
            pltpu.VMEM(columns_shape, F32),
        ],
        compiler_params=params(48),
        cost_estimate=cost(4 * rows * feature * hidden_units, 12 * feature * hidden_units, rows * hidden_units),
        name="feed_forward",
    )(
        resid, stacked, stacked, fc_w, stacked, proj_w, stacked,
    )
    output_blocks = exchange(after(out_blocks, cot_blocks))
    output = from_owners([output_blocks])

    own_index = tok * owned + jnp.arange(owned, dtype=jnp.int32)
    own_count = jnp.sum(
        jnp.where(
            (own_index // frame_slots)[:, None] == jnp.arange(video_count, dtype=jnp.int32)[None, :],
            frame_counts[None, :],
            0,
        ),
        axis=1,
    )
    own_live = (own_index % frame_slots < own_count).astype(jnp.int32)

    dest = jnp.arange(vids, dtype=jnp.int32)

    def slot_table(for_core):
        low_bit, high_bit = dest % 2 ^ vid % 2, dest // 2 ^ vid // 2
        return jnp.where(for_core == 0, 2 * low_bit + high_bit, 2 * high_bit + low_bit)

    level = tok // 2
    swapped = (level % 2) * (depth // 2) + level // 2
    table = jnp.concatenate([slot_table(core), slot_table(1 - core), core[None], swapped[None]]).astype(jnp.int32)

    def cross(bit_of_core):
        return [
            (v * toks + t, (v ^ bit_of_core[t % 2]) * toks + t) for v in range(vids) for t in range(toks)
        ]

    def send_over(stage, value):
        if stage == 0:
            return swap(value, "tok", toks, 1)
        if stage == 1:
            return lax.ppermute(value, both, cross((1, 2)))
        if stage == 2:
            return lax.ppermute(value, both, cross((2, 1)))
        return swap(value, "tok", toks, 2 if stage == 3 else 4)

    def sum_of(terms, dtype):
        value = terms[0].astype(F32)
        for term in terms[1:]:
            value = value + term.astype(F32)
        return value.astype(dtype)

    class Sum:
        def __init__(self, *grads):
            self.terms = [[keep] for keep, _ in grads]
            self.got = [send_over(0, send) for _, send in grads]
            self.stage = 0

        def step(self, ready):
            self.stage += 1
            terms = [one + [got] for one, got in zip(self.terms, after(self.got, ready))]
            if self.stage == 3:
                terms = [[term.reshape((depth,) + term.shape[2:]) for term in one] for one in terms]
            middle = terms[0][0].shape[0] // 2
            axis = terms[0][0].ndim - 3
            send = jnp.concatenate([sum_of([term[middle:] for term in one], BF16) for one in terms], axis=axis)
            terms = [[term[:middle] for term in one] for one in terms]
            if len(terms) > 1:
                terms = [[jnp.concatenate([sum_of(one, BF16) for one in terms], axis=axis)]]
            self.terms = terms
            self.got = [send_over(self.stage, send)]
            return send

        def end(self, ready):
            return sum_of(self.terms[0] + after(self.got, ready), F32)[0]

    half = (vids, depth)
    across = feature // LANES
    columns = feature // across

    def packed_out(*tail):
        return [jax.ShapeDtypeStruct(half + tail, BF16)] * 2

    if packed:
        proj_specs = [
            pl.BlockSpec(
                (1, depth, across * chunks, share, columns),
                lambda j, table, live, base=base: (table[base + jnp.minimum(j, chunks - 1)], 0, 0, 0, 0),
            )
            for base in (0, vids)
        ]
        proj_shapes = packed_out(across * chunks, share, columns)
        fc_specs = [pl.BlockSpec(half + (across, share, columns), lambda j, *_: (0, 0, j, 0, 0)) for _ in range(2)]
        fc_shapes = packed_out(across * (chunks + 1), share, columns)
    else:
        proj_specs = [pl.BlockSpec((feature, feature), lambda j, *_: (jnp.minimum(j, chunks - 1), 0))]
        proj_shapes = [jax.ShapeDtypeStruct((hidden_units, feature), F32)]
        fc_specs = [pl.BlockSpec((1, feature, feature), lambda j, *_: (j, 0, 0))]
        fc_shapes = [jax.ShapeDtypeStruct((chunks + 1, feature, feature), F32)]
    small_rows = owned + 8

    def chunk(index):
        return jnp.minimum(index, chunks - 1)

    def frame_of(index):
        return jnp.minimum(index, owned - 1)

    resid_grad, mixed_grad, small, fc_b_part, *ff_grads = pl.pallas_call(
        partial(feed_backward_kernel, packed, vids),
        grid_spec=pltpu.PrefetchScalarGridSpec(
            num_scalar_prefetch=2,
            grid=(max(chunks, owned) + 1,),
            in_specs=[
                resident(blocks_shape),
                pl.BlockSpec((1, slot_count, feature), lambda j, *_: (frame_of(j), 0, 0)),
                resident((live_rows, feature)),
                pl.BlockSpec((live_rows, feature), lambda j, *_: (0, chunk(j))),
                pl.BlockSpec((live_rows, feature), lambda j, *_: (0, chunk(j))),
                pl.BlockSpec((1, slot_count, feature), lambda j, *_: (frame_of(j), 0, 0)),
                row(6),
                pl.BlockSpec((feature, feature), lambda j, *_: (0, chunk(j))),
                pl.BlockSpec((feature, feature), lambda j, *_: (chunk(j), 0)),
                resident((feature, feature)),
            ],
            out_specs=[
                resident((owned, KEY_ROWS, feature)),
                resident((owned, KEY_ROWS, feature)),
                resident((small_rows, feature)),
                resident((chunks, feature)),
            ]
            + proj_specs
            + fc_specs,
            scratch_shapes=[
                pltpu.VMEM((live_rows, feature), BF16),
                pltpu.VMEM((live_rows, feature), BF16),
                pltpu.VMEM((live_rows, feature), F32),
                pltpu.VMEM((live_rows, feature), BF16),
                pltpu.VMEM((live_rows, feature), F32),
                pltpu.VMEM((live_rows, feature), BF16),
                pltpu.VMEM(columns_shape, F32),
            ],
        ),
        out_shape=[
            jax.ShapeDtypeStruct((owned, KEY_ROWS, feature), F32),
            jax.ShapeDtypeStruct((owned, KEY_ROWS, feature), BF16),
            jax.ShapeDtypeStruct((small_rows, feature), F32),
            jax.ShapeDtypeStruct((chunks, feature), F32),
        ]
        + proj_shapes
        + fc_shapes,
        compiler_params=params(48),
        cost_estimate=cost(8 * rows * feature * hidden_units, 12 * feature * hidden_units),
        name="feed_backward",
    )(
        table, own_live, cot_blocks, resid, hidden_low, act, slope, attended, stacked, fc_w, proj_w, attn_out_w,
    )
    proj_grads, fc_grads = ff_grads[: len(proj_shapes)], ff_grads[len(proj_shapes) :]

    parts = 2 if owned % 2 == 0 else 1
    part_frames = owned // parts
    part_blocks = (toks, slots * part_frames, feature)

    if packed:
        attn_specs = [resident(half + (across * 3 + 1, share, columns))] * 2
        attn_shapes = packed_out(across * 3 + 1, share, columns)
    else:
        attn_specs = [resident((4, feature, feature))]
        attn_shapes = [jax.ShapeDtypeStruct((4, feature, feature), F32)]
    part_rows = part_frames * KEY_ROWS

    def attention_backward(part, mixed_grad, small, others):
        first = part * part_frames
        final = part == parts - 1

        def by_part(*tail):
            return pl.BlockSpec(
                (1,) + tail, lambda f, *_: (first + jnp.minimum(f, part_frames - 1),) + (0,) * len(tail)
            )

        extra, extra_specs, scratch = [], [], []
        if final:
            extra = [hidden_kv.reshape(live_rows, feature), fc_b_own] + others
            extra_specs = [resident((live_rows, feature)), resident((chunks, feature))]
            extra_specs += [resident((part_rows, 3 * feature))] * len(others)
            scratch = [pltpu.VMEM((part_rows, 3 * feature), BF16)]
        return pl.pallas_call(
            partial(attention_backward_kernel, packed, vids, first, part_frames, final),
            grid_spec=pltpu.PrefetchScalarGridSpec(
                num_scalar_prefetch=1,
                grid=(part_frames + 4 * final,),
                in_specs=[
                    by_part(KEY_ROWS, feature),
                    by_part(slot_count, feature),
                    by_part(KEY_ROWS, 2 * feature),
                    by_part(HEADS, slot_count),
                    by_part(KEY_ROWS, feature),
                    by_part(KEY_ROWS, feature),
                    row(3),
                    resident((feature, 3 * feature)),
                    resident((small_rows, feature)),
                ]
                + extra_specs,
                out_specs=[
                    resident(part_blocks),
                    pl.BlockSpec(
                        (1, KEY_ROWS, 3 * feature), lambda f, *_: (jnp.minimum(f, part_frames - 1), 0, 0)
                    ),
                    resident((small_rows, feature)),
                ]
                + attn_specs * final,
                scratch_shapes=[pltpu.VMEM((feature // LANES, part_frames * slot_count, LANES), F32)] + scratch,
            ),
            out_shape=[
                jax.ShapeDtypeStruct(part_blocks, BF16),
                jax.ShapeDtypeStruct((part_frames, KEY_ROWS, 3 * feature), BF16),
                jax.ShapeDtypeStruct((small_rows, feature), F32),
            ]
            + attn_shapes * final,
            compiler_params=params(40),
            cost_estimate=cost(16 * rows * feature * feature // parts, 20 * rows * feature // parts),
            name="attention_backward",
        )(table, tokens, query, keyval, lse, mixed_grad, resid_grad, stacked, attn_in_w, small, *extra)

    if packed:
        ff_sum = Sum(fc_grads, proj_grads)
        mixed_grad = after(mixed_grad, output_blocks)
    fc_b_own = fc_b_part.reshape(devices, chunks, share).swapaxes(0, 1).reshape(chunks, feature)
    frame_blocks, joined_grads = [], []
    for part in range(parts):
        blocks, joined_grad, small, *attn_grads = attention_backward(part, mixed_grad, small, joined_grads)
        frame_blocks.append(exchange(blocks))
        joined_grads.append(joined_grad.reshape(part_rows, 3 * feature))
        if packed and part == 0:
            mixed_grad = after(mixed_grad, ff_sum.step(small))
    frames_grad = from_owners(frame_blocks)

    own_low = after(small[:owned].astype(BF16), frame_blocks)
    message_low = lax.all_to_all(
        jnp.broadcast_to(own_low[None], (devices, owned, feature)), both, split_axis=0, concat_axis=0, tiled=True
    )
    message_low = by_difference(message_low.reshape(vids, group_frames, feature)).reshape(message_rows, feature)
    if packed:
        attn_sum = Sum(after(attn_grads, frame_blocks[: parts - 1]))
        ready = attn_sum.step(small)
        ready = ff_sum.step(ready)
        ready = attn_sum.step(ready)
        message_low = after(message_low, ff_sum.step((ready, frame_blocks)))

    place = (vid * toks + tok) * share
    vec_lanes = (share + 127) // 128 * 128
    message_grad, msg_in_w_grad, msg_out_w_grad, msg_vec = pl.pallas_call(
        message_backward_kernel,
        grid_spec=pltpu.PrefetchScalarGridSpec(
            num_scalar_prefetch=1,
            grid=(1,),
            in_specs=[
                resident((message_rows, feature)),
                resident((message_rows, message_rows)),
                resident((message_rows, feature)),
                resident((message_rows, 3 * feature)),
                resident((message_rows, feature)),
                row(0),
                row(1),
                resident((feature, 3 * feature)),
                resident((feature, feature)),
            ],
            out_specs=[
                resident((message_rows, feature)),
                resident((share, 3 * feature)),
                resident((share, feature)),
                resident((8, vec_lanes)),
            ],
            scratch_shapes=[
                pltpu.VMEM((message_rows, feature), BF16),
                pltpu.VMEM((message_rows, 3 * feature), BF16),
            ],
        ),
        out_shape=(
            jax.ShapeDtypeStruct((message_rows, feature), BF16),
            jax.ShapeDtypeStruct((share, 3 * feature), F32),
            jax.ShapeDtypeStruct((share, feature), F32),
            jax.ShapeDtypeStruct((8, vec_lanes), F32),
        ),
        compiler_params=params(40),
        cost_estimate=cost(20 * message_rows * feature * feature, 10 * feature * feature),
        name="message_backward",
    )(
        place[None].astype(jnp.int32), message_all, allowed, message_low, joined, mixed,
        stacked, stacked, msg_in_w, msg_out_w,
    )
    messages_grad = lax.dynamic_slice(message_grad, (0, tok * piece), (group_frames, piece)).reshape(
        messages.shape
    )
    msg_vec = msg_vec[:, :share]

    def scatter(grad):
        return lax.psum_scatter(grad, both, scatter_dimension=0, tiled=True)

    if packed:
        def side_by_side(parts):
            return parts.transpose(1, 0, 2).reshape(share, -1)

        ready = attn_sum.step(message_grad)
        ready = ff_sum.step(ready)
        ready = attn_sum.step(ready)
        attn = ready = attn_sum.end(ready)
        ff = ff_sum.end(ready)
        attn_in_w_grad = side_by_side(attn[: 3 * across])
        own_vec = attn[3 * across].T
        count = across * chunks
        fc_w_grad = side_by_side(ff[:count])
        attn_out_w_grad = side_by_side(ff[count : count + across])
        proj_parts = ff[count + across :].reshape(chunks, across, share, columns)
        proj_w_grad = proj_parts.transpose(0, 2, 1, 3).reshape(chunks * share, feature)
    else:
        proj_w_grad = scatter(proj_grads[0])
        fc_w_grad = scatter(fc_grads[0][:chunks].transpose(1, 0, 2).reshape(feature, hidden_units))
        attn_out_w_grad = scatter(fc_grads[0][chunks])
        attn_in_w_grad = scatter(attn_grads[0][:3].transpose(1, 0, 2).reshape(feature, 3 * feature))
        own_vec = scatter(attn_grads[0][3, :, :LANES]).T
    fc_b_grad = own_vec[8 : 8 + chunks].reshape(-1)

    return (
        output,
        frames_grad,
        messages_grad,
        msg_vec[0],
        msg_vec[1],
        msg_in_w_grad,
        msg_vec[2:4],
        msg_out_w_grad,
        msg_vec[4],
        own_vec[2],
        own_vec[3],
        attn_in_w_grad,
        own_vec[:2],
        attn_out_w_grad,
        own_vec[6],
        own_vec[4],
        own_vec[5],
        fc_w_grad,
        fc_b_grad,
        proj_w_grad,
        own_vec[7],
    )


def solution(mesh):
    tokens = P("vid", None, "tok", None)
    rows, columns, one = P(("vid", "tok"), None), P(None, ("vid", "tok")), P(("vid", "tok"))
    in_specs = (tokens, P("vid", None, "tok"), P("vid"), tokens) + (P(),) * 18
    out_specs = (
        tokens, tokens, P("vid", None, "tok"),
        one, one, rows, columns, rows, one,
        one, one, rows, columns, rows, one,
        one, one, rows, one, rows, one,
    )
    return jax.shard_map(
        partial(shards, mesh.shape["vid"], mesh.shape["tok"]),
        mesh=mesh,
        in_specs=in_specs,
        out_specs=out_specs,
        check_vma=False,
    )
```

```python
from functools import partial

import jax
import jax.numpy as jnp
from jax import lax
from jax.experimental import pallas as pl
from jax.experimental.pallas import tpu as pltpu
from jax.sharding import PartitionSpec as P

HEADS = 12
HEAD = 64
PATCHES = 197
PAIR = 2 * HEAD
EPS = 1e-05
NEG = -1000000000.0
SLOPE = 1.702
F32 = jnp.float32
BF16 = jnp.bfloat16
MIB = 2**20

KEY_ROWS = (PATCHES + 1 + 15) // 16 * 16


def norm_parts(tensor):
    row_mean = jnp.mean(tensor, axis=-1, keepdims=True)
    centred = tensor - row_mean
    spread = jnp.mean(centred * centred, axis=-1, keepdims=True)
    inverse = lax.rsqrt(spread + EPS)
    return centred * inverse, inverse


def norm_back(grad_in, normed, inverse, gain):
    scaled = grad_in * gain
    return inverse * (
        scaled
        - jnp.mean(scaled, axis=-1, keepdims=True)
        - normed * jnp.mean(scaled * normed, axis=-1, keepdims=True)
    )


def dot_nn(left, right):
    return lax.dot_general(left, right, (((1,), (0,)), ((), ())), preferred_element_type=F32)


def dot_nt(left, right):
    return lax.dot_general(left, right, (((1,), (1,)), ((), ())), preferred_element_type=F32)


def dot_tn(left, right):
    return lax.dot_general(left, right, (((0,), (0,)), ((), ())), preferred_element_type=F32)


def lane_masks(dtype=BF16):
    lane = lax.broadcasted_iota(jnp.int32, (1, PAIR), 1)
    first = jnp.where(lane < HEAD, 1.0, 0.0)
    return first.astype(dtype), (1.0 - first).astype(dtype)


def column_sum(rows):
    return jnp.sum(rows, axis=0, keepdims=True)


def message_forward_kernel(
    msg_ref, allow_ref, gain_ref, shift_ref, in_w_ref, in_b_ref, out_w_ref, out_b_ref,
    joined_ref, mixed_ref, new_ref,
):
    feature = msg_ref.shape[1]
    message = msg_ref[...].astype(F32)
    normed, _ = norm_parts(message)
    hidden = (normed * gain_ref[...] + shift_ref[...]).astype(BF16)
    in_b = in_b_ref[...].astype(F32)
    for block in range(3):
        cols = slice(block * feature, (block + 1) * feature)
        part = dot_nn(hidden, in_w_ref[:, cols])
        if block != 1:
            part = part + in_b[block // 2 : block // 2 + 1]
        joined_ref[:, cols] = part.astype(BF16)
    allowed = allow_ref[...] > 0.5
    masks = lane_masks()
    scale = jnp.asarray(HEAD**-0.5, BF16)
    for pair in range(HEADS // 2):
        cols = slice(pair * PAIR, (pair + 1) * PAIR)
        query = joined_ref[:, cols]
        keys = joined_ref[:, feature + pair * PAIR : feature + (pair + 1) * PAIR]
        values = joined_ref[:, 2 * feature + pair * PAIR : 2 * feature + (pair + 1) * PAIR]
        total = None
        for mask in masks:
            score = dot_nt(query * (mask * scale), keys)
            score = jnp.where(allowed, score, NEG)
            weight = jnp.exp(score - jnp.max(score, axis=-1, keepdims=True))
            weight = weight / jnp.sum(weight, axis=-1, keepdims=True)
            part = dot_nn(weight.astype(BF16), values * mask)
            total = part if total is None else total + part
        mixed_ref[:, cols] = total.astype(BF16)
    new_ref[...] = message + (dot_nn(mixed_ref[...], out_w_ref[...]) + out_b_ref[...])


def message_backward_kernel(
    place_ref, msg_ref, allow_ref, low_ref, joined_ref, mixed_ref,
    gain_ref, shift_ref, in_w_ref, out_w_ref,
    grad_ref, in_w_grad_ref, out_w_grad_ref, vec_ref,
    mixed_grad_s, joined_grad_s,
):
    feature = msg_ref.shape[1]
    share = in_w_grad_ref.shape[0]
    message = msg_ref[...].astype(F32)
    normed, inverse = norm_parts(message)
    gain = gain_ref[...]
    hidden = (normed * gain + shift_ref[...]).astype(BF16)
    low = low_ref[...]
    low_wide = low.astype(F32)
    mixed_grad_s[...] = dot_nt(low, out_w_ref[...]).astype(BF16)
    allowed = allow_ref[...] > 0.5
    masks = lane_masks()
    scale = jnp.asarray(HEAD**-0.5, BF16)
    for pair in range(HEADS // 2):
        cols = slice(pair * PAIR, (pair + 1) * PAIR)
        key_cols = slice(feature + pair * PAIR, feature + (pair + 1) * PAIR)
        value_cols = slice(2 * feature + pair * PAIR, 2 * feature + (pair + 1) * PAIR)
        query = joined_ref[:, cols]
        keys = joined_ref[:, key_cols]
        values = joined_ref[:, value_cols]
        grad = mixed_grad_s[:, cols]
        grad_q = grad_k = grad_v = None
        for mask in masks:
            query_one = query * (mask * scale)
            grad_one = grad * mask
            score = jnp.where(allowed, dot_nt(query_one, keys), NEG)
            weight = jnp.exp(score - jnp.max(score, axis=-1, keepdims=True))
            weight = weight / jnp.sum(weight, axis=-1, keepdims=True)
            grad_weight = dot_nt(grad_one, values)
            inner = jnp.sum(weight * grad_weight, axis=-1, keepdims=True)
            grad_score = (weight * (grad_weight - inner)).astype(BF16)
            one_q = dot_nn(grad_score, keys * (mask * scale))
            one_k = dot_tn(grad_score, query_one)
            one_v = dot_tn(weight.astype(BF16), grad_one)
            grad_q = one_q if grad_q is None else grad_q + one_q
            grad_k = one_k if grad_k is None else grad_k + one_k
            grad_v = one_v if grad_v is None else grad_v + one_v
        joined_grad_s[:, cols] = grad_q.astype(BF16)
        joined_grad_s[:, key_cols] = grad_k.astype(BF16)
        joined_grad_s[:, value_cols] = grad_v.astype(BF16)
    joined_grad = joined_grad_s[...]
    hidden_grad = dot_nt(joined_grad, in_w_ref[...])
    grad_ref[...] = (low_wide + norm_back(hidden_grad, normed, inverse, gain)).astype(BF16)
    width = (share + 127) // 128 * 128
    row = lax.broadcasted_iota(jnp.int32, (feature, width), 0)
    col = lax.broadcasted_iota(jnp.int32, (feature, width), 1)
    pick = jnp.where((row == col + place_ref[0]) & (col < share), 1.0, 0.0)
    pick_low = pick.astype(BF16)
    own_hidden = dot_nn(hidden, pick_low).astype(BF16)
    own_mixed = dot_nn(mixed_ref[...], pick_low).astype(BF16)
    in_w_grad_ref[...] = dot_tn(own_hidden, joined_grad)[:share]
    out_w_grad_ref[...] = dot_tn(own_mixed, low)[:share]
    sums = jnp.concatenate(
        [
            column_sum(hidden_grad * normed),
            column_sum(hidden_grad),
            column_sum(joined_grad[:, :feature].astype(F32)),
            column_sum(joined_grad[:, 2 * feature :].astype(F32)),
            column_sum(low_wide),
            jnp.zeros((3, feature), F32),
        ],
        axis=0,
    )
    vec_ref[...] = lax.dot_general(
        sums, pick, (((1,), (0,)), ((), ())), precision=lax.Precision.HIGHEST, preferred_element_type=F32
    )


LANES = 128


def spread_rows(block_ref, scratch):
    sources, rows, _ = block_ref.shape
    for source in range(sources):
        for col in range(scratch.shape[0]):
            scratch[col, source * rows : (source + 1) * rows, :] = block_ref[
                source, :, col * LANES : (col + 1) * LANES
            ].astype(F32)


def gather_rows(scratch, block_ref):
    sources, rows, _ = block_ref.shape
    for source in range(sources):
        for col in range(scratch.shape[0]):
            block_ref[source, :, col * LANES : (col + 1) * LANES] = scratch[
                col, source * rows : (source + 1) * rows, :
            ].astype(BF16)


def take_frame(scratch, frame, count, stride):
    return jnp.concatenate(
        [scratch[col, pl.ds(frame, count, stride=stride), :] for col in range(scratch.shape[0])], axis=1
    )


def put_frame(scratch, frame, value, stride):
    for col in range(scratch.shape[0]):
        scratch[col, pl.ds(frame, value.shape[0], stride=stride), :] = value[:, col * LANES : (col + 1) * LANES]


def frame_places(slots, frame_slots, owned):
    for owner in range(frame_slots // owned):
        for frame in range(owned):
            yield owner, frame, owner * owned + frame


def to_owners_kernel(in_ref, out_ref, by_slot_s, by_owner_s):
    videos, slots, frame_slots, _ = in_ref.shape
    owners = out_ref.shape[0] // videos
    owned = frame_slots // owners
    for video in range(videos):
        for slot in range(slots):
            at = (video * slots + slot) * frame_slots
            for col in range(by_slot_s.shape[0]):
                by_slot_s[col, at : at + frame_slots, :] = in_ref[
                    video, slot, :, col * LANES : (col + 1) * LANES
                ].astype(F32)
        for owner, frame, place in frame_places(slots, frame_slots, owned):
            for col in range(by_slot_s.shape[0]):
                rows = by_slot_s[col, pl.ds(video * slots * frame_slots + place, slots, stride=frame_slots), :]
                first = (video * owners + owner) * slots * owned + frame
                by_owner_s[col, pl.ds(first, slots, stride=owned), :] = rows
    gather_rows(by_owner_s, out_ref)


def from_owners_kernel(parts, *refs):
    in_refs, out_ref, done_ref, by_owner_s, by_slot_s = refs[:parts], *refs[parts:]
    done_ref[...] = jnp.zeros_like(done_ref)
    videos, slots, frame_slots, _ = out_ref.shape
    owners = in_refs[0].shape[0] // videos
    owned = frame_slots // owners
    count = owned // parts
    for part, in_ref in enumerate(in_refs):
        spread_rows(in_ref, by_owner_s)
        size = in_ref.shape[1]
        for video in range(videos):
            for owner, frame, _ in frame_places(slots, frame_slots, owned):
                if frame >= count:
                    continue
                place = owner * owned + part * count + frame
                for col in range(by_slot_s.shape[0]):
                    first = (video * owners + owner) * size + frame
                    rows = by_owner_s[col, pl.ds(first, slots, stride=count), :]
                    by_slot_s[col, pl.ds(video * slots * frame_slots + place, slots, stride=frame_slots), :] = rows
    for video in range(videos):
        for slot in range(slots):
            at = (video * slots + slot) * frame_slots
            for col in range(by_slot_s.shape[0]):
                out_ref[video, slot, :, col * LANES : (col + 1) * LANES] = by_slot_s[
                    col, at : at + frame_slots, :
                ].astype(BF16)


def last_rows_kernel(at, in_ref, out_ref):
    for source in range(out_ref.shape[0]):
        out_ref[source] = in_ref[source, at:, :][: out_ref.shape[1]]


def attention_forward_kernel(
    owned, x_ref, new_ref, gain_ref, shift_ref, in_w_ref, in_b_ref, out_w_ref, out_b_ref,
    query_ref, keyval_ref, mixed_ref, lse_ref, resid_ref, tokens_ref, hidden_ref,
    rows_s,
):
    feature = x_ref.shape[2]
    slot_count = query_ref.shape[1]
    frame = pl.program_id(0)

    @pl.when(frame == 0)
    def _():
        spread_rows(x_ref, rows_s)

    gain = gain_ref[...]
    shift = shift_ref[...]
    frame_in = take_frame(rows_s, frame, slot_count, owned)
    normed, _ = norm_parts(frame_in)
    hidden = normed * gain + shift
    msg_normed, _ = norm_parts(new_ref[0])
    msg_hidden = msg_normed * gain + shift
    key_row = lax.broadcasted_iota(jnp.int32, (KEY_ROWS, 1), 0)
    tokens_ref[0] = jnp.where(key_row == PATCHES, new_ref[0], frame_in[:KEY_ROWS])
    hidden_kv = jnp.where(key_row == PATCHES, msg_hidden, hidden[:KEY_ROWS]).astype(BF16)
    hidden_ref[0] = hidden_kv
    hidden = hidden.astype(BF16)
    in_b = in_b_ref[...].astype(F32)
    query_ref[0] = (dot_nn(hidden, in_w_ref[:, :feature]) + in_b[0:1]).astype(BF16)
    keyval_ref[0, :, :feature] = dot_nn(hidden_kv, in_w_ref[:, feature : 2 * feature]).astype(BF16)
    keyval_ref[0, :, feature:] = (
        dot_nn(hidden_kv, in_w_ref[:, 2 * feature :]) + in_b[1:2]
    ).astype(BF16)
    allowed = key_row <= PATCHES
    masks = lane_masks()
    scale = jnp.asarray(HEAD**-0.5, BF16)
    for pair in range(HEADS // 2):
        cols = slice(pair * PAIR, (pair + 1) * PAIR)
        query = query_ref[0, :, cols]
        keys = keyval_ref[0, :, cols]
        values = keyval_ref[0, :, feature + pair * PAIR : feature + (pair + 1) * PAIR]
        total = None
        for side, mask in enumerate(masks):
            score = dot_nt(keys, query * (mask * scale))
            score = jnp.where(allowed, score, NEG)
            peak = jnp.max(score, axis=0, keepdims=True)
            weight = jnp.exp(score - peak)
            norm = jnp.sum(weight, axis=0, keepdims=True)
            lse_ref[0, 2 * pair + side : 2 * pair + side + 1, :] = peak + jnp.log(norm)
            weight = (weight * (1.0 / norm)).astype(BF16)
            part = dot_tn(weight, values * mask)
            total = part if total is None else total + part
        mixed_ref[0, :, cols] = total.astype(BF16)
    resid_ref[0] = take_frame(rows_s, frame, slot_count, owned) + (
        dot_nn(mixed_ref[0], out_w_ref[...]) + out_b_ref[...]
    )


def feed_forward_kernel(
    resid_ref, gain_ref, shift_ref, fc_w_ref, fc_b_ref, proj_w_ref, proj_b_ref,
    out_ref, hidden_low_ref, act_ref, slope_ref,
    hidden_s, out_s, rows_s,
):
    step = pl.program_id(0)
    frames, slot_count, feature = resid_ref.shape

    @pl.when(step == 0)
    def _():
        gain = gain_ref[...]
        shift = shift_ref[...]
        for frame in range(frames):
            normed, _ = norm_parts(resid_ref[frame])
            hidden = (normed * gain + shift).astype(BF16)
            hidden_s[frame * slot_count : (frame + 1) * slot_count, :] = hidden
            hidden_low_ref[frame * KEY_ROWS : (frame + 1) * KEY_ROWS, :] = hidden[:KEY_ROWS]
        out_s[...] = jnp.zeros_like(out_s)

    fc_b = fc_b_ref[...]
    batch = 2 if frames % 2 == 0 else 1
    batches = frames // batch
    size = batch * slot_count

    def pre_of(index):
        return dot_nn(hidden_s[index * size : (index + 1) * size, :], fc_w_ref[...]) + fc_b

    pre = pre_of(0)
    for index in range(batches):
        later = pre_of(index + 1) if index + 1 < batches else None
        gate = 0.5 + 0.5 * jnp.tanh((0.5 * SLOPE) * pre)
        active = pre * gate
        slope = (gate + SLOPE * active * (1.0 - gate)).astype(BF16)
        active = active.astype(BF16)
        for frame in range(batch):
            at = (index * batch + frame) * KEY_ROWS
            rows = slice(frame * slot_count, frame * slot_count + KEY_ROWS)
            slope_ref[at : at + KEY_ROWS, :] = slope[rows]
            act_ref[at : at + KEY_ROWS, :] = active[rows]
        out_s[index * size : (index + 1) * size, :] += dot_nn(active, proj_w_ref[...])
        pre = later

    @pl.when(step == pl.num_programs(0) - 1)
    def _():
        proj_b = proj_b_ref[...]
        for frame in range(frames):
            rows = out_s[frame * slot_count : (frame + 1) * slot_count, :]
            put_frame(rows_s, frame, resid_ref[frame] + (rows + proj_b), frames)
        gather_rows(rows_s, out_ref)


def owner_slots(table_ref, vids, depth, for_send):
    base = vids if for_send else 0
    for vid in range(vids):
        for level in range(depth):
            swapped = (level % 2) * (depth // 2) + level // 2
            yield vid, level, (table_ref[base + vid], swapped ^ table_ref[2 * vids + 1])


def store_share(value, keep_ref, send_ref, table_ref, vids, chunk=0):
    depth = keep_ref.shape[1]
    share, width = keep_ref.shape[-2:]
    low_core = table_ref[2 * vids] == 0
    slots = zip(owner_slots(table_ref, vids, depth, False), owner_slots(table_ref, vids, depth, True))
    for (vid, level, kept), (_, _, sent) in slots:
        at = ((vid * depth + level) * 2) * share
        for part in range(value.shape[1] // width):
            cols = slice(part * width, (part + 1) * width)
            first = value[at : at + share, cols].astype(BF16)
            second = value[at + share : at + 2 * share, cols].astype(BF16)
            keep_ref[kept + (chunk + part,)] = jnp.where(low_core, first, second)
            send_ref[sent + (chunk + part,)] = jnp.where(low_core, second, first)


def store_rows(value, keep_ref, send_ref, table_ref, vids):
    _, depth, count, share, width = keep_ref.shape
    across = value.shape[1] // width
    low_core = table_ref[2 * vids] == 0
    for level in range(depth):
        place = ((level % 2) * (depth // 2) + level // 2) ^ table_ref[2 * vids + 1]
        for part in range(count):
            cols = slice(part % across * width, (part % across + 1) * width)
            at = (2 * level * (count // across) + part // across) * share
            first = value[at : at + share, cols].astype(BF16)
            at += count // across * share
            second = value[at : at + share, cols].astype(BF16)
            keep_ref[0, place, part] = jnp.where(low_core, first, second)
            send_ref[0, place, part] = jnp.where(low_core, second, first)


def feed_backward_kernel(
    packed, vids, table_ref, live_ref,
    cot_ref, resid_ref, hidden_low_ref, act_ref, slope_ref, mixed_ref, gain_ref, fc_w_ref, proj_w_ref, out_w_ref,
    *refs,
):
    resid_grad_ref, mixed_grad_ref, vec_ref, fc_b_ref = refs[:4]
    grads = refs[4:-7]
    grad_s, pre_grad_s, hidden_grad_s, low_s, resid_s, mixed_s, rows_s = refs[-7:]
    step = pl.program_id(0)
    last = pl.num_programs(0) - 1
    frames, _, feature = resid_grad_ref.shape

    def finish(grad):
        if packed:
            store_share(grad, grads[2], grads[3], table_ref, vids)
        else:
            grads[1][0] = grad

    @pl.when(step == 0)
    def _():
        hidden_grad_s[...] = jnp.zeros_like(hidden_grad_s)
        spread_rows(cot_ref, rows_s)
        row = lax.broadcasted_iota(jnp.int32, (KEY_ROWS, 1), 0)
        total = None
        for frame in range(frames):
            keep = (row < PATCHES) & (live_ref[frame] > 0)
            grad = jnp.where(keep, take_frame(rows_s, frame, KEY_ROWS, frames), 0.0)
            grad_s[frame * KEY_ROWS : (frame + 1) * KEY_ROWS, :] = grad.astype(BF16)
            total = column_sum(grad) if total is None else total + column_sum(grad)
        spare = vec_ref.shape[0] - 1
        vec_ref[:spare, :] = jnp.zeros((spare, feature), F32)
        vec_ref[spare:, :] = total

    @pl.when(step < frames)
    def _():
        at = pl.multiple_of(step * KEY_ROWS, 16)
        resid_s[pl.ds(at, KEY_ROWS), :] = resid_ref[0, :KEY_ROWS, :]
        mixed_s[pl.ds(at, KEY_ROWS), :] = mixed_ref[0, :KEY_ROWS, :]

    @pl.when(step < last)
    def _():
        grad_act = dot_nt(grad_s[...], proj_w_ref[...])
        proj_grad = dot_tn(act_ref[...], grad_s[...])
        pre_grad = (grad_act * slope_ref[...].astype(F32)).astype(BF16)
        pre_grad_s[...] = pre_grad
        fc_b_ref[pl.ds(step, 1), :] = column_sum(pre_grad.astype(F32))
        if packed:
            store_rows(proj_grad, grads[0], grads[1], table_ref, vids)
        else:
            grads[0][...] = proj_grad
        hidden_grad_s[...] += dot_nt(pre_grad, fc_w_ref[...])
        finish(dot_tn(hidden_low_ref[...], pre_grad_s[...]))

    @pl.when(step == last)
    def _():
        gain = gain_ref[...]
        gain_grad = jnp.zeros((1, feature), F32)
        shift_grad = jnp.zeros((1, feature), F32)
        bias_grad = jnp.zeros((1, feature), F32)
        for frame in range(frames):
            rows = slice(frame * KEY_ROWS, (frame + 1) * KEY_ROWS)
            normed, inverse = norm_parts(resid_s[rows, :])
            hidden_grad = hidden_grad_s[rows, :]
            gain_grad += column_sum(hidden_grad * normed)
            shift_grad += column_sum(hidden_grad)
            resid_grad = grad_s[rows, :].astype(F32) + norm_back(hidden_grad, normed, inverse, gain)
            resid_grad_ref[frame] = resid_grad
            low = resid_grad.astype(BF16)
            low_s[rows, :] = low
            bias_grad += column_sum(low.astype(F32))
        spare = vec_ref.shape[0] - 4
        vec_ref[spare : spare + 1, :] = gain_grad
        vec_ref[spare + 1 : spare + 2, :] = shift_grad
        vec_ref[spare + 2 : spare + 3, :] = bias_grad
        mixed_grad = dot_nt(low_s[...], out_w_ref[...]).astype(BF16)
        for frame in range(frames):
            mixed_grad_ref[frame] = mixed_grad[frame * KEY_ROWS : (frame + 1) * KEY_ROWS]
        finish(dot_tn(mixed_s[...], low_s[...]))


def pair_backward(query, keys, values, grad, lse_of, allowed, masks, scale):
    grad_q = grad_k = grad_v = None
    for side, mask in enumerate(masks):
        query_one = query * (mask * scale)
        grad_one = grad * mask
        score = dot_nt(keys, query_one)
        weight = jnp.where(allowed, jnp.exp(score - lse_of(side)), 0.0)
        grad_weight = dot_nt(values, grad_one)
        inner = jnp.sum(weight * grad_weight, axis=0, keepdims=True)
        grad_score = (weight * (grad_weight - inner)).astype(BF16)
        one_v = dot_nn(weight.astype(BF16), grad_one)
        one_k = dot_nn(grad_score, query_one)
        one_q = dot_tn(grad_score, keys * (mask * scale))
        grad_q = one_q if grad_q is None else grad_q + one_q
        grad_k = one_k if grad_k is None else grad_k + one_k
        grad_v = one_v if grad_v is None else grad_v + one_v
    return grad_q.astype(BF16), grad_k.astype(BF16), grad_v.astype(BF16)


def attention_backward_kernel(
    packed, vids, first, count, final, table_ref,
    tokens_ref, query_ref, keyval_ref, lse_ref, mixed_grad_ref, resid_grad_ref, gain_ref, in_w_ref, earlier_ref, *refs,
):
    if final:
        hidden_ref, fc_b_ref, *others = refs[: -7 if packed else -6]
        refs = refs[len(others) + 2 :]
    frame_grad_ref, joined_ref, small_ref = refs[:3]
    rows_s = refs[-1] if not final else refs[-2]
    step = pl.program_id(0)
    feature = tokens_ref.shape[2]

    @pl.when(step < count)
    def _():
        gain = gain_ref[...]
        key_row = lax.broadcasted_iota(jnp.int32, (KEY_ROWS, 1), 0)
        allowed = key_row <= PATCHES
        masks = lane_masks()
        scale = jnp.asarray(HEAD**-0.5, BF16)
        for pair in range(HEADS // 2):
            cols = slice(pair * PAIR, (pair + 1) * PAIR)
            value_cols = slice(feature + pair * PAIR, feature + (pair + 1) * PAIR)

            def lse_of(side, head=2 * pair):
                return lse_ref[0, head + side : head + side + 1, :KEY_ROWS]

            grads = pair_backward(
                query_ref[0, :KEY_ROWS, cols], keyval_ref[0, :, cols], keyval_ref[0, :, value_cols],
                mixed_grad_ref[0, :, cols], lse_of, allowed, masks, scale,
            )
            for block, value in enumerate(grads):
                joined_ref[0, :, block * feature + pair * PAIR : block * feature + (pair + 1) * PAIR] = value
        joined = joined_ref[0]
        hidden_grad = dot_nt(joined, in_w_ref[...])
        normed, inverse = norm_parts(tokens_ref[0])
        tokens_grad = norm_back(hidden_grad, normed, inverse, gain)
        frame_grad = jnp.where(key_row < PATCHES, resid_grad_ref[0] + tokens_grad, 0.0)
        put_frame(rows_s, step, frame_grad, count)

        @pl.when(step == 0)
        def _():
            small_ref[...] = earlier_ref[...]

        sums = small_ref.shape[0] - 8
        small_ref[pl.ds(first + step, 1), :] = tokens_grad[PATCHES : PATCHES + 1]
        small_ref[sums : sums + 1, :] += column_sum(joined[:, :feature].astype(F32))
        small_ref[sums + 1 : sums + 2, :] += column_sum(joined[:, 2 * feature :].astype(F32))
        small_ref[sums + 2 : sums + 3, :] += column_sum(hidden_grad * normed)
        small_ref[sums + 3 : sums + 4, :] += column_sum(hidden_grad)
        if final:
            joined_s = refs[-1]
            joined_s[pl.ds(pl.multiple_of(step * KEY_ROWS, 16), KEY_ROWS), :] = joined

        @pl.when(step == count - 1)
        def _():
            live = count * KEY_ROWS
            rows_s[:, live:, :] = jnp.zeros((rows_s.shape[0], rows_s.shape[1] - live, LANES), F32)
            sources, size, _ = frame_grad_ref.shape
            rows = rows_s.shape[1] // sources
            for source in range(sources):
                for col in range(rows_s.shape[0]):
                    frame_grad_ref[source, :rows, col * LANES : (col + 1) * LANES] = rows_s[
                        col, source * rows : (source + 1) * rows, :
                    ].astype(BF16)
            if final:
                extra = jnp.concatenate([small_ref[:sums, :], jnp.zeros((size - rows - sums, feature), F32)])
                for source in range(sources):
                    frame_grad_ref[source, rows:, :] = extra.astype(BF16)

    if not final:
        return
    outs = refs[3:-2]
    joined_s = refs[-1]
    across = feature // LANES

    for block in range(3):

        @pl.when(step == count + block)
        def _(block=block):
            cols = slice(block * feature, (block + 1) * feature)
            split = len(others) * count * KEY_ROWS
            grad = dot_tn(hidden_ref[split:, :], joined_s[:, cols])
            for part, other in enumerate(others):
                size = count * KEY_ROWS
                grad = grad + dot_tn(hidden_ref[part * size : (part + 1) * size, :], other[:, cols])
            if packed:
                store_share(grad, outs[0], outs[1], table_ref, vids, block * across)
            else:
                outs[0][block] = grad

    @pl.when(step == count + 3)
    def _():
        sums = jnp.concatenate([small_ref[small_ref.shape[0] - 8 :, :], fc_b_ref[...]])
        row = lax.broadcasted_iota(jnp.int32, (sums.shape[0], LANES), 0)
        col = lax.broadcasted_iota(jnp.int32, (sums.shape[0], LANES), 1)
        turned = lax.dot_general(
            sums, jnp.where(row == col, 1.0, 0.0), (((0,), (0,)), ((), ())),
            precision=lax.Precision.HIGHEST, preferred_element_type=F32,
        )
        if packed:
            store_share(turned, outs[0], outs[1], table_ref, vids, 3 * across)
        else:
            outs[0][3] = jnp.concatenate([turned] * across, axis=1)


def sum_kernel(groups, wholes, *refs):
    out_ref = refs[-1]
    at, first = 0, wholes
    for count in groups:
        rows = refs[first].shape[1]
        value = refs[first][...].astype(F32)
        for ref in refs[first + 1 : first + count]:
            value = value + ref[...].astype(F32)
        for ref in refs[:wholes]:
            value = value + ref[:, at : at + rows, :].astype(F32)
        out_ref[:, at : at + rows, :] = value.astype(out_ref.dtype)
        at += rows
        first += count


def final_sum_kernel(terms, share, columns, *refs):
    in_refs, out_refs = refs[:terms], refs[terms:]
    block = 0

    def next_block():
        rows = slice(block * share, (block + 1) * share)
        value = in_refs[0][rows, :].astype(F32)
        for ref in in_refs[1:]:
            value = value + ref[rows, :].astype(F32)
        return value

    for out_ref, shape in zip(out_refs, columns):
        if shape is None:
            out_ref[...] = jnp.transpose(next_block())[: out_ref.shape[0]]
            block += 1
            continue
        for row in range(shape[0]):
            for col in range(shape[1]):
                out_ref[row * share : (row + 1) * share, col * LANES : (col + 1) * LANES] = next_block()
                block += 1


def resident(shape):
    return pl.BlockSpec(shape, lambda *_: (0,) * len(shape), pipeline_mode=pl.Buffered(1))


def params(mebibytes):
    return pltpu.CompilerParams(vmem_limit_bytes=60 * MIB)


def cost(flops, nbytes, transcendentals=0):
    return pl.CostEstimate(
        flops=10 * int(flops), bytes_accessed=10 * int(nbytes), transcendentals=10 * int(transcendentals)
    )


def with_ready(kernel, at, count):
    def body(*refs):
        kernel(*refs[:at], *refs[at + count :])

    return body


def ready_specs(count):
    return [pl.BlockSpec(memory_space=pl.ANY)] * count


def after(value, ready):
    return lax.optimization_barrier((value, ready))[0]


def add(left, right):
    return (left.astype(F32) + right.astype(F32)).astype(BF16)


def shards(
    vids, toks,
    frames, messages, frame_counts, cotangent,
    msg_gain, msg_shift, msg_in_w, msg_in_b, msg_out_w, msg_out_b,
    ln1_gain, ln1_shift, attn_in_w, attn_in_b, attn_out_w, attn_out_b,
    ln2_gain, ln2_shift, fc_w, fc_b, proj_w, proj_b,
):
    video_count, frame_slots, slots, feature = frames.shape
    devices = vids * toks
    group_frames = video_count * frame_slots
    owned = group_frames // toks
    owners = toks // video_count
    slot_count = slots * toks
    hidden_units = fc_w.shape[1]
    chunks = hidden_units // feature
    share = feature // devices
    vid = lax.axis_index("vid")
    tok = lax.axis_index("tok")
    core = tok % 2
    both = ("vid", "tok")
    depth = toks // 2
    packed = vids == 4 and toks == 8 and share % 8 == 0

    vectors = [msg_gain, msg_shift, msg_out_b, ln1_gain, ln1_shift, attn_out_b, ln2_gain, ln2_shift, proj_b]
    stacked = jnp.stack(vectors + [fc_b[at : at + feature] for at in range(0, hidden_units, feature)])
    stacked = stacked.astype(F32).reshape(-1, 1, feature)

    def row(index):
        return pl.BlockSpec((None, 1, feature), lambda *_: (index, 0, 0))

    def exchange(blocks):
        return lax.all_to_all(blocks, "tok", split_axis=0, concat_axis=0, tiled=True)

    slot_shape = (video_count, slots, frame_slots, feature)
    slot_scratch = pltpu.VMEM((feature // LANES, group_frames * slots, LANES), F32)

    def by_owner(tokens):
        return pl.pallas_call(
            to_owners_kernel,
            grid=(1,),
            in_specs=[resident(slot_shape)],
            out_specs=resident((toks, slots * owned, feature)),
            out_shape=jax.ShapeDtypeStruct((toks, slots * owned, feature), BF16),
            scratch_shapes=[slot_scratch, slot_scratch],
            compiler_params=params(40),
            cost_estimate=cost(0, slots * feature),
            name="to_owners",
        )(tokens.transpose(0, 2, 1, 3))

    def from_owners(blocks, ready=()):
        by_slot, done = pl.pallas_call(
            with_ready(partial(from_owners_kernel, len(blocks)), len(blocks), len(ready)),
            grid=(1,),
            in_specs=[resident(block.shape) for block in blocks] + ready_specs(len(ready)),
            out_specs=[resident(slot_shape), resident((8, LANES))],
            out_shape=[jax.ShapeDtypeStruct(slot_shape, BF16), jax.ShapeDtypeStruct((8, LANES), F32)],
            scratch_shapes=[
                pltpu.VMEM((feature // LANES, toks * max(block.shape[1] for block in blocks), LANES), F32),
                slot_scratch,
            ],
            compiler_params=params(40),
            cost_estimate=cost(0, slots * feature),
            name="from_owners",
        )(*blocks, *ready)
        return by_slot.transpose(0, 2, 1, 3), done

    def swap(rows, axis, size, bit):
        return lax.ppermute(rows, axis, [(i, i ^ bit) for i in range(size)])

    def over_levels(rows):
        return [rows] + [swap(rows, "tok", toks, 2 * step) for step in range(1, depth)]

    def in_order(rows):
        rows = rows.reshape((2, depth) + rows.shape[2:]).swapaxes(0, 1)
        rows = rows.reshape((toks,) + rows.shape[2:])
        bit = 1
        while bit < toks:
            pairs = rows.reshape((toks // (2 * bit), 2, bit) + rows.shape[1:])
            turned = jnp.where((tok // bit) % 2 == 1, pairs[:, ::-1], pairs)
            rows = turned.reshape(rows.shape)
            bit *= 2
        return rows

    group_index = jnp.arange(group_frames, dtype=jnp.int32)
    live_group = group_index % frame_slots < jnp.repeat(frame_counts, frame_slots)
    piece = messages.shape[-1]
    width = (piece + 1 + 127) // 128 * 128
    payload = jnp.concatenate(
        [
            messages.reshape(group_frames, piece),
            live_group.astype(BF16)[:, None],
            jnp.zeros((group_frames, width - piece - 1), BF16),
        ],
        axis=1,
    )
    x_blocks = by_owner(frames)
    levels = over_levels(after(payload, x_blocks))
    x_blocks = exchange(after(x_blocks, levels))
    gathered = jnp.stack(levels)
    gathered = in_order(jnp.stack([gathered, swap(gathered, "tok", toks, 1)]))[None]
    bit = 1
    while bit < vids:
        gathered = jnp.concatenate([gathered, swap(gathered, "vid", vids, bit)])
        bit *= 2
    message_rows = vids * group_frames
    message_all = gathered[..., :piece].transpose(0, 2, 1, 3).reshape(message_rows, feature)
    live_all = gathered[:, 0, :, piece].reshape(message_rows) > 0.5
    row_video = jnp.arange(message_rows, dtype=jnp.int32) // frame_slots
    allowed = ((row_video[:, None] == row_video[None, :]) & live_all[None, :]).astype(F32)

    joined, mixed, message_new = pl.pallas_call(
        message_forward_kernel,
        grid=(1,),
        in_specs=[
            resident((message_rows, feature)),
            resident((message_rows, message_rows)),
            row(0),
            row(1),
            resident((feature, 3 * feature)),
            resident((2, feature)),
            resident((feature, feature)),
            row(2),
        ],
        out_specs=[
            resident((message_rows, 3 * feature)),
            resident((message_rows, feature)),
            resident((message_rows, feature)),
        ],
        out_shape=(
            jax.ShapeDtypeStruct((message_rows, 3 * feature), BF16),
            jax.ShapeDtypeStruct((message_rows, feature), BF16),
            jax.ShapeDtypeStruct((message_rows, feature), F32),
        ),
        compiler_params=params(40),
        cost_estimate=cost(8 * message_rows * feature * feature, 8 * feature * feature),
        name="message_forward",
    )(
        message_all, allowed, stacked, stacked, msg_in_w, msg_in_b, msg_out_w, stacked,
    )
    cot_blocks = exchange(after(by_owner(cotangent), (x_blocks, message_new)))
    own_new = lax.dynamic_slice(message_new, (tok * owned, 0), (owned, feature)).reshape(owned, 1, feature)

    rows = owned * slot_count
    live_rows = owned * KEY_ROWS
    blocks_shape = (toks, slots * owned, feature)
    columns_shape = (feature // LANES, rows, LANES)

    def by_frame(*tail):
        return pl.BlockSpec((1,) + tail, lambda f, *_: (f,) + (0,) * len(tail))

    query, keyval, attended, lse, resid, tokens, hidden_kv = pl.pallas_call(
        partial(attention_forward_kernel, owned),
        grid=(owned,),
        in_specs=[
            resident(blocks_shape),
            by_frame(1, feature),
            row(3),
            row(4),
            resident((feature, 3 * feature)),
            resident((2, feature)),
            resident((feature, feature)),
            row(5),
        ],
        out_specs=[
            by_frame(slot_count, feature),
            by_frame(KEY_ROWS, 2 * feature),
            by_frame(slot_count, feature),
            by_frame(HEADS, slot_count),
            by_frame(slot_count, feature),
            by_frame(KEY_ROWS, feature),
            by_frame(KEY_ROWS, feature),
        ],
        out_shape=(
            jax.ShapeDtypeStruct((owned, slot_count, feature), BF16),
            jax.ShapeDtypeStruct((owned, KEY_ROWS, 2 * feature), BF16),
            jax.ShapeDtypeStruct((owned, slot_count, feature), BF16),
            jax.ShapeDtypeStruct((owned, HEADS, slot_count), F32),
            jax.ShapeDtypeStruct((owned, slot_count, feature), F32),
            jax.ShapeDtypeStruct((owned, KEY_ROWS, feature), F32),
            jax.ShapeDtypeStruct((owned, KEY_ROWS, feature), BF16),
        ),
        scratch_shapes=[pltpu.VMEM(columns_shape, F32)],
        compiler_params=params(40),
        cost_estimate=cost(10 * rows * feature * feature, 12 * rows * feature, rows * slot_count * HEADS),
        name="attention_forward",
    )(
        x_blocks, own_new, stacked, stacked, attn_in_w, attn_in_b, attn_out_w, stacked,
    )

    out_blocks, hidden_low, act, slope = pl.pallas_call(
        feed_forward_kernel,
        grid=(chunks,),
        in_specs=[
            resident((owned, slot_count, feature)),
            row(6),
            row(7),
            pl.BlockSpec((feature, feature), lambda j: (0, j)),
            pl.BlockSpec((None, 1, feature), lambda j: (9 + j, 0, 0)),
            pl.BlockSpec((feature, feature), lambda j: (j, 0)),
            row(8),
        ],
        out_specs=[
            resident(blocks_shape),
            resident((live_rows, feature)),
            pl.BlockSpec((live_rows, feature), lambda j: (0, j)),
            pl.BlockSpec((live_rows, feature), lambda j: (0, j)),
        ],
        out_shape=(
            jax.ShapeDtypeStruct(blocks_shape, BF16),
            jax.ShapeDtypeStruct((live_rows, feature), BF16),
            jax.ShapeDtypeStruct((live_rows, hidden_units), BF16),
            jax.ShapeDtypeStruct((live_rows, hidden_units), BF16),
        ),
        scratch_shapes=[
            pltpu.VMEM((rows, feature), BF16),
            pltpu.VMEM((rows, feature), F32),
            pltpu.VMEM(columns_shape, F32),
        ],
        compiler_params=params(48),
        cost_estimate=cost(4 * rows * feature * hidden_units, 12 * feature * hidden_units, rows * hidden_units),
        name="feed_forward",
    )(
        resid, stacked, stacked, fc_w, stacked, proj_w, stacked,
    )
    output_blocks = exchange(after(out_blocks, cot_blocks))

    own_index = tok * owned + jnp.arange(owned, dtype=jnp.int32)
    own_count = jnp.sum(
        jnp.where(
            (own_index // frame_slots)[:, None] == jnp.arange(video_count, dtype=jnp.int32)[None, :],
            frame_counts[None, :],
            0,
        ),
        axis=1,
    )
    own_live = (own_index % frame_slots < own_count).astype(jnp.int32)

    dest = jnp.arange(vids, dtype=jnp.int32)

    def slot_table(for_core):
        low_bit, high_bit = dest % 2 ^ vid % 2, dest // 2 ^ vid // 2
        return jnp.where(for_core == 0, 2 * low_bit + high_bit, 2 * high_bit + low_bit)

    level = tok // 2
    swapped = (level % 2) * (depth // 2) + level // 2
    table = jnp.concatenate([slot_table(core), slot_table(1 - core), core[None], swapped[None]]).astype(jnp.int32)

    def cross(bit_of_core):
        return [
            (v * toks + t, (v ^ bit_of_core[t % 2]) * toks + t) for v in range(vids) for t in range(toks)
        ]

    def send_over(stage, value):
        if stage == 0:
            return swap(value, "tok", toks, 1)
        if stage == 1:
            return lax.ppermute(value, both, cross((1, 2)))
        return lax.ppermute(value, both, cross((2, 1)))

    def sum_slots(parts, wholes, first, count, ready, dtype=BF16):
        batch = next(size for size in (4, 2, 1) if count % size == 0 and (size == 1 or count > size or len(parts) > 1))
        batch = min(batch, 2) if len(parts) > 1 else batch
        operands = list(wholes) + [term for terms in parts for term in terms]
        rows = sum(terms[0].shape[1] for terms in parts)
        return pl.pallas_call(
            with_ready(
                partial(sum_kernel, [len(terms) for terms in parts], len(wholes)), len(operands), len(ready)
            ),
            grid=(count // batch,),
            in_specs=[
                pl.BlockSpec((batch,) + term.shape[1:], lambda i: (first // batch + i, 0, 0)) for term in operands
            ]
            + ready_specs(len(ready)),
            out_specs=pl.BlockSpec((batch, rows, LANES), lambda i: (i, 0, 0)),
            out_shape=jax.ShapeDtypeStruct((count, rows, LANES), dtype),
            compiler_params=params(40),
            cost_estimate=cost(0, rows * LANES),
            name="sum_slots",
        )(*operands, *ready)

    class Sum:
        def __init__(self, *grads):
            self.parts = [[keep.reshape(keep.shape[0] * keep.shape[1], -1, LANES)] for keep, _ in grads]
            self.got = [send_over(0, send.reshape(vids * depth, -1, LANES)) for _, send in grads]
            self.slots = vids * depth
            self.stage = 0

        def step(self, *ready):
            self.stage += 1
            if self.stage == 1:
                self.parts = [terms + [got] for terms, got in zip(self.parts, self.got)]
                self.whole = []
            else:
                self.whole = self.whole + self.got
            if self.stage == 3:
                value = sum_slots(self.parts, self.whole, 0, depth, ready)
                self.whole, self.parts = [value[0]], []
                steps = [(at % 2) * (depth // 2) + at // 2 for at in range(depth)]
                self.got = [swap(value[at], "tok", toks, 2 * steps[at]) for at in range(1, depth)]
                return value
            self.slots //= 2
            send = sum_slots(self.parts, self.whole, self.slots, self.slots, ready)
            self.got = [send_over(self.stage, send)]
            return send

        def end(self, shapes, *ready):
            operands = self.whole + self.got
            out_shape = [
                jax.ShapeDtypeStruct((16, share) if shape is None else (shape[0] * share, shape[1] * LANES), F32)
                for shape in shapes
            ]
            return pl.pallas_call(
                with_ready(partial(final_sum_kernel, len(operands), share, shapes), len(operands), len(ready)),
                grid=(1,),
                in_specs=[resident(term.shape) for term in operands] + ready_specs(len(ready)),
                out_specs=[resident(out.shape) for out in out_shape],
                out_shape=out_shape,
                compiler_params=params(40),
                cost_estimate=cost(0, feature * LANES),
                name="final_sum",
            )(*operands, *ready)

    half = (vids, depth)
    across = feature // LANES
    columns = feature // across

    def packed_out(*tail):
        return [jax.ShapeDtypeStruct(half + tail, BF16)] * 2

    if packed:
        proj_specs = [
            pl.BlockSpec(
                (1, depth, across * chunks, share, columns),
                lambda j, table, live, base=base: (table[base + jnp.minimum(j, chunks - 1)], 0, 0, 0, 0),
            )
            for base in (0, vids)
        ]
        proj_shapes = packed_out(across * chunks, share, columns)
        fc_specs = [pl.BlockSpec(half + (across, share, columns), lambda j, *_: (0, 0, j, 0, 0)) for _ in range(2)]
        fc_shapes = packed_out(across * (chunks + 1), share, columns)
    else:
        proj_specs = [pl.BlockSpec((feature, feature), lambda j, *_: (jnp.minimum(j, chunks - 1), 0))]
        proj_shapes = [jax.ShapeDtypeStruct((hidden_units, feature), F32)]
        fc_specs = [pl.BlockSpec((1, feature, feature), lambda j, *_: (j, 0, 0))]
        fc_shapes = [jax.ShapeDtypeStruct((chunks + 1, feature, feature), F32)]
    small_rows = owned + 8

    def chunk(index):
        return jnp.minimum(index, chunks - 1)

    def frame_of(index):
        return jnp.minimum(index, owned - 1)

    resid_grad, mixed_grad, small, fc_b_part, *ff_grads = pl.pallas_call(
        partial(feed_backward_kernel, packed, vids),
        grid_spec=pltpu.PrefetchScalarGridSpec(
            num_scalar_prefetch=2,
            grid=(max(chunks, owned) + 1,),
            in_specs=[
                resident(blocks_shape),
                pl.BlockSpec((1, slot_count, feature), lambda j, *_: (frame_of(j), 0, 0)),
                resident((live_rows, feature)),
                pl.BlockSpec((live_rows, feature), lambda j, *_: (0, chunk(j))),
                pl.BlockSpec((live_rows, feature), lambda j, *_: (0, chunk(j))),
                pl.BlockSpec((1, slot_count, feature), lambda j, *_: (frame_of(j), 0, 0)),
                row(6),
                pl.BlockSpec((feature, feature), lambda j, *_: (0, chunk(j))),
                pl.BlockSpec((feature, feature), lambda j, *_: (chunk(j), 0)),
                resident((feature, feature)),
            ],
            out_specs=[
                resident((owned, KEY_ROWS, feature)),
                resident((owned, KEY_ROWS, feature)),
                resident((small_rows, feature)),
                resident((chunks, feature)),
            ]
            + proj_specs
            + fc_specs,
            scratch_shapes=[
                pltpu.VMEM((live_rows, feature), BF16),
                pltpu.VMEM((live_rows, feature), BF16),
                pltpu.VMEM((live_rows, feature), F32),
                pltpu.VMEM((live_rows, feature), BF16),
                pltpu.VMEM((live_rows, feature), F32),
                pltpu.VMEM((live_rows, feature), BF16),
                pltpu.VMEM(columns_shape, F32),
            ],
        ),
        out_shape=[
            jax.ShapeDtypeStruct((owned, KEY_ROWS, feature), F32),
            jax.ShapeDtypeStruct((owned, KEY_ROWS, feature), BF16),
            jax.ShapeDtypeStruct((small_rows, feature), F32),
            jax.ShapeDtypeStruct((chunks, feature), F32),
        ]
        + proj_shapes
        + fc_shapes,
        compiler_params=params(48),
        cost_estimate=cost(8 * rows * feature * hidden_units, 12 * feature * hidden_units),
        name="feed_backward",
    )(
        table, own_live, cot_blocks, resid, hidden_low, act, slope, attended, stacked, fc_w, proj_w, attn_out_w,
    )
    proj_grads, fc_grads = ff_grads[: len(proj_shapes)], ff_grads[len(proj_shapes) :]

    parts = 2 if owned % 2 == 0 else 1
    part_frames = owned // parts
    part_blocks = (toks, slots * part_frames, feature)

    if packed:
        attn_specs = [resident(half + (across * 3 + 1, share, columns))] * 2
        attn_shapes = packed_out(across * 3 + 1, share, columns)
    else:
        attn_specs = [resident((4, feature, feature))]
        attn_shapes = [jax.ShapeDtypeStruct((4, feature, feature), F32)]
    part_rows = part_frames * KEY_ROWS

    def attention_backward(part, small, others, ready):
        first = part * part_frames
        final = part == parts - 1

        def by_part(*tail):
            return pl.BlockSpec(
                (1,) + tail, lambda f, *_: (first + jnp.minimum(f, part_frames - 1),) + (0,) * len(tail)
            )

        extra, extra_specs, scratch = [], [], []
        out_blocks = part_blocks
        if final:
            out_blocks = (toks, slots * part_frames + (owned + 7) // 8 * 8, feature)
            extra = [hidden_kv.reshape(live_rows, feature), fc_b_own] + others
            extra_specs = [resident((live_rows, feature)), resident((chunks, feature))]
            extra_specs += [resident((part_rows, 3 * feature))] * len(others)
            scratch = [pltpu.VMEM((part_rows, 3 * feature), BF16)]
        return pl.pallas_call(
            with_ready(
                partial(attention_backward_kernel, packed, vids, first, part_frames, final),
                10 + len(extra),
                len(ready),
            ),
            grid_spec=pltpu.PrefetchScalarGridSpec(
                num_scalar_prefetch=1,
                grid=(part_frames + 4 * final,),
                in_specs=[
                    by_part(KEY_ROWS, feature),
                    by_part(slot_count, feature),
                    by_part(KEY_ROWS, 2 * feature),
                    by_part(HEADS, slot_count),
                    by_part(KEY_ROWS, feature),
                    by_part(KEY_ROWS, feature),
                    row(3),
                    resident((feature, 3 * feature)),
                    resident((small_rows, feature)),
                ]
                + extra_specs
                + ready_specs(len(ready)),
                out_specs=[
                    resident(out_blocks),
                    pl.BlockSpec(
                        (1, KEY_ROWS, 3 * feature), lambda f, *_: (jnp.minimum(f, part_frames - 1), 0, 0)
                    ),
                    resident((small_rows, feature)),
                ]
                + attn_specs * final,
                scratch_shapes=[pltpu.VMEM((feature // LANES, part_frames * slot_count, LANES), F32)] + scratch,
            ),
            out_shape=[
                jax.ShapeDtypeStruct(out_blocks, BF16),
                jax.ShapeDtypeStruct((part_frames, KEY_ROWS, 3 * feature), BF16),
                jax.ShapeDtypeStruct((small_rows, feature), F32),
            ]
            + attn_shapes * final,
            compiler_params=params(40),
            cost_estimate=cost(16 * rows * feature * feature // parts, 20 * rows * feature // parts),
            name="attention_backward",
        )(table, tokens, query, keyval, lse, mixed_grad, resid_grad, stacked, attn_in_w, small, *extra, *ready)

    if packed:
        ff_sum = Sum(fc_grads, proj_grads)
    ready = [output_blocks]
    fc_b_own = fc_b_part.reshape(devices, chunks, share).swapaxes(0, 1).reshape(chunks, feature)
    frame_blocks, joined_grads = [], []
    for part in range(parts):
        blocks, joined_grad, small, *attn_grads = attention_backward(part, small, joined_grads, ready)
        joined_grads.append(joined_grad.reshape(part_rows, 3 * feature))
        if packed and part == 0:
            ready = [ff_sum.step(small)]
            blocks = after(blocks, ready)
        frame_blocks.append(exchange(blocks))
    ready = small
    if packed:
        attn_sum = Sum(after(attn_grads, frame_blocks[: parts - 1]))
        ready = attn_sum.step(small)
        ready = ff_sum.step(ready)
    output, ready = from_owners([output_blocks], [ready])
    message_low = pl.pallas_call(
        with_ready(partial(last_rows_kernel, slots * part_frames), 1, 1),
        grid=(1,),
        in_specs=[resident(frame_blocks[-1].shape)] + ready_specs(1),
        out_specs=resident((toks, owned, feature)),
        out_shape=jax.ShapeDtypeStruct((toks, owned, feature), BF16),
        cost_estimate=cost(0, toks * feature),
        name="last_rows",
    )(frame_blocks[-1], ready)
    if packed:
        ready = ff_sum.step(message_low)
        ready = attn_sum.step(ready)
    message_low = message_low.reshape(group_frames, feature)
    bit = 1
    while bit < vids:
        message_low = message_low if bit == 1 else after(message_low, ready)
        message_low = jnp.concatenate([message_low, swap(message_low, "vid", vids, bit)])
        bit *= 2
    if packed:
        ready = attn_sum.step(message_low)
    frames_grad, done = from_owners(frame_blocks, [ready])

    place = (vid * toks + tok) * share
    vec_lanes = (share + 127) // 128 * 128
    message_grad, msg_in_w_grad, msg_out_w_grad, msg_vec = pl.pallas_call(
        with_ready(message_backward_kernel, 10, 1),
        grid_spec=pltpu.PrefetchScalarGridSpec(
            num_scalar_prefetch=1,
            grid=(1,),
            in_specs=[
                resident((message_rows, feature)),
                resident((message_rows, message_rows)),
                resident((message_rows, feature)),
                resident((message_rows, 3 * feature)),
                resident((message_rows, feature)),
                row(0),
                row(1),
                resident((feature, 3 * feature)),
                resident((feature, feature)),
            ]
            + ready_specs(1),
            out_specs=[
                resident((message_rows, feature)),
                resident((share, 3 * feature)),
                resident((share, feature)),
                resident((8, vec_lanes)),
            ],
            scratch_shapes=[
                pltpu.VMEM((message_rows, feature), BF16),
                pltpu.VMEM((message_rows, 3 * feature), BF16),
            ],
        ),
        out_shape=(
            jax.ShapeDtypeStruct((message_rows, feature), BF16),
            jax.ShapeDtypeStruct((share, 3 * feature), F32),
            jax.ShapeDtypeStruct((share, feature), F32),
            jax.ShapeDtypeStruct((8, vec_lanes), F32),
        ),
        compiler_params=params(40),
        cost_estimate=cost(message_rows * feature, message_rows * feature),
        name="message_backward",
    )(
        place[None].astype(jnp.int32), message_all, allowed, message_low, joined, mixed,
        stacked, stacked, msg_in_w, msg_out_w, done,
    )
    messages_grad = lax.dynamic_slice(message_grad, (0, tok * piece), (group_frames, piece)).reshape(
        messages.shape
    )
    msg_vec = msg_vec[:, :share]

    def scatter(grad):
        return lax.psum_scatter(grad, both, scatter_dimension=0, tiled=True)

    if packed:
        shapes = [(1, across * chunks), (1, across), (chunks, across)]
        fc_w_grad, attn_out_w_grad, proj_w_grad = ff_sum.end(shapes, done, messages_grad, msg_vec)
        attn_in_w_grad, own_vec = attn_sum.end([(1, 3 * across), None])
    else:
        proj_w_grad = scatter(proj_grads[0])
        fc_w_grad = scatter(fc_grads[0][:chunks].transpose(1, 0, 2).reshape(feature, hidden_units))
        attn_out_w_grad = scatter(fc_grads[0][chunks])
        attn_in_w_grad = scatter(attn_grads[0][:3].transpose(1, 0, 2).reshape(feature, 3 * feature))
        own_vec = scatter(attn_grads[0][3, :, :LANES]).T
    fc_b_grad = own_vec[8 : 8 + chunks].reshape(-1)

    return (
        output,
        frames_grad,
        messages_grad,
        msg_vec[0],
        msg_vec[1],
        msg_in_w_grad,
        msg_vec[2:4],
        msg_out_w_grad,
        msg_vec[4],
        own_vec[2],
        own_vec[3],
        attn_in_w_grad,
        own_vec[:2],
        attn_out_w_grad,
        own_vec[6],
        own_vec[4],
        own_vec[5],
        fc_w_grad,
        fc_b_grad,
        proj_w_grad,
        own_vec[7],
    )


def solution(mesh):
    tokens = P("vid", None, "tok", None)
    rows, columns, one = P(("vid", "tok"), None), P(None, ("vid", "tok")), P(("vid", "tok"))
    in_specs = (tokens, P("vid", None, "tok"), P("vid"), tokens) + (P(),) * 18
    out_specs = (
        tokens, tokens, P("vid", None, "tok"),
        one, one, rows, columns, rows, one,
        one, one, rows, columns, rows, one,
        one, one, rows, one, rows, one,
    )
    return jax.shard_map(
        partial(shards, mesh.shape["vid"], mesh.shape["tok"]),
        mesh=mesh,
        in_specs=in_specs,
        out_specs=out_specs,
        check_vma=False,
    )
```

```python
from functools import partial

import jax
import jax.numpy as jnp
from jax import lax
from jax.experimental import pallas as pl
from jax.experimental.pallas import tpu as pltpu
from jax.sharding import PartitionSpec as P

HEADS = 12
HEAD = 64
PATCHES = 197
PAIR = 2 * HEAD
EPS = 1e-05
NEG = -1000000000.0
SLOPE = 1.702
F32 = jnp.float32
BF16 = jnp.bfloat16
MIB = 2**20

KEY_ROWS = (PATCHES + 1 + 15) // 16 * 16


def norm_parts(tensor):
    row_mean = jnp.mean(tensor, axis=-1, keepdims=True)
    centred = tensor - row_mean
    spread = jnp.mean(centred * centred, axis=-1, keepdims=True)
    inverse = lax.rsqrt(spread + EPS)
    return centred * inverse, inverse


def norm_back(grad_in, normed, inverse, gain):
    scaled = grad_in * gain
    return inverse * (
        scaled
        - jnp.mean(scaled, axis=-1, keepdims=True)
        - normed * jnp.mean(scaled * normed, axis=-1, keepdims=True)
    )


def dot_nn(left, right):
    return lax.dot_general(left, right, (((1,), (0,)), ((), ())), preferred_element_type=F32)


def dot_nt(left, right):
    return lax.dot_general(left, right, (((1,), (1,)), ((), ())), preferred_element_type=F32)


def dot_tn(left, right):
    return lax.dot_general(left, right, (((0,), (0,)), ((), ())), preferred_element_type=F32)


def lane_masks(dtype=BF16):
    lane = lax.broadcasted_iota(jnp.int32, (1, PAIR), 1)
    first = jnp.where(lane < HEAD, 1.0, 0.0)
    return first.astype(dtype), (1.0 - first).astype(dtype)


def column_sum(rows):
    return jnp.sum(rows, axis=0, keepdims=True)


def message_forward_kernel(
    msg_ref, allow_ref, gain_ref, shift_ref, in_w_ref, in_b_ref, out_w_ref, out_b_ref,
    joined_ref, mixed_ref, new_ref,
):
    feature = msg_ref.shape[1]
    message = msg_ref[...].astype(F32)
    normed, _ = norm_parts(message)
    hidden = (normed * gain_ref[...] + shift_ref[...]).astype(BF16)
    in_b = in_b_ref[...].astype(F32)
    for block in range(3):
        cols = slice(block * feature, (block + 1) * feature)
        part = dot_nn(hidden, in_w_ref[:, cols])
        if block != 1:
            part = part + in_b[block // 2 : block // 2 + 1]
        joined_ref[:, cols] = part.astype(BF16)
    allowed = allow_ref[...] > 0.5
    masks = lane_masks()
    scale = jnp.asarray(HEAD**-0.5, BF16)
    for pair in range(HEADS // 2):
        cols = slice(pair * PAIR, (pair + 1) * PAIR)
        query = joined_ref[:, cols]
        keys = joined_ref[:, feature + pair * PAIR : feature + (pair + 1) * PAIR]
        values = joined_ref[:, 2 * feature + pair * PAIR : 2 * feature + (pair + 1) * PAIR]
        total = None
        for mask in masks:
            score = dot_nt(query * (mask * scale), keys)
            score = jnp.where(allowed, score, NEG)
            weight = jnp.exp(score - jnp.max(score, axis=-1, keepdims=True))
            weight = weight / jnp.sum(weight, axis=-1, keepdims=True)
            part = dot_nn(weight.astype(BF16), values * mask)
            total = part if total is None else total + part
        mixed_ref[:, cols] = total.astype(BF16)
    new_ref[...] = message + (dot_nn(mixed_ref[...], out_w_ref[...]) + out_b_ref[...])


def message_backward_kernel(
    place_ref, msg_ref, allow_ref, low_ref, joined_ref, mixed_ref,
    gain_ref, shift_ref, in_w_ref, out_w_ref,
    grad_ref, in_w_grad_ref, out_w_grad_ref, gain_grad_ref, shift_grad_ref, in_b_grad_ref, out_b_grad_ref,
    mixed_grad_s, joined_grad_s,
):
    feature = msg_ref.shape[1]
    share = in_w_grad_ref.shape[0]
    message = msg_ref[...].astype(F32)
    normed, inverse = norm_parts(message)
    gain = gain_ref[...]
    hidden = (normed * gain + shift_ref[...]).astype(BF16)
    low = low_ref[...]
    low_wide = low.astype(F32)
    mixed_grad_s[...] = dot_nt(low, out_w_ref[...]).astype(BF16)
    allowed = allow_ref[...] > 0.5
    masks = lane_masks()
    scale = jnp.asarray(HEAD**-0.5, BF16)
    for pair in range(HEADS // 2):
        cols = slice(pair * PAIR, (pair + 1) * PAIR)
        key_cols = slice(feature + pair * PAIR, feature + (pair + 1) * PAIR)
        value_cols = slice(2 * feature + pair * PAIR, 2 * feature + (pair + 1) * PAIR)
        query = joined_ref[:, cols]
        keys = joined_ref[:, key_cols]
        values = joined_ref[:, value_cols]
        grad = mixed_grad_s[:, cols]
        grad_q = grad_k = grad_v = None
        for mask in masks:
            query_one = query * (mask * scale)
            grad_one = grad * mask
            score = jnp.where(allowed, dot_nt(query_one, keys), NEG)
            weight = jnp.exp(score - jnp.max(score, axis=-1, keepdims=True))
            weight = weight / jnp.sum(weight, axis=-1, keepdims=True)
            grad_weight = dot_nt(grad_one, values)
            inner = jnp.sum(weight * grad_weight, axis=-1, keepdims=True)
            grad_score = (weight * (grad_weight - inner)).astype(BF16)
            one_q = dot_nn(grad_score, keys * (mask * scale))
            one_k = dot_tn(grad_score, query_one)
            one_v = dot_tn(weight.astype(BF16), grad_one)
            grad_q = one_q if grad_q is None else grad_q + one_q
            grad_k = one_k if grad_k is None else grad_k + one_k
            grad_v = one_v if grad_v is None else grad_v + one_v
        joined_grad_s[:, cols] = grad_q.astype(BF16)
        joined_grad_s[:, key_cols] = grad_k.astype(BF16)
        joined_grad_s[:, value_cols] = grad_v.astype(BF16)
    joined_grad = joined_grad_s[...]
    hidden_grad = dot_nt(joined_grad, in_w_ref[...])
    grad_ref[...] = (low_wide + norm_back(hidden_grad, normed, inverse, gain)).astype(BF16)
    width = (share + 127) // 128 * 128
    row = lax.broadcasted_iota(jnp.int32, (feature, width), 0)
    col = lax.broadcasted_iota(jnp.int32, (feature, width), 1)
    pick = jnp.where((row == col + place_ref[0]) & (col < share), 1.0, 0.0)
    pick_low = pick.astype(BF16)
    own_hidden = dot_nn(hidden, pick_low).astype(BF16)
    own_mixed = dot_nn(mixed_ref[...], pick_low).astype(BF16)
    in_w_grad_ref[...] = dot_tn(own_hidden, joined_grad)[:share]
    out_w_grad_ref[...] = dot_tn(own_mixed, low)[:share]
    sums = jnp.concatenate(
        [
            column_sum(hidden_grad * normed),
            column_sum(hidden_grad),
            column_sum(joined_grad[:, :feature].astype(F32)),
            column_sum(joined_grad[:, 2 * feature :].astype(F32)),
            column_sum(low_wide),
            jnp.zeros((3, feature), F32),
        ],
        axis=0,
    )
    own = lax.dot_general(
        sums, pick, (((1,), (0,)), ((), ())), precision=lax.Precision.HIGHEST, preferred_element_type=F32
    )
    gain_grad_ref[...] = own[0, :share]
    shift_grad_ref[...] = own[1, :share]
    in_b_grad_ref[...] = own[2:4, :share]
    out_b_grad_ref[...] = own[4, :share]


LANES = 128


def spread_rows(block_ref, scratch):
    sources, rows, _ = block_ref.shape
    for source in range(sources):
        for col in range(scratch.shape[0]):
            scratch[col, source * rows : (source + 1) * rows, :] = block_ref[
                source, :, col * LANES : (col + 1) * LANES
            ].astype(F32)


def gather_rows(scratch, block_ref):
    sources, rows, _ = block_ref.shape
    for source in range(sources):
        for col in range(scratch.shape[0]):
            block_ref[source, :, col * LANES : (col + 1) * LANES] = scratch[
                col, source * rows : (source + 1) * rows, :
            ].astype(BF16)


def take_frame(scratch, frame, count, stride):
    return jnp.concatenate(
        [scratch[col, pl.ds(frame, count, stride=stride), :] for col in range(scratch.shape[0])], axis=1
    )


def put_frame(scratch, frame, value, stride):
    for col in range(scratch.shape[0]):
        scratch[col, pl.ds(frame, value.shape[0], stride=stride), :] = value[:, col * LANES : (col + 1) * LANES]


def frame_places(slots, frame_slots, owned):
    for owner in range(frame_slots // owned):
        for frame in range(owned):
            yield owner, frame, owner * owned + frame


def to_owners_kernel(in_ref, out_ref, by_slot_s, by_owner_s):
    videos, slots, frame_slots, _ = in_ref.shape
    owners = out_ref.shape[0] // videos
    owned = frame_slots // owners
    for video in range(videos):
        for slot in range(slots):
            at = (video * slots + slot) * frame_slots
            for col in range(by_slot_s.shape[0]):
                by_slot_s[col, at : at + frame_slots, :] = in_ref[
                    video, slot, :, col * LANES : (col + 1) * LANES
                ].astype(F32)
        for owner, frame, place in frame_places(slots, frame_slots, owned):
            for col in range(by_slot_s.shape[0]):
                rows = by_slot_s[col, pl.ds(video * slots * frame_slots + place, slots, stride=frame_slots), :]
                first = (video * owners + owner) * slots * owned + frame
                by_owner_s[col, pl.ds(first, slots, stride=owned), :] = rows
    gather_rows(by_owner_s, out_ref)


def from_owners_kernel(parts, *refs):
    in_refs, out_ref, done_ref, by_owner_s, by_slot_s = refs[:parts], *refs[parts:]
    done_ref[...] = jnp.zeros_like(done_ref)
    videos, slots, frame_slots, _ = out_ref.shape
    owners = in_refs[0].shape[0] // videos
    owned = frame_slots // owners
    count = owned // parts
    for part, in_ref in enumerate(in_refs):
        spread_rows(in_ref, by_owner_s)
        size = in_ref.shape[1]
        for video in range(videos):
            for owner, frame, _ in frame_places(slots, frame_slots, owned):
                if frame >= count:
                    continue
                place = owner * owned + part * count + frame
                for col in range(by_slot_s.shape[0]):
                    first = (video * owners + owner) * size + frame
                    rows = by_owner_s[col, pl.ds(first, slots, stride=count), :]
                    by_slot_s[col, pl.ds(video * slots * frame_slots + place, slots, stride=frame_slots), :] = rows
    for video in range(videos):
        for slot in range(slots):
            at = (video * slots + slot) * frame_slots
            for col in range(by_slot_s.shape[0]):
                out_ref[video, slot, :, col * LANES : (col + 1) * LANES] = by_slot_s[
                    col, at : at + frame_slots, :
                ].astype(BF16)


def last_rows_kernel(at, in_ref, out_ref):
    for source in range(out_ref.shape[0]):
        out_ref[source] = in_ref[source, at:, :][: out_ref.shape[1]]


def attention_forward_kernel(
    owned, x_ref, new_ref, gain_ref, shift_ref, in_w_ref, in_b_ref, out_w_ref, out_b_ref,
    query_ref, keyval_ref, mixed_ref, lse_ref, resid_ref, tokens_ref, hidden_ref,
    rows_s,
):
    feature = x_ref.shape[2]
    slot_count = query_ref.shape[1]
    frame = pl.program_id(0)

    @pl.when(frame == 0)
    def _():
        spread_rows(x_ref, rows_s)

    gain = gain_ref[...]
    shift = shift_ref[...]
    frame_in = take_frame(rows_s, frame, slot_count, owned)
    normed, _ = norm_parts(frame_in)
    hidden = normed * gain + shift
    msg_normed, _ = norm_parts(new_ref[0])
    msg_hidden = msg_normed * gain + shift
    key_row = lax.broadcasted_iota(jnp.int32, (KEY_ROWS, 1), 0)
    tokens_ref[0] = jnp.where(key_row == PATCHES, new_ref[0], frame_in[:KEY_ROWS])
    hidden_kv = jnp.where(key_row == PATCHES, msg_hidden, hidden[:KEY_ROWS]).astype(BF16)
    hidden_ref[0] = hidden_kv
    hidden = hidden.astype(BF16)
    in_b = in_b_ref[...].astype(F32)
    query_ref[0] = (dot_nn(hidden, in_w_ref[:, :feature]) + in_b[0:1]).astype(BF16)
    keyval_ref[0, :, :feature] = dot_nn(hidden_kv, in_w_ref[:, feature : 2 * feature]).astype(BF16)
    keyval_ref[0, :, feature:] = (
        dot_nn(hidden_kv, in_w_ref[:, 2 * feature :]) + in_b[1:2]
    ).astype(BF16)
    allowed = key_row <= PATCHES
    masks = lane_masks()
    scale = jnp.asarray(HEAD**-0.5, BF16)
    for pair in range(HEADS // 2):
        cols = slice(pair * PAIR, (pair + 1) * PAIR)
        query = query_ref[0, :, cols]
        keys = keyval_ref[0, :, cols]
        values = keyval_ref[0, :, feature + pair * PAIR : feature + (pair + 1) * PAIR]
        total = None
        for side, mask in enumerate(masks):
            score = dot_nt(keys, query * (mask * scale))
            score = jnp.where(allowed, score, NEG)
            peak = jnp.max(score, axis=0, keepdims=True)
            weight = jnp.exp(score - peak)
            norm = jnp.sum(weight, axis=0, keepdims=True)
            lse_ref[0, 2 * pair + side : 2 * pair + side + 1, :] = peak + jnp.log(norm)
            weight = (weight * (1.0 / norm)).astype(BF16)
            part = dot_tn(weight, values * mask)
            total = part if total is None else total + part
        mixed_ref[0, :, cols] = total.astype(BF16)
    resid_ref[0] = take_frame(rows_s, frame, slot_count, owned) + (
        dot_nn(mixed_ref[0], out_w_ref[...]) + out_b_ref[...]
    )


def feed_forward_kernel(
    resid_ref, gain_ref, shift_ref, fc_w_ref, fc_b_ref, proj_w_ref, proj_b_ref,
    out_ref, hidden_low_ref, act_ref, slope_ref,
    hidden_s, out_s, rows_s,
):
    step = pl.program_id(0)
    frames, slot_count, feature = resid_ref.shape

    @pl.when(step == 0)
    def _():
        gain = gain_ref[...]
        shift = shift_ref[...]
        for frame in range(frames):
            normed, _ = norm_parts(resid_ref[frame])
            hidden = (normed * gain + shift).astype(BF16)
            hidden_s[frame * slot_count : (frame + 1) * slot_count, :] = hidden
            hidden_low_ref[frame * KEY_ROWS : (frame + 1) * KEY_ROWS, :] = hidden[:KEY_ROWS]
        out_s[...] = jnp.zeros_like(out_s)

    fc_b = fc_b_ref[...]
    batch = 2 if frames % 2 == 0 else 1
    batches = frames // batch
    size = batch * slot_count

    def pre_of(index):
        return dot_nn(hidden_s[index * size : (index + 1) * size, :], fc_w_ref[...]) + fc_b

    pre = pre_of(0)
    for index in range(batches):
        later = pre_of(index + 1) if index + 1 < batches else None
        gate = 0.5 + 0.5 * jnp.tanh((0.5 * SLOPE) * pre)
        active = pre * gate
        slope = (gate + SLOPE * active * (1.0 - gate)).astype(BF16)
        active = active.astype(BF16)
        for frame in range(batch):
            at = (index * batch + frame) * KEY_ROWS
            rows = slice(frame * slot_count, frame * slot_count + KEY_ROWS)
            slope_ref[at : at + KEY_ROWS, :] = slope[rows]
            act_ref[at : at + KEY_ROWS, :] = active[rows]
        out_s[index * size : (index + 1) * size, :] += dot_nn(active, proj_w_ref[...])
        pre = later

    @pl.when(step == pl.num_programs(0) - 1)
    def _():
        proj_b = proj_b_ref[...]
        for frame in range(frames):
            rows = out_s[frame * slot_count : (frame + 1) * slot_count, :]
            put_frame(rows_s, frame, resid_ref[frame] + (rows + proj_b), frames)
        gather_rows(rows_s, out_ref)


def owner_slots(table_ref, vids, depth, for_send):
    base = vids if for_send else 0
    for vid in range(vids):
        for level in range(depth):
            swapped = (level % 2) * (depth // 2) + level // 2
            yield vid, level, (table_ref[base + vid], swapped ^ table_ref[2 * vids + 1])


def store_share(value, keep_ref, send_ref, table_ref, vids, chunk=0):
    depth = keep_ref.shape[1]
    share, width = keep_ref.shape[-2:]
    low_core = table_ref[2 * vids] == 0
    slots = zip(owner_slots(table_ref, vids, depth, False), owner_slots(table_ref, vids, depth, True))
    for (vid, level, kept), (_, _, sent) in slots:
        at = ((vid * depth + level) * 2) * share
        for part in range(value.shape[1] // width):
            cols = slice(part * width, (part + 1) * width)
            first = value[at : at + share, cols].astype(BF16)
            second = value[at + share : at + 2 * share, cols].astype(BF16)
            keep_ref[kept + (chunk + part,)] = jnp.where(low_core, first, second)
            send_ref[sent + (chunk + part,)] = jnp.where(low_core, second, first)


def store_rows(value, keep_ref, send_ref, table_ref, vids):
    _, depth, count, share, width = keep_ref.shape
    across = value.shape[1] // width
    low_core = table_ref[2 * vids] == 0
    for level in range(depth):
        place = ((level % 2) * (depth // 2) + level // 2) ^ table_ref[2 * vids + 1]
        for part in range(count):
            cols = slice(part % across * width, (part % across + 1) * width)
            at = (2 * level * (count // across) + part // across) * share
            first = value[at : at + share, cols].astype(BF16)
            at += count // across * share
            second = value[at : at + share, cols].astype(BF16)
            keep_ref[0, place, part] = jnp.where(low_core, first, second)
            send_ref[0, place, part] = jnp.where(low_core, second, first)


def feed_backward_kernel(
    packed, vids, table_ref, live_ref,
    cot_ref, resid_ref, hidden_low_ref, act_ref, slope_ref, mixed_ref, gain_ref, fc_w_ref, proj_w_ref, out_w_ref,
    *refs,
):
    resid_grad_ref, mixed_grad_ref, vec_ref, fc_b_ref = refs[:4]
    grads = refs[4:-7]
    grad_s, pre_grad_s, hidden_grad_s, low_s, resid_s, mixed_s, rows_s = refs[-7:]
    step = pl.program_id(0)
    last = pl.num_programs(0) - 1
    frames, _, feature = resid_grad_ref.shape

    def finish(grad):
        if packed:
            store_share(grad, grads[2], grads[3], table_ref, vids)
        else:
            grads[1][0] = grad

    @pl.when(step == 0)
    def _():
        hidden_grad_s[...] = jnp.zeros_like(hidden_grad_s)
        spread_rows(cot_ref, rows_s)
        row = lax.broadcasted_iota(jnp.int32, (KEY_ROWS, 1), 0)
        total = None
        for frame in range(frames):
            keep = (row < PATCHES) & (live_ref[frame] > 0)
            grad = jnp.where(keep, take_frame(rows_s, frame, KEY_ROWS, frames), 0.0)
            grad_s[frame * KEY_ROWS : (frame + 1) * KEY_ROWS, :] = grad.astype(BF16)
            total = column_sum(grad) if total is None else total + column_sum(grad)
        spare = vec_ref.shape[0] - 1
        vec_ref[:spare, :] = jnp.zeros((spare, feature), F32)
        vec_ref[spare:, :] = total

    @pl.when(step < frames)
    def _():
        at = pl.multiple_of(step * KEY_ROWS, 16)
        resid_s[pl.ds(at, KEY_ROWS), :] = resid_ref[0, :KEY_ROWS, :]
        mixed_s[pl.ds(at, KEY_ROWS), :] = mixed_ref[0, :KEY_ROWS, :]

    @pl.when(step < last)
    def _():
        grad_act = dot_nt(grad_s[...], proj_w_ref[...])
        proj_grad = dot_tn(act_ref[...], grad_s[...])
        pre_grad = (grad_act * slope_ref[...].astype(F32)).astype(BF16)
        pre_grad_s[...] = pre_grad
        fc_b_ref[pl.ds(step, 1), :] = column_sum(pre_grad.astype(F32))
        if packed:
            store_rows(proj_grad, grads[0], grads[1], table_ref, vids)
        else:
            grads[0][...] = proj_grad
        hidden_grad_s[...] += dot_nt(pre_grad, fc_w_ref[...])
        finish(dot_tn(hidden_low_ref[...], pre_grad_s[...]))

    @pl.when(step == last)
    def _():
        gain = gain_ref[...]
        gain_grad = jnp.zeros((1, feature), F32)
        shift_grad = jnp.zeros((1, feature), F32)
        bias_grad = jnp.zeros((1, feature), F32)
        for frame in range(frames):
            rows = slice(frame * KEY_ROWS, (frame + 1) * KEY_ROWS)
            normed, inverse = norm_parts(resid_s[rows, :])
            hidden_grad = hidden_grad_s[rows, :]
            gain_grad += column_sum(hidden_grad * normed)
            shift_grad += column_sum(hidden_grad)
            resid_grad = grad_s[rows, :].astype(F32) + norm_back(hidden_grad, normed, inverse, gain)
            resid_grad_ref[frame] = resid_grad
            low = resid_grad.astype(BF16)
            low_s[rows, :] = low
            bias_grad += column_sum(low.astype(F32))
        spare = vec_ref.shape[0] - 4
        vec_ref[spare : spare + 1, :] = gain_grad
        vec_ref[spare + 1 : spare + 2, :] = shift_grad
        vec_ref[spare + 2 : spare + 3, :] = bias_grad
        mixed_grad = dot_nt(low_s[...], out_w_ref[...]).astype(BF16)
        for frame in range(frames):
            mixed_grad_ref[frame] = mixed_grad[frame * KEY_ROWS : (frame + 1) * KEY_ROWS]
        finish(dot_tn(mixed_s[...], low_s[...]))


def pair_backward(query, keys, values, grad, lse_of, allowed, masks, scale):
    grad_q = grad_k = grad_v = None
    for side, mask in enumerate(masks):
        query_one = query * (mask * scale)
        grad_one = grad * mask
        score = dot_nt(keys, query_one)
        weight = jnp.where(allowed, jnp.exp(score - lse_of(side)), 0.0)
        grad_weight = dot_nt(values, grad_one)
        inner = jnp.sum(weight * grad_weight, axis=0, keepdims=True)
        grad_score = (weight * (grad_weight - inner)).astype(BF16)
        one_v = dot_nn(weight.astype(BF16), grad_one)
        one_k = dot_nn(grad_score, query_one)
        one_q = dot_tn(grad_score, keys * (mask * scale))
        grad_q = one_q if grad_q is None else grad_q + one_q
        grad_k = one_k if grad_k is None else grad_k + one_k
        grad_v = one_v if grad_v is None else grad_v + one_v
    return grad_q.astype(BF16), grad_k.astype(BF16), grad_v.astype(BF16)


def attention_backward_kernel(
    packed, vids, first, count, final, table_ref,
    tokens_ref, query_ref, keyval_ref, lse_ref, mixed_grad_ref, resid_grad_ref, gain_ref, in_w_ref, earlier_ref, *refs,
):
    if final:
        hidden_ref, fc_b_ref, *others = refs[: -7 if packed else -6]
        refs = refs[len(others) + 2 :]
    frame_grad_ref, joined_ref, small_ref = refs[:3]
    rows_s = refs[-1] if not final else refs[-2]
    step = pl.program_id(0)
    feature = tokens_ref.shape[2]

    @pl.when(step < count)
    def _():
        gain = gain_ref[...]
        key_row = lax.broadcasted_iota(jnp.int32, (KEY_ROWS, 1), 0)
        allowed = key_row <= PATCHES
        masks = lane_masks()
        scale = jnp.asarray(HEAD**-0.5, BF16)
        for pair in range(HEADS // 2):
            cols = slice(pair * PAIR, (pair + 1) * PAIR)
            value_cols = slice(feature + pair * PAIR, feature + (pair + 1) * PAIR)

            def lse_of(side, head=2 * pair):
                return lse_ref[0, head + side : head + side + 1, :KEY_ROWS]

            grads = pair_backward(
                query_ref[0, :KEY_ROWS, cols], keyval_ref[0, :, cols], keyval_ref[0, :, value_cols],
                mixed_grad_ref[0, :, cols], lse_of, allowed, masks, scale,
            )
            for block, value in enumerate(grads):
                joined_ref[0, :, block * feature + pair * PAIR : block * feature + (pair + 1) * PAIR] = value
        joined = joined_ref[0]
        hidden_grad = dot_nt(joined, in_w_ref[...])
        normed, inverse = norm_parts(tokens_ref[0])
        tokens_grad = norm_back(hidden_grad, normed, inverse, gain)
        frame_grad = jnp.where(key_row < PATCHES, resid_grad_ref[0] + tokens_grad, 0.0)
        put_frame(rows_s, step, frame_grad, count)

        @pl.when(step == 0)
        def _():
            small_ref[...] = earlier_ref[...]

        sums = small_ref.shape[0] - 8
        small_ref[pl.ds(first + step, 1), :] = tokens_grad[PATCHES : PATCHES + 1]
        small_ref[sums : sums + 1, :] += column_sum(joined[:, :feature].astype(F32))
        small_ref[sums + 1 : sums + 2, :] += column_sum(joined[:, 2 * feature :].astype(F32))
        small_ref[sums + 2 : sums + 3, :] += column_sum(hidden_grad * normed)
        small_ref[sums + 3 : sums + 4, :] += column_sum(hidden_grad)
        if final:
            joined_s = refs[-1]
            joined_s[pl.ds(pl.multiple_of(step * KEY_ROWS, 16), KEY_ROWS), :] = joined

        @pl.when(step == count - 1)
        def _():
            live = count * KEY_ROWS
            rows_s[:, live:, :] = jnp.zeros((rows_s.shape[0], rows_s.shape[1] - live, LANES), F32)
            sources, size, _ = frame_grad_ref.shape
            rows = rows_s.shape[1] // sources
            for source in range(sources):
                for col in range(rows_s.shape[0]):
                    frame_grad_ref[source, :rows, col * LANES : (col + 1) * LANES] = rows_s[
                        col, source * rows : (source + 1) * rows, :
                    ].astype(BF16)
            if final:
                extra = jnp.concatenate([small_ref[:sums, :], jnp.zeros((size - rows - sums, feature), F32)])
                for source in range(sources):
                    frame_grad_ref[source, rows:, :] = extra.astype(BF16)

    if not final:
        return
    outs = refs[3:-2]
    joined_s = refs[-1]
    across = feature // LANES

    for block in range(3):

        @pl.when(step == count + block)
        def _(block=block):
            cols = slice(block * feature, (block + 1) * feature)
            split = len(others) * count * KEY_ROWS
            grad = dot_tn(hidden_ref[split:, :], joined_s[:, cols])
            for part, other in enumerate(others):
                size = count * KEY_ROWS
                grad = grad + dot_tn(hidden_ref[part * size : (part + 1) * size, :], other[:, cols])
            if packed:
                store_share(grad, outs[0], outs[1], table_ref, vids, block * across)
            else:
                outs[0][block] = grad

    @pl.when(step == count + 3)
    def _():
        sums = jnp.concatenate([small_ref[small_ref.shape[0] - 8 :, :], fc_b_ref[...]])
        row = lax.broadcasted_iota(jnp.int32, (sums.shape[0], LANES), 0)
        col = lax.broadcasted_iota(jnp.int32, (sums.shape[0], LANES), 1)
        turned = lax.dot_general(
            sums, jnp.where(row == col, 1.0, 0.0), (((0,), (0,)), ((), ())),
            precision=lax.Precision.HIGHEST, preferred_element_type=F32,
        )
        if packed:
            store_share(turned, outs[0], outs[1], table_ref, vids, 3 * across)
        else:
            outs[0][3] = jnp.concatenate([turned] * across, axis=1)


def sum_kernel(groups, wholes, *refs):
    out_ref = refs[-1]
    at, first = 0, wholes
    for count in groups:
        rows = refs[first].shape[1]
        value = refs[first][...].astype(F32)
        for ref in refs[first + 1 : first + count]:
            value = value + ref[...].astype(F32)
        for ref in refs[:wholes]:
            value = value + ref[:, at : at + rows, :].astype(F32)
        out_ref[:, at : at + rows, :] = value.astype(out_ref.dtype)
        at += rows
        first += count


def final_sum_kernel(terms, share, columns, *refs):
    in_refs, out_refs = refs[:terms], refs[terms:]
    block = 0

    def next_block():
        rows = slice(block * share, (block + 1) * share)
        value = in_refs[0][rows, :].astype(F32)
        for ref in in_refs[1:]:
            value = value + ref[rows, :].astype(F32)
        return value

    for out_ref, shape in zip(out_refs, columns):
        if shape is None:
            turned = jnp.transpose(next_block())
            block += 1
            out_ref[...] = turned[:2]
            for row, vec_ref in enumerate(out_refs[-6:]):
                vec_ref[...] = turned[2 + row]
            out_refs[-7][...] = turned[8 : 8 + out_refs[-7].shape[0]]
            return
        for row in range(shape[0]):
            for col in range(shape[1]):
                out_ref[row * share : (row + 1) * share, col * LANES : (col + 1) * LANES] = next_block()
                block += 1


def resident(shape):
    return pl.BlockSpec(shape, lambda *_: (0,) * len(shape), pipeline_mode=pl.Buffered(1))


def params(mebibytes):
    return pltpu.CompilerParams(vmem_limit_bytes=60 * MIB)


def cost(flops, nbytes, transcendentals=0):
    return pl.CostEstimate(
        flops=10 * int(flops), bytes_accessed=10 * int(nbytes), transcendentals=10 * int(transcendentals)
    )


def with_ready(kernel, at, count):
    def body(*refs):
        kernel(*refs[:at], *refs[at + count :])

    return body


def ready_specs(count):
    return [pl.BlockSpec(memory_space=pl.ANY)] * count


def after(value, ready):
    return lax.optimization_barrier((value, ready))[0]


def add(left, right):
    return (left.astype(F32) + right.astype(F32)).astype(BF16)


def shards(
    vids, toks,
    frames, messages, frame_counts, cotangent,
    msg_gain, msg_shift, msg_in_w, msg_in_b, msg_out_w, msg_out_b,
    ln1_gain, ln1_shift, attn_in_w, attn_in_b, attn_out_w, attn_out_b,
    ln2_gain, ln2_shift, fc_w, fc_b, proj_w, proj_b,
):
    video_count, frame_slots, slots, feature = frames.shape
    devices = vids * toks
    group_frames = video_count * frame_slots
    owned = group_frames // toks
    owners = toks // video_count
    slot_count = slots * toks
    hidden_units = fc_w.shape[1]
    chunks = hidden_units // feature
    share = feature // devices
    vid = lax.axis_index("vid")
    tok = lax.axis_index("tok")
    core = tok % 2
    both = ("vid", "tok")
    depth = toks // 2
    packed = vids == 4 and toks == 8 and share % 8 == 0

    vectors = [msg_gain, msg_shift, msg_out_b, ln1_gain, ln1_shift, attn_out_b, ln2_gain, ln2_shift, proj_b]
    stacked = jnp.stack(vectors + [fc_b[at : at + feature] for at in range(0, hidden_units, feature)])
    stacked = stacked.astype(F32).reshape(-1, 1, feature)

    def row(index):
        return pl.BlockSpec((None, 1, feature), lambda *_: (index, 0, 0))

    def exchange(blocks):
        return lax.all_to_all(blocks, "tok", split_axis=0, concat_axis=0, tiled=True)

    slot_shape = (video_count, slots, frame_slots, feature)
    slot_scratch = pltpu.VMEM((feature // LANES, group_frames * slots, LANES), F32)

    def by_owner(tokens):
        return pl.pallas_call(
            to_owners_kernel,
            grid=(1,),
            in_specs=[resident(slot_shape)],
            out_specs=resident((toks, slots * owned, feature)),
            out_shape=jax.ShapeDtypeStruct((toks, slots * owned, feature), BF16),
            scratch_shapes=[slot_scratch, slot_scratch],
            compiler_params=params(40),
            cost_estimate=cost(0, slots * feature),
            name="to_owners",
        )(tokens.transpose(0, 2, 1, 3))

    def from_owners(blocks, ready=()):
        by_slot, done = pl.pallas_call(
            with_ready(partial(from_owners_kernel, len(blocks)), len(blocks), len(ready)),
            grid=(1,),
            in_specs=[resident(block.shape) for block in blocks] + ready_specs(len(ready)),
            out_specs=[resident(slot_shape), resident((8, LANES))],
            out_shape=[jax.ShapeDtypeStruct(slot_shape, BF16), jax.ShapeDtypeStruct((8, LANES), F32)],
            scratch_shapes=[
                pltpu.VMEM((feature // LANES, toks * max(block.shape[1] for block in blocks), LANES), F32),
                slot_scratch,
            ],
            compiler_params=params(40),
            cost_estimate=cost(0, slots * feature),
            name="from_owners",
        )(*blocks, *ready)
        return by_slot.transpose(0, 2, 1, 3), done

    def swap(rows, axis, size, bit):
        return lax.ppermute(rows, axis, [(i, i ^ bit) for i in range(size)])

    def over_levels(rows):
        return [rows] + [swap(rows, "tok", toks, 2 * step) for step in range(1, depth)]

    def in_order(rows):
        rows = rows.reshape((2, depth) + rows.shape[2:]).swapaxes(0, 1)
        rows = rows.reshape((toks,) + rows.shape[2:])
        bit = 1
        while bit < toks:
            pairs = rows.reshape((toks // (2 * bit), 2, bit) + rows.shape[1:])
            turned = jnp.where((tok // bit) % 2 == 1, pairs[:, ::-1], pairs)
            rows = turned.reshape(rows.shape)
            bit *= 2
        return rows

    group_index = jnp.arange(group_frames, dtype=jnp.int32)
    live_group = group_index % frame_slots < jnp.repeat(frame_counts, frame_slots)
    piece = messages.shape[-1]
    width = (piece + 1 + 127) // 128 * 128
    payload = jnp.concatenate(
        [
            messages.reshape(group_frames, piece),
            live_group.astype(BF16)[:, None],
            jnp.zeros((group_frames, width - piece - 1), BF16),
        ],
        axis=1,
    )
    x_blocks = by_owner(frames)
    levels = over_levels(after(payload, x_blocks))
    x_blocks = exchange(after(x_blocks, levels))
    gathered = jnp.stack(levels)
    gathered = in_order(jnp.stack([gathered, swap(gathered, "tok", toks, 1)]))[None]
    bit = 1
    while bit < vids:
        gathered = jnp.concatenate([gathered, swap(gathered, "vid", vids, bit)])
        bit *= 2
    message_rows = vids * group_frames
    message_all = gathered[..., :piece].transpose(0, 2, 1, 3).reshape(message_rows, feature)
    live_all = gathered[:, 0, :, piece].reshape(message_rows) > 0.5
    row_video = jnp.arange(message_rows, dtype=jnp.int32) // frame_slots
    allowed = ((row_video[:, None] == row_video[None, :]) & live_all[None, :]).astype(F32)

    joined, mixed, message_new = pl.pallas_call(
        message_forward_kernel,
        grid=(1,),
        in_specs=[
            resident((message_rows, feature)),
            resident((message_rows, message_rows)),
            row(0),
            row(1),
            resident((feature, 3 * feature)),
            resident((2, feature)),
            resident((feature, feature)),
            row(2),
        ],
        out_specs=[
            resident((message_rows, 3 * feature)),
            resident((message_rows, feature)),
            resident((message_rows, feature)),
        ],
        out_shape=(
            jax.ShapeDtypeStruct((message_rows, 3 * feature), BF16),
            jax.ShapeDtypeStruct((message_rows, feature), BF16),
            jax.ShapeDtypeStruct((message_rows, feature), F32),
        ),
        compiler_params=params(40),
        cost_estimate=cost(8 * message_rows * feature * feature, 8 * feature * feature),
        name="message_forward",
    )(
        message_all, allowed, stacked, stacked, msg_in_w, msg_in_b, msg_out_w, stacked,
    )
    cot_blocks = exchange(after(by_owner(cotangent), (x_blocks, message_new)))
    own_new = lax.dynamic_slice(message_new, (tok * owned, 0), (owned, feature)).reshape(owned, 1, feature)

    rows = owned * slot_count
    live_rows = owned * KEY_ROWS
    blocks_shape = (toks, slots * owned, feature)
    columns_shape = (feature // LANES, rows, LANES)

    def by_frame(*tail):
        return pl.BlockSpec((1,) + tail, lambda f, *_: (f,) + (0,) * len(tail))

    query, keyval, attended, lse, resid, tokens, hidden_kv = pl.pallas_call(
        partial(attention_forward_kernel, owned),
        grid=(owned,),
        in_specs=[
            resident(blocks_shape),
            by_frame(1, feature),
            row(3),
            row(4),
            resident((feature, 3 * feature)),
            resident((2, feature)),
            resident((feature, feature)),
            row(5),
        ],
        out_specs=[
            by_frame(slot_count, feature),
            by_frame(KEY_ROWS, 2 * feature),
            by_frame(slot_count, feature),
            by_frame(HEADS, slot_count),
            by_frame(slot_count, feature),
            by_frame(KEY_ROWS, feature),
            by_frame(KEY_ROWS, feature),
        ],
        out_shape=(
            jax.ShapeDtypeStruct((owned, slot_count, feature), BF16),
            jax.ShapeDtypeStruct((owned, KEY_ROWS, 2 * feature), BF16),
            jax.ShapeDtypeStruct((owned, slot_count, feature), BF16),
            jax.ShapeDtypeStruct((owned, HEADS, slot_count), F32),
            jax.ShapeDtypeStruct((owned, slot_count, feature), F32),
            jax.ShapeDtypeStruct((owned, KEY_ROWS, feature), F32),
            jax.ShapeDtypeStruct((owned, KEY_ROWS, feature), BF16),
        ),
        scratch_shapes=[pltpu.VMEM(columns_shape, F32)],
        compiler_params=params(40),
        cost_estimate=cost(10 * rows * feature * feature, 12 * rows * feature, rows * slot_count * HEADS),
        name="attention_forward",
    )(
        x_blocks, own_new, stacked, stacked, attn_in_w, attn_in_b, attn_out_w, stacked,
    )

    out_blocks, hidden_low, act, slope = pl.pallas_call(
        feed_forward_kernel,
        grid=(chunks,),
        in_specs=[
            resident((owned, slot_count, feature)),
            row(6),
            row(7),
            pl.BlockSpec((feature, feature), lambda j: (0, j)),
            pl.BlockSpec((None, 1, feature), lambda j: (9 + j, 0, 0)),
            pl.BlockSpec((feature, feature), lambda j: (j, 0)),
            row(8),
        ],
        out_specs=[
            resident(blocks_shape),
            resident((live_rows, feature)),
            pl.BlockSpec((live_rows, feature), lambda j: (0, j)),
            pl.BlockSpec((live_rows, feature), lambda j: (0, j)),
        ],
        out_shape=(
            jax.ShapeDtypeStruct(blocks_shape, BF16),
            jax.ShapeDtypeStruct((live_rows, feature), BF16),
            jax.ShapeDtypeStruct((live_rows, hidden_units), BF16),
            jax.ShapeDtypeStruct((live_rows, hidden_units), BF16),
        ),
        scratch_shapes=[
            pltpu.VMEM((rows, feature), BF16),
            pltpu.VMEM((rows, feature), F32),
            pltpu.VMEM(columns_shape, F32),
        ],
        compiler_params=params(48),
        cost_estimate=cost(4 * rows * feature * hidden_units, 12 * feature * hidden_units, rows * hidden_units),
        name="feed_forward",
    )(
        resid, stacked, stacked, fc_w, stacked, proj_w, stacked,
    )
    output_blocks = exchange(after(out_blocks, cot_blocks))

    own_index = tok * owned + jnp.arange(owned, dtype=jnp.int32)
    own_count = jnp.sum(
        jnp.where(
            (own_index // frame_slots)[:, None] == jnp.arange(video_count, dtype=jnp.int32)[None, :],
            frame_counts[None, :],
            0,
        ),
        axis=1,
    )
    own_live = (own_index % frame_slots < own_count).astype(jnp.int32)

    dest = jnp.arange(vids, dtype=jnp.int32)

    def slot_table(for_core):
        low_bit, high_bit = dest % 2 ^ vid % 2, dest // 2 ^ vid // 2
        return jnp.where(for_core == 0, 2 * low_bit + high_bit, 2 * high_bit + low_bit)

    level = tok // 2
    swapped = (level % 2) * (depth // 2) + level // 2
    table = jnp.concatenate([slot_table(core), slot_table(1 - core), core[None], swapped[None]]).astype(jnp.int32)

    def cross(bit_of_core):
        return [
            (v * toks + t, (v ^ bit_of_core[t % 2]) * toks + t) for v in range(vids) for t in range(toks)
        ]

    def send_over(stage, value):
        if stage == 0:
            return swap(value, "tok", toks, 1)
        if stage == 1:
            return lax.ppermute(value, both, cross((1, 2)))
        return lax.ppermute(value, both, cross((2, 1)))

    def sum_slots(parts, wholes, first, count, ready, dtype=BF16):
        batch = next(size for size in (4, 2, 1) if count % size == 0 and (size == 1 or count > size or len(parts) > 1))
        batch = min(batch, 2) if len(parts) > 1 else batch
        operands = list(wholes) + [term for terms in parts for term in terms]
        rows = sum(terms[0].shape[1] for terms in parts)
        return pl.pallas_call(
            with_ready(
                partial(sum_kernel, [len(terms) for terms in parts], len(wholes)), len(operands), len(ready)
            ),
            grid=(count // batch,),
            in_specs=[
                pl.BlockSpec((batch,) + term.shape[1:], lambda i: (first // batch + i, 0, 0)) for term in operands
            ]
            + ready_specs(len(ready)),
            out_specs=pl.BlockSpec((batch, rows, LANES), lambda i: (i, 0, 0)),
            out_shape=jax.ShapeDtypeStruct((count, rows, LANES), dtype),
            compiler_params=params(40),
            cost_estimate=cost(0, rows * LANES),
            name="sum_slots",
        )(*operands, *ready)

    class Sum:
        def __init__(self, *grads):
            self.parts = [[keep.reshape(keep.shape[0] * keep.shape[1], -1, LANES)] for keep, _ in grads]
            self.got = [send_over(0, send.reshape(vids * depth, -1, LANES)) for _, send in grads]
            self.slots = vids * depth
            self.stage = 0

        def step(self, *ready):
            self.stage += 1
            if self.stage == 1:
                self.parts = [terms + [got] for terms, got in zip(self.parts, self.got)]
                self.whole = []
            else:
                self.whole = self.whole + self.got
            if self.stage == 3:
                value = sum_slots(self.parts, self.whole, 0, depth, ready)
                self.whole, self.parts = [value[0]], []
                steps = [(at % 2) * (depth // 2) + at // 2 for at in range(depth)]
                self.got = [swap(value[at], "tok", toks, 2 * steps[at]) for at in range(1, depth)]
                return value
            self.slots //= 2
            send = sum_slots(self.parts, self.whole, self.slots, self.slots, ready)
            self.got = [send_over(self.stage, send)]
            return send

        def end(self, shapes, *ready):
            operands = self.whole + self.got
            out_shape = []
            for shape in shapes:
                if shape is None:
                    sizes = [(2, share), (chunks, share)] + [(share,)] * 6
                else:
                    sizes = [(shape[0] * share, shape[1] * LANES)]
                out_shape += [jax.ShapeDtypeStruct(size, F32) for size in sizes]
            return pl.pallas_call(
                with_ready(partial(final_sum_kernel, len(operands), share, shapes), len(operands), len(ready)),
                grid=(1,),
                in_specs=[resident(term.shape) for term in operands] + ready_specs(len(ready)),
                out_specs=[resident(out.shape) for out in out_shape],
                out_shape=out_shape,
                compiler_params=params(40),
                cost_estimate=cost(0, feature * LANES),
                name="final_sum",
            )(*operands, *ready)

    half = (vids, depth)
    across = feature // LANES
    columns = feature // across

    def packed_out(*tail):
        return [jax.ShapeDtypeStruct(half + tail, BF16)] * 2

    if packed:
        proj_specs = [
            pl.BlockSpec(
                (1, depth, across * chunks, share, columns),
                lambda j, table, live, base=base: (table[base + jnp.minimum(j, chunks - 1)], 0, 0, 0, 0),
            )
            for base in (0, vids)
        ]
        proj_shapes = packed_out(across * chunks, share, columns)
        fc_specs = [pl.BlockSpec(half + (across, share, columns), lambda j, *_: (0, 0, j, 0, 0)) for _ in range(2)]
        fc_shapes = packed_out(across * (chunks + 1), share, columns)
    else:
        proj_specs = [pl.BlockSpec((feature, feature), lambda j, *_: (jnp.minimum(j, chunks - 1), 0))]
        proj_shapes = [jax.ShapeDtypeStruct((hidden_units, feature), F32)]
        fc_specs = [pl.BlockSpec((1, feature, feature), lambda j, *_: (j, 0, 0))]
        fc_shapes = [jax.ShapeDtypeStruct((chunks + 1, feature, feature), F32)]
    small_rows = owned + 8

    def chunk(index):
        return jnp.minimum(index, chunks - 1)

    def frame_of(index):
        return jnp.minimum(index, owned - 1)

    resid_grad, mixed_grad, small, fc_b_part, *ff_grads = pl.pallas_call(
        partial(feed_backward_kernel, packed, vids),
        grid_spec=pltpu.PrefetchScalarGridSpec(
            num_scalar_prefetch=2,
            grid=(max(chunks, owned) + 1,),
            in_specs=[
                resident(blocks_shape),
                pl.BlockSpec((1, slot_count, feature), lambda j, *_: (frame_of(j), 0, 0)),
                resident((live_rows, feature)),
                pl.BlockSpec((live_rows, feature), lambda j, *_: (0, chunk(j))),
                pl.BlockSpec((live_rows, feature), lambda j, *_: (0, chunk(j))),
                pl.BlockSpec((1, slot_count, feature), lambda j, *_: (frame_of(j), 0, 0)),
                row(6),
                pl.BlockSpec((feature, feature), lambda j, *_: (0, chunk(j))),
                pl.BlockSpec((feature, feature), lambda j, *_: (chunk(j), 0)),
                resident((feature, feature)),
            ],
            out_specs=[
                resident((owned, KEY_ROWS, feature)),
                resident((owned, KEY_ROWS, feature)),
                resident((small_rows, feature)),
                resident((chunks, feature)),
            ]
            + proj_specs
            + fc_specs,
            scratch_shapes=[
                pltpu.VMEM((live_rows, feature), BF16),
                pltpu.VMEM((live_rows, feature), BF16),
                pltpu.VMEM((live_rows, feature), F32),
                pltpu.VMEM((live_rows, feature), BF16),
                pltpu.VMEM((live_rows, feature), F32),
                pltpu.VMEM((live_rows, feature), BF16),
                pltpu.VMEM(columns_shape, F32),
            ],
        ),
        out_shape=[
            jax.ShapeDtypeStruct((owned, KEY_ROWS, feature), F32),
            jax.ShapeDtypeStruct((owned, KEY_ROWS, feature), BF16),
            jax.ShapeDtypeStruct((small_rows, feature), F32),
            jax.ShapeDtypeStruct((chunks, feature), F32),
        ]
        + proj_shapes
        + fc_shapes,
        compiler_params=params(48),
        cost_estimate=cost(8 * rows * feature * hidden_units, 12 * feature * hidden_units),
        name="feed_backward",
    )(
        table, own_live, cot_blocks, resid, hidden_low, act, slope, attended, stacked, fc_w, proj_w, attn_out_w,
    )
    proj_grads, fc_grads = ff_grads[: len(proj_shapes)], ff_grads[len(proj_shapes) :]

    parts = 2 if owned % 2 == 0 else 1
    part_frames = owned // parts
    part_blocks = (toks, slots * part_frames, feature)

    if packed:
        attn_specs = [resident(half + (across * 3 + 1, share, columns))] * 2
        attn_shapes = packed_out(across * 3 + 1, share, columns)
    else:
        attn_specs = [resident((4, feature, feature))]
        attn_shapes = [jax.ShapeDtypeStruct((4, feature, feature), F32)]
    part_rows = part_frames * KEY_ROWS

    def attention_backward(part, small, others, ready):
        first = part * part_frames
        final = part == parts - 1

        def by_part(*tail):
            return pl.BlockSpec(
                (1,) + tail, lambda f, *_: (first + jnp.minimum(f, part_frames - 1),) + (0,) * len(tail)
            )

        extra, extra_specs, scratch = [], [], []
        out_blocks = part_blocks
        if final:
            out_blocks = (toks, slots * part_frames + (owned + 7) // 8 * 8, feature)
            extra = [hidden_kv.reshape(live_rows, feature), fc_b_own] + others
            extra_specs = [resident((live_rows, feature)), resident((chunks, feature))]
            extra_specs += [resident((part_rows, 3 * feature))] * len(others)
            scratch = [pltpu.VMEM((part_rows, 3 * feature), BF16)]
        return pl.pallas_call(
            with_ready(
                partial(attention_backward_kernel, packed, vids, first, part_frames, final),
                10 + len(extra),
                len(ready),
            ),
            grid_spec=pltpu.PrefetchScalarGridSpec(
                num_scalar_prefetch=1,
                grid=(part_frames + 4 * final,),
                in_specs=[
                    by_part(KEY_ROWS, feature),
                    by_part(slot_count, feature),
                    by_part(KEY_ROWS, 2 * feature),
                    by_part(HEADS, slot_count),
                    by_part(KEY_ROWS, feature),
                    by_part(KEY_ROWS, feature),
                    row(3),
                    resident((feature, 3 * feature)),
                    resident((small_rows, feature)),
                ]
                + extra_specs
                + ready_specs(len(ready)),
                out_specs=[
                    resident(out_blocks),
                    pl.BlockSpec(
                        (1, KEY_ROWS, 3 * feature), lambda f, *_: (jnp.minimum(f, part_frames - 1), 0, 0)
                    ),
                    resident((small_rows, feature)),
                ]
                + attn_specs * final,
                scratch_shapes=[pltpu.VMEM((feature // LANES, part_frames * slot_count, LANES), F32)] + scratch,
            ),
            out_shape=[
                jax.ShapeDtypeStruct(out_blocks, BF16),
                jax.ShapeDtypeStruct((part_frames, KEY_ROWS, 3 * feature), BF16),
                jax.ShapeDtypeStruct((small_rows, feature), F32),
            ]
            + attn_shapes * final,
            compiler_params=params(40),
            cost_estimate=cost(16 * rows * feature * feature // parts, 20 * rows * feature // parts),
            name="attention_backward",
        )(table, tokens, query, keyval, lse, mixed_grad, resid_grad, stacked, attn_in_w, small, *extra, *ready)

    if packed:
        ff_sum = Sum(fc_grads, proj_grads)
    ready = [output_blocks]
    fc_b_own = fc_b_part.reshape(devices, chunks, share).swapaxes(0, 1).reshape(chunks, feature)
    frame_blocks, joined_grads = [], []
    for part in range(parts):
        blocks, joined_grad, small, *attn_grads = attention_backward(part, small, joined_grads, ready)
        joined_grads.append(joined_grad.reshape(part_rows, 3 * feature))
        if packed and part == 0:
            ready = [ff_sum.step(small)]
            blocks = after(blocks, ready)
        frame_blocks.append(exchange(blocks))
    ready = small
    if packed:
        attn_sum = Sum(after(attn_grads, frame_blocks[: parts - 1]))
        ready = attn_sum.step(small)
        ready = ff_sum.step(ready)
    output, ready = from_owners([output_blocks], [ready])
    message_low = pl.pallas_call(
        with_ready(partial(last_rows_kernel, slots * part_frames), 1, 1),
        grid=(1,),
        in_specs=[resident(frame_blocks[-1].shape)] + ready_specs(1),
        out_specs=resident((toks, owned, feature)),
        out_shape=jax.ShapeDtypeStruct((toks, owned, feature), BF16),
        cost_estimate=cost(0, toks * feature),
        name="last_rows",
    )(frame_blocks[-1], ready)
    if packed:
        ready = ff_sum.step(message_low)
        ready = attn_sum.step(ready)
    message_low = message_low.reshape(group_frames, feature)
    bit = 1
    while bit < vids:
        message_low = message_low if bit == 1 else after(message_low, ready)
        message_low = jnp.concatenate([message_low, swap(message_low, "vid", vids, bit)])
        bit *= 2
    if packed:
        ready = attn_sum.step(message_low)
    frames_grad, done = from_owners(frame_blocks, [ready])

    place = (vid * toks + tok) * share
    message_grad, msg_in_w_grad, msg_out_w_grad, *msg_vec = pl.pallas_call(
        with_ready(message_backward_kernel, 10, 1),
        grid_spec=pltpu.PrefetchScalarGridSpec(
            num_scalar_prefetch=1,
            grid=(1,),
            in_specs=[
                resident((message_rows, feature)),
                resident((message_rows, message_rows)),
                resident((message_rows, feature)),
                resident((message_rows, 3 * feature)),
                resident((message_rows, feature)),
                row(0),
                row(1),
                resident((feature, 3 * feature)),
                resident((feature, feature)),
            ]
            + ready_specs(1),
            out_specs=[
                resident((message_rows, feature)),
                resident((share, 3 * feature)),
                resident((share, feature)),
                resident((share,)),
                resident((share,)),
                resident((2, share)),
                resident((share,)),
            ],
            scratch_shapes=[
                pltpu.VMEM((message_rows, feature), BF16),
                pltpu.VMEM((message_rows, 3 * feature), BF16),
            ],
        ),
        out_shape=(
            jax.ShapeDtypeStruct((message_rows, feature), BF16),
            jax.ShapeDtypeStruct((share, 3 * feature), F32),
            jax.ShapeDtypeStruct((share, feature), F32),
            jax.ShapeDtypeStruct((share,), F32),
            jax.ShapeDtypeStruct((share,), F32),
            jax.ShapeDtypeStruct((2, share), F32),
            jax.ShapeDtypeStruct((share,), F32),
        ),
        compiler_params=params(40),
        cost_estimate=cost(message_rows * feature, message_rows * feature),
        name="message_backward",
    )(
        place[None].astype(jnp.int32), message_all, allowed, message_low, joined, mixed,
        stacked, stacked, msg_in_w, msg_out_w, done,
    )
    messages_grad = lax.dynamic_slice(message_grad, (0, tok * piece), (group_frames, piece)).reshape(
        messages.shape
    )

    def scatter(grad):
        return lax.psum_scatter(grad, both, scatter_dimension=0, tiled=True)

    if packed:
        shapes = [(1, across * chunks), (1, across), (chunks, across)]
        fc_w_grad, attn_out_w_grad, proj_w_grad = ff_sum.end(shapes, done, messages_grad)
        attn_in_w_grad, in_b_grad, fc_b_grad, *vec_grads = attn_sum.end([(1, 3 * across), None])
    else:
        proj_w_grad = scatter(proj_grads[0])
        fc_w_grad = scatter(fc_grads[0][:chunks].transpose(1, 0, 2).reshape(feature, hidden_units))
        attn_out_w_grad = scatter(fc_grads[0][chunks])
        attn_in_w_grad = scatter(attn_grads[0][:3].transpose(1, 0, 2).reshape(feature, 3 * feature))
        own_vec = scatter(attn_grads[0][3, :, :LANES]).T
        in_b_grad, fc_b_grad, vec_grads = own_vec[:2], own_vec[8 : 8 + chunks], list(own_vec[2:8])
    fc_b_grad = fc_b_grad.reshape(-1)

    return (
        output,
        frames_grad,
        messages_grad,
        msg_vec[0],
        msg_vec[1],
        msg_in_w_grad,
        msg_vec[2],
        msg_out_w_grad,
        msg_vec[3],
        vec_grads[0],
        vec_grads[1],
        attn_in_w_grad,
        in_b_grad,
        attn_out_w_grad,
        vec_grads[4],
        vec_grads[2],
        vec_grads[3],
        fc_w_grad,
        fc_b_grad,
        proj_w_grad,
        vec_grads[5],
    )


def solution(mesh):
    tokens = P("vid", None, "tok", None)
    rows, columns, one = P(("vid", "tok"), None), P(None, ("vid", "tok")), P(("vid", "tok"))
    in_specs = (tokens, P("vid", None, "tok"), P("vid"), tokens) + (P(),) * 18
    out_specs = (
        tokens, tokens, P("vid", None, "tok"),
        one, one, rows, columns, rows, one,
        one, one, rows, columns, rows, one,
        one, one, rows, one, rows, one,
    )
    return jax.shard_map(
        partial(shards, mesh.shape["vid"], mesh.shape["tok"]),
        mesh=mesh,
        in_specs=in_specs,
        out_specs=out_specs,
        check_vma=False,
    )
```

```python
from functools import partial

import jax
import jax.numpy as jnp
from jax import lax
from jax.experimental import pallas as pl
from jax.experimental.pallas import tpu as pltpu
from jax.sharding import PartitionSpec as P

HEADS = 12
HEAD = 64
PATCHES = 197
PAIR = 2 * HEAD
EPS = 1e-05
NEG = -1000000000.0
SLOPE = 1.702
F32 = jnp.float32
BF16 = jnp.bfloat16
MIB = 2**20

KEY_ROWS = (PATCHES + 1 + 15) // 16 * 16


def norm_parts(tensor):
    row_mean = jnp.mean(tensor, axis=-1, keepdims=True)
    centred = tensor - row_mean
    spread = jnp.mean(centred * centred, axis=-1, keepdims=True)
    inverse = lax.rsqrt(spread + EPS)
    return centred * inverse, inverse


def norm_back(grad_in, normed, inverse, gain):
    scaled = grad_in * gain
    return inverse * (
        scaled
        - jnp.mean(scaled, axis=-1, keepdims=True)
        - normed * jnp.mean(scaled * normed, axis=-1, keepdims=True)
    )


def dot_nn(left, right):
    return lax.dot_general(left, right, (((1,), (0,)), ((), ())), preferred_element_type=F32)


def dot_nt(left, right):
    return lax.dot_general(left, right, (((1,), (1,)), ((), ())), preferred_element_type=F32)


def dot_tn(left, right):
    return lax.dot_general(left, right, (((0,), (0,)), ((), ())), preferred_element_type=F32)


def lane_masks(dtype=BF16):
    lane = lax.broadcasted_iota(jnp.int32, (1, PAIR), 1)
    first = jnp.where(lane < HEAD, 1.0, 0.0)
    return first.astype(dtype), (1.0 - first).astype(dtype)


def column_sum(rows):
    return jnp.sum(rows, axis=0, keepdims=True)


def message_forward_kernel(
    msg_ref, allow_ref, gain_ref, shift_ref, in_w_ref, in_b_ref, out_w_ref, out_b_ref,
    joined_ref, mixed_ref, new_ref,
):
    feature = msg_ref.shape[1]
    message = msg_ref[...].astype(F32)
    normed, _ = norm_parts(message)
    hidden = (normed * gain_ref[...] + shift_ref[...]).astype(BF16)
    in_b = in_b_ref[...].astype(F32)
    for block in range(3):
        cols = slice(block * feature, (block + 1) * feature)
        part = dot_nn(hidden, in_w_ref[:, cols])
        if block != 1:
            part = part + in_b[block // 2 : block // 2 + 1]
        joined_ref[:, cols] = part.astype(BF16)
    allowed = allow_ref[...] > 0.5
    masks = lane_masks()
    scale = jnp.asarray(HEAD**-0.5, BF16)
    for pair in range(HEADS // 2):
        cols = slice(pair * PAIR, (pair + 1) * PAIR)
        query = joined_ref[:, cols]
        keys = joined_ref[:, feature + pair * PAIR : feature + (pair + 1) * PAIR]
        values = joined_ref[:, 2 * feature + pair * PAIR : 2 * feature + (pair + 1) * PAIR]
        total = None
        for mask in masks:
            score = dot_nt(query * (mask * scale), keys)
            score = jnp.where(allowed, score, NEG)
            weight = jnp.exp(score - jnp.max(score, axis=-1, keepdims=True))
            weight = weight / jnp.sum(weight, axis=-1, keepdims=True)
            part = dot_nn(weight.astype(BF16), values * mask)
            total = part if total is None else total + part
        mixed_ref[:, cols] = total.astype(BF16)
    new_ref[...] = message + (dot_nn(mixed_ref[...], out_w_ref[...]) + out_b_ref[...])


def message_backward_kernel(
    place_ref, msg_ref, allow_ref, low_ref, joined_ref, mixed_ref,
    gain_ref, shift_ref, in_w_ref, out_w_ref,
    grad_ref, in_w_grad_ref, out_w_grad_ref, gain_grad_ref, shift_grad_ref, in_b_grad_ref, out_b_grad_ref,
    mixed_grad_s, joined_grad_s,
):
    feature = msg_ref.shape[1]
    share = in_w_grad_ref.shape[0]
    message = msg_ref[...].astype(F32)
    normed, inverse = norm_parts(message)
    gain = gain_ref[...]
    hidden = (normed * gain + shift_ref[...]).astype(BF16)
    low = low_ref[...]
    low_wide = low.astype(F32)
    mixed_grad_s[...] = dot_nt(low, out_w_ref[...]).astype(BF16)
    allowed = allow_ref[...] > 0.5
    masks = lane_masks()
    scale = jnp.asarray(HEAD**-0.5, BF16)
    for pair in range(HEADS // 2):
        cols = slice(pair * PAIR, (pair + 1) * PAIR)
        key_cols = slice(feature + pair * PAIR, feature + (pair + 1) * PAIR)
        value_cols = slice(2 * feature + pair * PAIR, 2 * feature + (pair + 1) * PAIR)
        query = joined_ref[:, cols]
        keys = joined_ref[:, key_cols]
        values = joined_ref[:, value_cols]
        grad = mixed_grad_s[:, cols]
        grad_q = grad_k = grad_v = None
        for mask in masks:
            query_one = query * (mask * scale)
            grad_one = grad * mask
            score = jnp.where(allowed, dot_nt(query_one, keys), NEG)
            weight = jnp.exp(score - jnp.max(score, axis=-1, keepdims=True))
            weight = weight / jnp.sum(weight, axis=-1, keepdims=True)
            grad_weight = dot_nt(grad_one, values)
            inner = jnp.sum(weight * grad_weight, axis=-1, keepdims=True)
            grad_score = (weight * (grad_weight - inner)).astype(BF16)
            one_q = dot_nn(grad_score, keys * (mask * scale))
            one_k = dot_tn(grad_score, query_one)
            one_v = dot_tn(weight.astype(BF16), grad_one)
            grad_q = one_q if grad_q is None else grad_q + one_q
            grad_k = one_k if grad_k is None else grad_k + one_k
            grad_v = one_v if grad_v is None else grad_v + one_v
        joined_grad_s[:, cols] = grad_q.astype(BF16)
        joined_grad_s[:, key_cols] = grad_k.astype(BF16)
        joined_grad_s[:, value_cols] = grad_v.astype(BF16)
    joined_grad = joined_grad_s[...]
    hidden_grad = dot_nt(joined_grad, in_w_ref[...])
    grad_ref[...] = (low_wide + norm_back(hidden_grad, normed, inverse, gain)).astype(BF16)
    width = (share + 127) // 128 * 128
    row = lax.broadcasted_iota(jnp.int32, (feature, width), 0)
    col = lax.broadcasted_iota(jnp.int32, (feature, width), 1)
    pick = jnp.where((row == col + place_ref[0]) & (col < share), 1.0, 0.0)
    pick_low = pick.astype(BF16)
    own_hidden = dot_nn(hidden, pick_low).astype(BF16)
    own_mixed = dot_nn(mixed_ref[...], pick_low).astype(BF16)
    in_w_grad_ref[...] = dot_tn(own_hidden, joined_grad)[:share]
    out_w_grad_ref[...] = dot_tn(own_mixed, low)[:share]
    sums = jnp.concatenate(
        [
            column_sum(hidden_grad * normed),
            column_sum(hidden_grad),
            column_sum(joined_grad[:, :feature].astype(F32)),
            column_sum(joined_grad[:, 2 * feature :].astype(F32)),
            column_sum(low_wide),
            jnp.zeros((3, feature), F32),
        ],
        axis=0,
    )
    own = lax.dot_general(
        sums, pick, (((1,), (0,)), ((), ())), precision=lax.Precision.HIGHEST, preferred_element_type=F32
    )
    gain_grad_ref[...] = own[0, :share]
    shift_grad_ref[...] = own[1, :share]
    in_b_grad_ref[...] = own[2:4, :share]
    out_b_grad_ref[...] = own[4, :share]


LANES = 128


def spread_rows(block_ref, scratch):
    sources, rows, _ = block_ref.shape
    for source in range(sources):
        for col in range(scratch.shape[0]):
            scratch[col, source * rows : (source + 1) * rows, :] = block_ref[
                source, :, col * LANES : (col + 1) * LANES
            ].astype(F32)


def gather_rows(scratch, block_ref):
    sources, rows, _ = block_ref.shape
    for source in range(sources):
        for col in range(scratch.shape[0]):
            block_ref[source, :, col * LANES : (col + 1) * LANES] = scratch[
                col, source * rows : (source + 1) * rows, :
            ].astype(BF16)


def take_frame(scratch, frame, count, stride):
    return jnp.concatenate(
        [scratch[col, pl.ds(frame, count, stride=stride), :] for col in range(scratch.shape[0])], axis=1
    )


def put_frame(scratch, frame, value, stride):
    for col in range(scratch.shape[0]):
        scratch[col, pl.ds(frame, value.shape[0], stride=stride), :] = value[:, col * LANES : (col + 1) * LANES]


def frame_places(slots, frame_slots, owned):
    for owner in range(frame_slots // owned):
        for frame in range(owned):
            yield owner, frame, owner * owned + frame


def to_owners_kernel(in_ref, out_ref, by_slot_s, by_owner_s):
    videos, slots, frame_slots, _ = in_ref.shape
    owners = out_ref.shape[0] // videos
    owned = frame_slots // owners
    for video in range(videos):
        for slot in range(slots):
            at = (video * slots + slot) * frame_slots
            for col in range(by_slot_s.shape[0]):
                by_slot_s[col, at : at + frame_slots, :] = in_ref[
                    video, slot, :, col * LANES : (col + 1) * LANES
                ].astype(F32)
        for owner, frame, place in frame_places(slots, frame_slots, owned):
            for col in range(by_slot_s.shape[0]):
                rows = by_slot_s[col, pl.ds(video * slots * frame_slots + place, slots, stride=frame_slots), :]
                first = (video * owners + owner) * slots * owned + frame
                by_owner_s[col, pl.ds(first, slots, stride=owned), :] = rows
    gather_rows(by_owner_s, out_ref)


def from_owners_kernel(parts, *refs):
    in_refs, out_ref, done_ref, by_owner_s, by_slot_s = refs[:parts], *refs[parts:]
    done_ref[...] = jnp.zeros_like(done_ref)
    videos, slots, frame_slots, _ = out_ref.shape
    owners = in_refs[0].shape[0] // videos
    owned = frame_slots // owners
    count = owned // parts
    for part, in_ref in enumerate(in_refs):
        spread_rows(in_ref, by_owner_s)
        size = in_ref.shape[1]
        for video in range(videos):
            for owner, frame, _ in frame_places(slots, frame_slots, owned):
                if frame >= count:
                    continue
                place = owner * owned + part * count + frame
                for col in range(by_slot_s.shape[0]):
                    first = (video * owners + owner) * size + frame
                    rows = by_owner_s[col, pl.ds(first, slots, stride=count), :]
                    by_slot_s[col, pl.ds(video * slots * frame_slots + place, slots, stride=frame_slots), :] = rows
    for video in range(videos):
        for slot in range(slots):
            at = (video * slots + slot) * frame_slots
            for col in range(by_slot_s.shape[0]):
                out_ref[video, slot, :, col * LANES : (col + 1) * LANES] = by_slot_s[
                    col, at : at + frame_slots, :
                ].astype(BF16)


def last_rows_kernel(at, in_ref, out_ref):
    for source in range(out_ref.shape[0]):
        out_ref[source] = in_ref[source, at:, :][: out_ref.shape[1]]


def attention_forward_kernel(
    owned, x_ref, new_ref, gain_ref, shift_ref, in_w_ref, in_b_ref, out_w_ref, out_b_ref,
    query_ref, keyval_ref, mixed_ref, lse_ref, resid_ref, tokens_ref, hidden_ref,
    rows_s,
):
    feature = x_ref.shape[2]
    slot_count = query_ref.shape[1]
    frame = pl.program_id(0)

    @pl.when(frame == 0)
    def _():
        spread_rows(x_ref, rows_s)

    gain = gain_ref[...]
    shift = shift_ref[...]
    frame_in = take_frame(rows_s, frame, slot_count, owned)
    normed, _ = norm_parts(frame_in)
    hidden = normed * gain + shift
    msg_normed, _ = norm_parts(new_ref[0])
    msg_hidden = msg_normed * gain + shift
    key_row = lax.broadcasted_iota(jnp.int32, (KEY_ROWS, 1), 0)
    tokens_ref[0] = jnp.where(key_row == PATCHES, new_ref[0], frame_in[:KEY_ROWS])
    hidden_kv = jnp.where(key_row == PATCHES, msg_hidden, hidden[:KEY_ROWS]).astype(BF16)
    hidden_ref[0] = hidden_kv
    hidden = hidden.astype(BF16)
    in_b = in_b_ref[...].astype(F32)
    query_ref[0] = (dot_nn(hidden, in_w_ref[:, :feature]) + in_b[0:1]).astype(BF16)
    keyval_ref[0, :, :feature] = dot_nn(hidden_kv, in_w_ref[:, feature : 2 * feature]).astype(BF16)
    keyval_ref[0, :, feature:] = (
        dot_nn(hidden_kv, in_w_ref[:, 2 * feature :]) + in_b[1:2]
    ).astype(BF16)
    allowed = key_row <= PATCHES
    masks = lane_masks()
    scale = jnp.asarray(HEAD**-0.5, BF16)
    for pair in range(HEADS // 2):
        cols = slice(pair * PAIR, (pair + 1) * PAIR)
        query = query_ref[0, :, cols]
        keys = keyval_ref[0, :, cols]
        values = keyval_ref[0, :, feature + pair * PAIR : feature + (pair + 1) * PAIR]
        total = None
        for side, mask in enumerate(masks):
            score = dot_nt(keys, query * (mask * scale))
            score = jnp.where(allowed, score, NEG)
            peak = jnp.max(score, axis=0, keepdims=True)
            weight = jnp.exp(score - peak)
            norm = jnp.sum(weight, axis=0, keepdims=True)
            lse_ref[0, 2 * pair + side : 2 * pair + side + 1, :] = peak + jnp.log(norm)
            weight = (weight * (1.0 / norm)).astype(BF16)
            part = dot_tn(weight, values * mask)
            total = part if total is None else total + part
        mixed_ref[0, :, cols] = total.astype(BF16)
    resid_ref[0] = take_frame(rows_s, frame, slot_count, owned) + (
        dot_nn(mixed_ref[0], out_w_ref[...]) + out_b_ref[...]
    )


def feed_forward_kernel(
    resid_ref, gain_ref, shift_ref, fc_w_ref, fc_b_ref, proj_w_ref, proj_b_ref,
    out_ref, hidden_low_ref, act_ref, slope_ref,
    hidden_s, out_s, rows_s,
):
    step = pl.program_id(0)
    frames, slot_count, feature = resid_ref.shape

    @pl.when(step == 0)
    def _():
        gain = gain_ref[...]
        shift = shift_ref[...]
        for frame in range(frames):
            normed, _ = norm_parts(resid_ref[frame])
            hidden = (normed * gain + shift).astype(BF16)
            hidden_s[frame * slot_count : (frame + 1) * slot_count, :] = hidden
            hidden_low_ref[frame * KEY_ROWS : (frame + 1) * KEY_ROWS, :] = hidden[:KEY_ROWS]
        out_s[...] = jnp.zeros_like(out_s)

    fc_b = fc_b_ref[...]
    batch = 2 if frames % 2 == 0 else 1
    batches = frames // batch
    size = batch * slot_count

    def pre_of(index):
        return dot_nn(hidden_s[index * size : (index + 1) * size, :], fc_w_ref[...]) + fc_b

    pre = pre_of(0)
    for index in range(batches):
        later = pre_of(index + 1) if index + 1 < batches else None
        gate = 0.5 + 0.5 * jnp.tanh((0.5 * SLOPE) * pre)
        active = pre * gate
        slope = (gate + SLOPE * active * (1.0 - gate)).astype(BF16)
        active = active.astype(BF16)
        for frame in range(batch):
            at = (index * batch + frame) * KEY_ROWS
            rows = slice(frame * slot_count, frame * slot_count + KEY_ROWS)
            slope_ref[at : at + KEY_ROWS, :] = slope[rows]
            act_ref[at : at + KEY_ROWS, :] = active[rows]
        out_s[index * size : (index + 1) * size, :] += dot_nn(active, proj_w_ref[...])
        pre = later

    @pl.when(step == pl.num_programs(0) - 1)
    def _():
        proj_b = proj_b_ref[...]
        for frame in range(frames):
            rows = out_s[frame * slot_count : (frame + 1) * slot_count, :]
            put_frame(rows_s, frame, resid_ref[frame] + (rows + proj_b), frames)
        gather_rows(rows_s, out_ref)


def owner_slots(table_ref, vids, depth, for_send):
    base = vids if for_send else 0
    for vid in range(vids):
        for level in range(depth):
            swapped = (level % 2) * (depth // 2) + level // 2
            yield vid, level, (table_ref[base + vid], swapped ^ table_ref[2 * vids + 1])


def store_share(value, keep_ref, send_ref, table_ref, vids, chunk=0):
    depth = keep_ref.shape[1]
    share, width = keep_ref.shape[-2:]
    low_core = table_ref[2 * vids] == 0
    slots = zip(owner_slots(table_ref, vids, depth, False), owner_slots(table_ref, vids, depth, True))
    for (vid, level, kept), (_, _, sent) in slots:
        at = ((vid * depth + level) * 2) * share
        for part in range(value.shape[1] // width):
            cols = slice(part * width, (part + 1) * width)
            first = value[at : at + share, cols].astype(BF16)
            second = value[at + share : at + 2 * share, cols].astype(BF16)
            keep_ref[kept + (chunk + part,)] = jnp.where(low_core, first, second)
            send_ref[sent + (chunk + part,)] = jnp.where(low_core, second, first)


def store_rows(value, keep_ref, send_ref, table_ref, vids):
    _, depth, count, share, width = keep_ref.shape
    across = value.shape[1] // width
    low_core = table_ref[2 * vids] == 0
    for level in range(depth):
        place = ((level % 2) * (depth // 2) + level // 2) ^ table_ref[2 * vids + 1]
        for part in range(count):
            cols = slice(part % across * width, (part % across + 1) * width)
            at = (2 * level * (count // across) + part // across) * share
            first = value[at : at + share, cols].astype(BF16)
            at += count // across * share
            second = value[at : at + share, cols].astype(BF16)
            keep_ref[0, place, part] = jnp.where(low_core, first, second)
            send_ref[0, place, part] = jnp.where(low_core, second, first)


def feed_backward_kernel(
    packed, vids, table_ref, live_ref,
    cot_ref, resid_ref, hidden_low_ref, act_ref, slope_ref, mixed_ref, gain_ref, fc_w_ref, proj_w_ref, out_w_ref,
    *refs,
):
    resid_grad_ref, mixed_grad_ref, vec_ref, fc_b_ref = refs[:4]
    grads = refs[4:-7]
    grad_s, pre_grad_s, hidden_grad_s, low_s, resid_s, mixed_s, rows_s = refs[-7:]
    step = pl.program_id(0)
    last = pl.num_programs(0) - 1
    frames, _, feature = resid_grad_ref.shape

    def finish(grad):
        if packed:
            store_share(grad, grads[2], grads[3], table_ref, vids)
        else:
            grads[1][0] = grad

    @pl.when(step == 0)
    def _():
        hidden_grad_s[...] = jnp.zeros_like(hidden_grad_s)
        spread_rows(cot_ref, rows_s)
        row = lax.broadcasted_iota(jnp.int32, (KEY_ROWS, 1), 0)
        total = None
        for frame in range(frames):
            keep = (row < PATCHES) & (live_ref[frame] > 0)
            grad = jnp.where(keep, take_frame(rows_s, frame, KEY_ROWS, frames), 0.0)
            grad_s[frame * KEY_ROWS : (frame + 1) * KEY_ROWS, :] = grad.astype(BF16)
            total = column_sum(grad) if total is None else total + column_sum(grad)
        spare = vec_ref.shape[0] - 1
        vec_ref[:spare, :] = jnp.zeros((spare, feature), F32)
        vec_ref[spare:, :] = total

    @pl.when(step < frames)
    def _():
        at = pl.multiple_of(step * KEY_ROWS, 16)
        resid_s[pl.ds(at, KEY_ROWS), :] = resid_ref[0, :KEY_ROWS, :]
        mixed_s[pl.ds(at, KEY_ROWS), :] = mixed_ref[0, :KEY_ROWS, :]

    @pl.when(step < last)
    def _():
        grad_act = dot_nt(grad_s[...], proj_w_ref[...])
        proj_grad = dot_tn(act_ref[...], grad_s[...])
        pre_grad = (grad_act * slope_ref[...].astype(F32)).astype(BF16)
        pre_grad_s[...] = pre_grad
        fc_b_ref[pl.ds(step, 1), :] = column_sum(pre_grad.astype(F32))
        if packed:
            store_rows(proj_grad, grads[0], grads[1], table_ref, vids)
        else:
            grads[0][...] = proj_grad
        hidden_grad_s[...] += dot_nt(pre_grad, fc_w_ref[...])
        finish(dot_tn(hidden_low_ref[...], pre_grad_s[...]))

    @pl.when(step == last)
    def _():
        gain = gain_ref[...]
        gain_grad = jnp.zeros((1, feature), F32)
        shift_grad = jnp.zeros((1, feature), F32)
        bias_grad = jnp.zeros((1, feature), F32)
        for frame in range(frames):
            rows = slice(frame * KEY_ROWS, (frame + 1) * KEY_ROWS)
            normed, inverse = norm_parts(resid_s[rows, :])
            hidden_grad = hidden_grad_s[rows, :]
            gain_grad += column_sum(hidden_grad * normed)
            shift_grad += column_sum(hidden_grad)
            resid_grad = grad_s[rows, :].astype(F32) + norm_back(hidden_grad, normed, inverse, gain)
            resid_grad_ref[frame] = resid_grad
            low = resid_grad.astype(BF16)
            low_s[rows, :] = low
            bias_grad += column_sum(low.astype(F32))
        spare = vec_ref.shape[0] - 4
        vec_ref[spare : spare + 1, :] = gain_grad
        vec_ref[spare + 1 : spare + 2, :] = shift_grad
        vec_ref[spare + 2 : spare + 3, :] = bias_grad
        mixed_grad = dot_nt(low_s[...], out_w_ref[...]).astype(BF16)
        for frame in range(frames):
            mixed_grad_ref[frame] = mixed_grad[frame * KEY_ROWS : (frame + 1) * KEY_ROWS]
        finish(dot_tn(mixed_s[...], low_s[...]))


def pair_backward(query, keys, values, grad, lse_of, allowed, masks, scale):
    grad_q = grad_k = grad_v = None
    for side, mask in enumerate(masks):
        query_one = query * (mask * scale)
        grad_one = grad * mask
        score = dot_nt(keys, query_one)
        weight = jnp.where(allowed, jnp.exp(score - lse_of(side)), 0.0)
        grad_weight = dot_nt(values, grad_one)
        inner = jnp.sum(weight * grad_weight, axis=0, keepdims=True)
        grad_score = (weight * (grad_weight - inner)).astype(BF16)
        one_v = dot_nn(weight.astype(BF16), grad_one)
        one_k = dot_nn(grad_score, query_one)
        one_q = dot_tn(grad_score, keys * (mask * scale))
        grad_q = one_q if grad_q is None else grad_q + one_q
        grad_k = one_k if grad_k is None else grad_k + one_k
        grad_v = one_v if grad_v is None else grad_v + one_v
    return grad_q.astype(BF16), grad_k.astype(BF16), grad_v.astype(BF16)


def attention_backward_kernel(
    packed, vids, first, count, final, table_ref,
    tokens_ref, query_ref, keyval_ref, lse_ref, mixed_grad_ref, resid_grad_ref, gain_ref, in_w_ref, earlier_ref, *refs,
):
    if final:
        hidden_ref, fc_b_ref, *others = refs[: -7 if packed else -6]
        refs = refs[len(others) + 2 :]
    frame_grad_ref, joined_ref, small_ref = refs[:3]
    rows_s = refs[-1] if not final else refs[-2]
    step = pl.program_id(0)
    feature = tokens_ref.shape[2]

    @pl.when(step < count)
    def _():
        gain = gain_ref[...]
        key_row = lax.broadcasted_iota(jnp.int32, (KEY_ROWS, 1), 0)
        allowed = key_row <= PATCHES
        masks = lane_masks()
        scale = jnp.asarray(HEAD**-0.5, BF16)
        for pair in range(HEADS // 2):
            cols = slice(pair * PAIR, (pair + 1) * PAIR)
            value_cols = slice(feature + pair * PAIR, feature + (pair + 1) * PAIR)

            def lse_of(side, head=2 * pair):
                return lse_ref[0, head + side : head + side + 1, :KEY_ROWS]

            grads = pair_backward(
                query_ref[0, :KEY_ROWS, cols], keyval_ref[0, :, cols], keyval_ref[0, :, value_cols],
                mixed_grad_ref[0, :, cols], lse_of, allowed, masks, scale,
            )
            for block, value in enumerate(grads):
                joined_ref[0, :, block * feature + pair * PAIR : block * feature + (pair + 1) * PAIR] = value
        joined = joined_ref[0]
        hidden_grad = dot_nt(joined, in_w_ref[...])
        normed, inverse = norm_parts(tokens_ref[0])
        tokens_grad = norm_back(hidden_grad, normed, inverse, gain)
        frame_grad = jnp.where(key_row < PATCHES, resid_grad_ref[0] + tokens_grad, 0.0)
        put_frame(rows_s, step, frame_grad, count)

        @pl.when(step == 0)
        def _():
            small_ref[...] = earlier_ref[...]

        sums = small_ref.shape[0] - 8
        small_ref[pl.ds(first + step, 1), :] = tokens_grad[PATCHES : PATCHES + 1]
        small_ref[sums : sums + 1, :] += column_sum(joined[:, :feature].astype(F32))
        small_ref[sums + 1 : sums + 2, :] += column_sum(joined[:, 2 * feature :].astype(F32))
        small_ref[sums + 2 : sums + 3, :] += column_sum(hidden_grad * normed)
        small_ref[sums + 3 : sums + 4, :] += column_sum(hidden_grad)
        if final:
            joined_s = refs[-1]
            joined_s[pl.ds(pl.multiple_of(step * KEY_ROWS, 16), KEY_ROWS), :] = joined

        @pl.when(step == count - 1)
        def _():
            live = count * KEY_ROWS
            rows_s[:, live:, :] = jnp.zeros((rows_s.shape[0], rows_s.shape[1] - live, LANES), F32)
            sources, size, _ = frame_grad_ref.shape
            rows = rows_s.shape[1] // sources
            for source in range(sources):
                for col in range(rows_s.shape[0]):
                    frame_grad_ref[source, :rows, col * LANES : (col + 1) * LANES] = rows_s[
                        col, source * rows : (source + 1) * rows, :
                    ].astype(BF16)
            if final:
                extra = jnp.concatenate([small_ref[:sums, :], jnp.zeros((size - rows - sums, feature), F32)])
                for source in range(sources):
                    frame_grad_ref[source, rows:, :] = extra.astype(BF16)

    if not final:
        return
    outs = refs[3:-2]
    joined_s = refs[-1]
    across = feature // LANES

    for block in range(3):

        @pl.when(step == count + block)
        def _(block=block):
            cols = slice(block * feature, (block + 1) * feature)
            split = len(others) * count * KEY_ROWS
            grad = dot_tn(hidden_ref[split:, :], joined_s[:, cols])
            for part, other in enumerate(others):
                size = count * KEY_ROWS
                grad = grad + dot_tn(hidden_ref[part * size : (part + 1) * size, :], other[:, cols])
            if packed:
                store_share(grad, outs[0], outs[1], table_ref, vids, block * across)
            else:
                outs[0][block] = grad

    @pl.when(step == count + 3)
    def _():
        sums = jnp.concatenate([small_ref[small_ref.shape[0] - 8 :, :], fc_b_ref[...]])
        row = lax.broadcasted_iota(jnp.int32, (sums.shape[0], LANES), 0)
        col = lax.broadcasted_iota(jnp.int32, (sums.shape[0], LANES), 1)
        turned = lax.dot_general(
            sums, jnp.where(row == col, 1.0, 0.0), (((0,), (0,)), ((), ())),
            precision=lax.Precision.HIGHEST, preferred_element_type=F32,
        )
        if packed:
            store_share(turned, outs[0], outs[1], table_ref, vids, 3 * across)
        else:
            outs[0][3] = jnp.concatenate([turned] * across, axis=1)


def sum_kernel(groups, wholes, *refs):
    out_ref = refs[-1]
    at, first = 0, wholes
    for count in groups:
        rows = refs[first].shape[1]
        value = refs[first][...].astype(F32)
        for ref in refs[first + 1 : first + count]:
            value = value + ref[...].astype(F32)
        for ref in refs[:wholes]:
            value = value + ref[:, at : at + rows, :].astype(F32)
        out_ref[:, at : at + rows, :] = value.astype(out_ref.dtype)
        at += rows
        first += count


def final_sum_kernel(terms, share, columns, *refs):
    in_refs, out_refs = refs[:terms], refs[terms:]
    block = 0

    def next_block():
        rows = slice(block * share, (block + 1) * share)
        value = in_refs[0][rows, :].astype(F32)
        for ref in in_refs[1:]:
            value = value + ref[rows, :].astype(F32)
        return value

    for out_ref, shape in zip(out_refs, columns):
        if shape is None:
            turned = jnp.transpose(next_block())
            block += 1
            out_ref[...] = turned[:2]
            for row, vec_ref in enumerate(out_refs[-6:]):
                vec_ref[...] = turned[2 + row]
            out_refs[-7][...] = turned[8 : 8 + out_refs[-7].shape[0]]
            return
        for row in range(shape[0]):
            for col in range(shape[1]):
                out_ref[row * share : (row + 1) * share, col * LANES : (col + 1) * LANES] = next_block()
                block += 1


def resident(shape):
    return pl.BlockSpec(shape, lambda *_: (0,) * len(shape), pipeline_mode=pl.Buffered(1))


def params(mebibytes):
    return pltpu.CompilerParams(vmem_limit_bytes=60 * MIB)


def cost(flops, nbytes, transcendentals=0):
    return pl.CostEstimate(
        flops=10 * int(flops), bytes_accessed=10 * int(nbytes), transcendentals=10 * int(transcendentals)
    )


def with_ready(kernel, at, count):
    def body(*refs):
        kernel(*refs[:at], *refs[at + count :])

    return body


def ready_specs(count):
    return [pl.BlockSpec(memory_space=pl.ANY)] * count


def after(value, ready):
    return lax.optimization_barrier((value, ready))[0]


def add(left, right):
    return (left.astype(F32) + right.astype(F32)).astype(BF16)


def shards(
    vids, toks,
    frames, messages, frame_counts, cotangent,
    msg_gain, msg_shift, msg_in_w, msg_in_b, msg_out_w, msg_out_b,
    ln1_gain, ln1_shift, attn_in_w, attn_in_b, attn_out_w, attn_out_b,
    ln2_gain, ln2_shift, fc_w, fc_b, proj_w, proj_b,
):
    video_count, frame_slots, slots, feature = frames.shape
    devices = vids * toks
    group_frames = video_count * frame_slots
    owned = group_frames // toks
    owners = toks // video_count
    slot_count = slots * toks
    hidden_units = fc_w.shape[1]
    chunks = hidden_units // feature
    share = feature // devices
    vid = lax.axis_index("vid")
    tok = lax.axis_index("tok")
    core = tok % 2
    both = ("vid", "tok")
    depth = toks // 2
    packed = vids == 4 and toks == 8 and share % 8 == 0

    vectors = [msg_gain, msg_shift, msg_out_b, ln1_gain, ln1_shift, attn_out_b, ln2_gain, ln2_shift, proj_b]
    stacked = jnp.stack(vectors + [fc_b[at : at + feature] for at in range(0, hidden_units, feature)])
    stacked = stacked.astype(F32).reshape(-1, 1, feature)

    def row(index):
        return pl.BlockSpec((None, 1, feature), lambda *_: (index, 0, 0))

    def exchange(blocks):
        return lax.all_to_all(blocks, "tok", split_axis=0, concat_axis=0, tiled=True)

    slot_shape = (video_count, slots, frame_slots, feature)
    slot_scratch = pltpu.VMEM((feature // LANES, group_frames * slots, LANES), F32)

    def by_owner(tokens):
        return pl.pallas_call(
            to_owners_kernel,
            grid=(1,),
            in_specs=[resident(slot_shape)],
            out_specs=resident((toks, slots * owned, feature)),
            out_shape=jax.ShapeDtypeStruct((toks, slots * owned, feature), BF16),
            scratch_shapes=[slot_scratch, slot_scratch],
            compiler_params=params(40),
            cost_estimate=cost(0, slots * feature),
            name="to_owners",
        )(tokens.transpose(0, 2, 1, 3))

    def from_owners(blocks, ready=()):
        by_slot, done = pl.pallas_call(
            with_ready(partial(from_owners_kernel, len(blocks)), len(blocks), len(ready)),
            grid=(1,),
            in_specs=[resident(block.shape) for block in blocks] + ready_specs(len(ready)),
            out_specs=[resident(slot_shape), resident((8, LANES))],
            out_shape=[jax.ShapeDtypeStruct(slot_shape, BF16), jax.ShapeDtypeStruct((8, LANES), F32)],
            scratch_shapes=[
                pltpu.VMEM((feature // LANES, toks * max(block.shape[1] for block in blocks), LANES), F32),
                slot_scratch,
            ],
            compiler_params=params(40),
            cost_estimate=cost(0, slots * feature),
            name="from_owners",
        )(*blocks, *ready)
        return by_slot.transpose(0, 2, 1, 3), done

    def swap(rows, axis, size, bit):
        return lax.ppermute(rows, axis, [(i, i ^ bit) for i in range(size)])

    def over_levels(rows):
        return [rows] + [swap(rows, "tok", toks, 2 * step) for step in range(1, depth)]

    def in_order(rows):
        rows = rows.reshape((2, depth) + rows.shape[2:]).swapaxes(0, 1)
        rows = rows.reshape((toks,) + rows.shape[2:])
        bit = 1
        while bit < toks:
            pairs = rows.reshape((toks // (2 * bit), 2, bit) + rows.shape[1:])
            turned = jnp.where((tok // bit) % 2 == 1, pairs[:, ::-1], pairs)
            rows = turned.reshape(rows.shape)
            bit *= 2
        return rows

    group_index = jnp.arange(group_frames, dtype=jnp.int32)
    live_group = group_index % frame_slots < jnp.repeat(frame_counts, frame_slots)
    piece = messages.shape[-1]
    width = (piece + 1 + 127) // 128 * 128
    payload = jnp.concatenate(
        [
            messages.reshape(group_frames, piece),
            live_group.astype(BF16)[:, None],
            jnp.zeros((group_frames, width - piece - 1), BF16),
        ],
        axis=1,
    )
    x_blocks = by_owner(frames)
    levels = over_levels(after(payload, x_blocks))
    x_blocks = exchange(after(x_blocks, levels))
    gathered = jnp.stack(levels)
    gathered = in_order(jnp.stack([gathered, swap(gathered, "tok", toks, 1)]))[None]
    bit = 1
    while bit < vids:
        gathered = jnp.concatenate([gathered, swap(gathered, "vid", vids, bit)])
        bit *= 2
    message_rows = vids * group_frames
    message_all = gathered[..., :piece].transpose(0, 2, 1, 3).reshape(message_rows, feature)
    live_all = gathered[:, 0, :, piece].reshape(message_rows) > 0.5
    row_video = jnp.arange(message_rows, dtype=jnp.int32) // frame_slots
    allowed = ((row_video[:, None] == row_video[None, :]) & live_all[None, :]).astype(F32)

    joined, mixed, message_new = pl.pallas_call(
        message_forward_kernel,
        grid=(1,),
        in_specs=[
            resident((message_rows, feature)),
            resident((message_rows, message_rows)),
            row(0),
            row(1),
            resident((feature, 3 * feature)),
            resident((2, feature)),
            resident((feature, feature)),
            row(2),
        ],
        out_specs=[
            resident((message_rows, 3 * feature)),
            resident((message_rows, feature)),
            resident((message_rows, feature)),
        ],
        out_shape=(
            jax.ShapeDtypeStruct((message_rows, 3 * feature), BF16),
            jax.ShapeDtypeStruct((message_rows, feature), BF16),
            jax.ShapeDtypeStruct((message_rows, feature), F32),
        ),
        compiler_params=params(40),
        cost_estimate=cost(8 * message_rows * feature * feature, 8 * feature * feature),
        name="message_forward",
    )(
        message_all, allowed, stacked, stacked, msg_in_w, msg_in_b, msg_out_w, stacked,
    )
    cot_blocks = exchange(after(by_owner(cotangent), (x_blocks, message_new)))
    own_new = lax.dynamic_slice(message_new, (tok * owned, 0), (owned, feature)).reshape(owned, 1, feature)

    rows = owned * slot_count
    live_rows = owned * KEY_ROWS
    blocks_shape = (toks, slots * owned, feature)
    columns_shape = (feature // LANES, rows, LANES)

    def by_frame(*tail):
        return pl.BlockSpec((1,) + tail, lambda f, *_: (f,) + (0,) * len(tail))

    query, keyval, attended, lse, resid, tokens, hidden_kv = pl.pallas_call(
        partial(attention_forward_kernel, owned),
        grid=(owned,),
        in_specs=[
            resident(blocks_shape),
            by_frame(1, feature),
            row(3),
            row(4),
            resident((feature, 3 * feature)),
            resident((2, feature)),
            resident((feature, feature)),
            row(5),
        ],
        out_specs=[
            by_frame(slot_count, feature),
            by_frame(KEY_ROWS, 2 * feature),
            by_frame(slot_count, feature),
            by_frame(HEADS, slot_count),
            by_frame(slot_count, feature),
            by_frame(KEY_ROWS, feature),
            by_frame(KEY_ROWS, feature),
        ],
        out_shape=(
            jax.ShapeDtypeStruct((owned, slot_count, feature), BF16),
            jax.ShapeDtypeStruct((owned, KEY_ROWS, 2 * feature), BF16),
            jax.ShapeDtypeStruct((owned, slot_count, feature), BF16),
            jax.ShapeDtypeStruct((owned, HEADS, slot_count), F32),
            jax.ShapeDtypeStruct((owned, slot_count, feature), F32),
            jax.ShapeDtypeStruct((owned, KEY_ROWS, feature), F32),
            jax.ShapeDtypeStruct((owned, KEY_ROWS, feature), BF16),
        ),
        scratch_shapes=[pltpu.VMEM(columns_shape, F32)],
        compiler_params=params(40),
        cost_estimate=cost(10 * rows * feature * feature, 12 * rows * feature, rows * slot_count * HEADS),
        name="attention_forward",
    )(
        x_blocks, own_new, stacked, stacked, attn_in_w, attn_in_b, attn_out_w, stacked,
    )

    out_blocks, hidden_low, act, slope = pl.pallas_call(
        feed_forward_kernel,
        grid=(chunks,),
        in_specs=[
            resident((owned, slot_count, feature)),
            row(6),
            row(7),
            pl.BlockSpec((feature, feature), lambda j: (0, j)),
            pl.BlockSpec((None, 1, feature), lambda j: (9 + j, 0, 0)),
            pl.BlockSpec((feature, feature), lambda j: (j, 0)),
            row(8),
        ],
        out_specs=[
            resident(blocks_shape),
            resident((live_rows, feature)),
            pl.BlockSpec((live_rows, feature), lambda j: (0, j)),
            pl.BlockSpec((live_rows, feature), lambda j: (0, j)),
        ],
        out_shape=(
            jax.ShapeDtypeStruct(blocks_shape, BF16),
            jax.ShapeDtypeStruct((live_rows, feature), BF16),
            jax.ShapeDtypeStruct((live_rows, hidden_units), BF16),
            jax.ShapeDtypeStruct((live_rows, hidden_units), BF16),
        ),
        scratch_shapes=[
            pltpu.VMEM((rows, feature), BF16),
            pltpu.VMEM((rows, feature), F32),
            pltpu.VMEM(columns_shape, F32),
        ],
        compiler_params=params(48),
        cost_estimate=cost(4 * rows * feature * hidden_units, 12 * feature * hidden_units, rows * hidden_units),
        name="feed_forward",
    )(
        resid, stacked, stacked, fc_w, stacked, proj_w, stacked,
    )
    output_blocks = exchange(after(out_blocks, cot_blocks))

    own_index = tok * owned + jnp.arange(owned, dtype=jnp.int32)
    own_count = jnp.sum(
        jnp.where(
            (own_index // frame_slots)[:, None] == jnp.arange(video_count, dtype=jnp.int32)[None, :],
            frame_counts[None, :],
            0,
        ),
        axis=1,
    )
    own_live = (own_index % frame_slots < own_count).astype(jnp.int32)

    dest = jnp.arange(vids, dtype=jnp.int32)

    def slot_table(for_core):
        low_bit, high_bit = dest % 2 ^ vid % 2, dest // 2 ^ vid // 2
        return jnp.where(for_core == 0, 2 * low_bit + high_bit, 2 * high_bit + low_bit)

    level = tok // 2
    swapped = (level % 2) * (depth // 2) + level // 2
    table = jnp.concatenate([slot_table(core), slot_table(1 - core), core[None], swapped[None]]).astype(jnp.int32)

    def cross(bit_of_core):
        return [
            (v * toks + t, (v ^ bit_of_core[t % 2]) * toks + t) for v in range(vids) for t in range(toks)
        ]

    def send_over(stage, value):
        if stage == 0:
            return swap(value, "tok", toks, 1)
        if stage == 1:
            return lax.ppermute(value, both, cross((1, 2)))
        return lax.ppermute(value, both, cross((2, 1)))

    def sum_slots(parts, wholes, first, count, ready, dtype=BF16):
        batch = next(size for size in (4, 2, 1) if count % size == 0 and (size == 1 or count > size or len(parts) > 1))
        batch = min(batch, 2) if len(parts) > 1 else batch
        operands = list(wholes) + [term for terms in parts for term in terms]
        rows = sum(terms[0].shape[1] for terms in parts)
        return pl.pallas_call(
            with_ready(
                partial(sum_kernel, [len(terms) for terms in parts], len(wholes)), len(operands), len(ready)
            ),
            grid=(count // batch,),
            in_specs=[
                pl.BlockSpec((batch,) + term.shape[1:], lambda i: (first // batch + i, 0, 0)) for term in operands
            ]
            + ready_specs(len(ready)),
            out_specs=pl.BlockSpec((batch, rows, LANES), lambda i: (i, 0, 0)),
            out_shape=jax.ShapeDtypeStruct((count, rows, LANES), dtype),
            compiler_params=params(40),
            cost_estimate=cost(0, rows * LANES),
            name="sum_slots",
        )(*operands, *ready)

    class Sum:
        def __init__(self, *grads):
            self.parts = [[keep.reshape(keep.shape[0] * keep.shape[1], -1, LANES)] for keep, _ in grads]
            self.got = [send_over(0, send.reshape(vids * depth, -1, LANES)) for _, send in grads]
            self.slots = vids * depth
            self.stage = 0

        def step(self, *ready):
            self.stage += 1
            if self.stage == 1:
                self.parts = [terms + [got] for terms, got in zip(self.parts, self.got)]
                self.whole = []
            else:
                self.whole = self.whole + self.got
            if self.stage == 3:
                value = sum_slots(self.parts, self.whole, 0, depth, ready)
                self.whole, self.parts = [value[0]], []
                steps = [(at % 2) * (depth // 2) + at // 2 for at in range(depth)]
                self.got = [swap(value[at], "tok", toks, 2 * steps[at]) for at in range(1, depth)]
                return value
            self.slots //= 2
            send = sum_slots(self.parts, self.whole, self.slots, self.slots, ready)
            self.got = [send_over(self.stage, send)]
            return send

        def end(self, shapes, *ready):
            operands = self.whole + self.got
            out_shape = []
            for shape in shapes:
                if shape is None:
                    sizes = [(2, share), (chunks, share)] + [(share,)] * 6
                else:
                    sizes = [(shape[0] * share, shape[1] * LANES)]
                out_shape += [jax.ShapeDtypeStruct(size, F32) for size in sizes]
            return pl.pallas_call(
                with_ready(partial(final_sum_kernel, len(operands), share, shapes), len(operands), len(ready)),
                grid=(1,),
                in_specs=[resident(term.shape) for term in operands] + ready_specs(len(ready)),
                out_specs=[resident(out.shape) for out in out_shape],
                out_shape=out_shape,
                compiler_params=params(40),
                cost_estimate=cost(0, feature * LANES),
                name="final_sum",
            )(*operands, *ready)

    half = (vids, depth)
    across = feature // LANES
    columns = feature // across

    def packed_out(*tail):
        return [jax.ShapeDtypeStruct(half + tail, BF16)] * 2

    if packed:
        proj_specs = [
            pl.BlockSpec(
                (1, depth, across * chunks, share, columns),
                lambda j, table, live, base=base: (table[base + jnp.minimum(j, chunks - 1)], 0, 0, 0, 0),
            )
            for base in (0, vids)
        ]
        proj_shapes = packed_out(across * chunks, share, columns)
        fc_specs = [pl.BlockSpec(half + (across, share, columns), lambda j, *_: (0, 0, j, 0, 0)) for _ in range(2)]
        fc_shapes = packed_out(across * (chunks + 1), share, columns)
    else:
        proj_specs = [pl.BlockSpec((feature, feature), lambda j, *_: (jnp.minimum(j, chunks - 1), 0))]
        proj_shapes = [jax.ShapeDtypeStruct((hidden_units, feature), F32)]
        fc_specs = [pl.BlockSpec((1, feature, feature), lambda j, *_: (j, 0, 0))]
        fc_shapes = [jax.ShapeDtypeStruct((chunks + 1, feature, feature), F32)]
    small_rows = owned + 8

    def chunk(index):
        return jnp.minimum(index, chunks - 1)

    def frame_of(index):
        return jnp.minimum(index, owned - 1)

    resid_grad, mixed_grad, small, fc_b_part, *ff_grads = pl.pallas_call(
        partial(feed_backward_kernel, packed, vids),
        grid_spec=pltpu.PrefetchScalarGridSpec(
            num_scalar_prefetch=2,
            grid=(max(chunks, owned) + 1,),
            in_specs=[
                resident(blocks_shape),
                pl.BlockSpec((1, slot_count, feature), lambda j, *_: (frame_of(j), 0, 0)),
                resident((live_rows, feature)),
                pl.BlockSpec((live_rows, feature), lambda j, *_: (0, chunk(j))),
                pl.BlockSpec((live_rows, feature), lambda j, *_: (0, chunk(j))),
                pl.BlockSpec((1, slot_count, feature), lambda j, *_: (frame_of(j), 0, 0)),
                row(6),
                pl.BlockSpec((feature, feature), lambda j, *_: (0, chunk(j))),
                pl.BlockSpec((feature, feature), lambda j, *_: (chunk(j), 0)),
                resident((feature, feature)),
            ],
            out_specs=[
                resident((owned, KEY_ROWS, feature)),
                resident((owned, KEY_ROWS, feature)),
                resident((small_rows, feature)),
                resident((chunks, feature)),
            ]
            + proj_specs
            + fc_specs,
            scratch_shapes=[
                pltpu.VMEM((live_rows, feature), BF16),
                pltpu.VMEM((live_rows, feature), BF16),
                pltpu.VMEM((live_rows, feature), F32),
                pltpu.VMEM((live_rows, feature), BF16),
                pltpu.VMEM((live_rows, feature), F32),
                pltpu.VMEM((live_rows, feature), BF16),
                pltpu.VMEM(columns_shape, F32),
            ],
        ),
        out_shape=[
            jax.ShapeDtypeStruct((owned, KEY_ROWS, feature), F32),
            jax.ShapeDtypeStruct((owned, KEY_ROWS, feature), BF16),
            jax.ShapeDtypeStruct((small_rows, feature), F32),
            jax.ShapeDtypeStruct((chunks, feature), F32),
        ]
        + proj_shapes
        + fc_shapes,
        compiler_params=params(48),
        cost_estimate=cost(8 * rows * feature * hidden_units, 12 * feature * hidden_units),
        name="feed_backward",
    )(
        table, own_live, cot_blocks, resid, hidden_low, act, slope, attended, stacked, fc_w, proj_w, attn_out_w,
    )
    proj_grads, fc_grads = ff_grads[: len(proj_shapes)], ff_grads[len(proj_shapes) :]

    parts = 2 if owned % 2 == 0 else 1
    part_frames = owned // parts
    part_blocks = (toks, slots * part_frames, feature)

    if packed:
        attn_specs = [resident(half + (across * 3 + 1, share, columns))] * 2
        attn_shapes = packed_out(across * 3 + 1, share, columns)
    else:
        attn_specs = [resident((4, feature, feature))]
        attn_shapes = [jax.ShapeDtypeStruct((4, feature, feature), F32)]
    part_rows = part_frames * KEY_ROWS

    def attention_backward(part, small, others, ready):
        first = part * part_frames
        final = part == parts - 1

        def by_part(*tail):
            return pl.BlockSpec(
                (1,) + tail, lambda f, *_: (first + jnp.minimum(f, part_frames - 1),) + (0,) * len(tail)
            )

        extra, extra_specs, scratch = [], [], []
        out_blocks = part_blocks
        if final:
            out_blocks = (toks, slots * part_frames + (owned + 7) // 8 * 8, feature)
            extra = [hidden_kv.reshape(live_rows, feature), fc_b_own] + others
            extra_specs = [resident((live_rows, feature)), resident((chunks, feature))]
            extra_specs += [resident((part_rows, 3 * feature))] * len(others)
            scratch = [pltpu.VMEM((part_rows, 3 * feature), BF16)]
        return pl.pallas_call(
            with_ready(
                partial(attention_backward_kernel, packed, vids, first, part_frames, final),
                10 + len(extra),
                len(ready),
            ),
            grid_spec=pltpu.PrefetchScalarGridSpec(
                num_scalar_prefetch=1,
                grid=(part_frames + 4 * final,),
                in_specs=[
                    by_part(KEY_ROWS, feature),
                    by_part(slot_count, feature),
                    by_part(KEY_ROWS, 2 * feature),
                    by_part(HEADS, slot_count),
                    by_part(KEY_ROWS, feature),
                    by_part(KEY_ROWS, feature),
                    row(3),
                    resident((feature, 3 * feature)),
                    resident((small_rows, feature)),
                ]
                + extra_specs
                + ready_specs(len(ready)),
                out_specs=[
                    resident(out_blocks),
                    pl.BlockSpec(
                        (1, KEY_ROWS, 3 * feature), lambda f, *_: (jnp.minimum(f, part_frames - 1), 0, 0)
                    ),
                    resident((small_rows, feature)),
                ]
                + attn_specs * final,
                scratch_shapes=[pltpu.VMEM((feature // LANES, part_frames * slot_count, LANES), F32)] + scratch,
            ),
            out_shape=[
                jax.ShapeDtypeStruct(out_blocks, BF16),
                jax.ShapeDtypeStruct((part_frames, KEY_ROWS, 3 * feature), BF16),
                jax.ShapeDtypeStruct((small_rows, feature), F32),
            ]
            + attn_shapes * final,
            compiler_params=params(40),
            cost_estimate=cost(16 * rows * feature * feature // parts, 20 * rows * feature // parts),
            name="attention_backward",
        )(table, tokens, query, keyval, lse, mixed_grad, resid_grad, stacked, attn_in_w, small, *extra, *ready)

    if packed:
        ff_sum = Sum(fc_grads, proj_grads)
    ready = [output_blocks]
    fc_b_own = fc_b_part.reshape(devices, chunks, share).swapaxes(0, 1).reshape(chunks, feature)
    frame_blocks, joined_grads = [], []
    for part in range(parts):
        blocks, joined_grad, small, *attn_grads = attention_backward(part, small, joined_grads, ready)
        joined_grads.append(joined_grad.reshape(part_rows, 3 * feature))
        if packed and part == 0:
            ready = [ff_sum.step(small)]
            blocks = after(blocks, ready)
        frame_blocks.append(exchange(blocks))
    ready = small
    if packed:
        attn_sum = Sum(after(attn_grads, frame_blocks[: parts - 1]))
        ready = ff_sum.step(small)
        ready = attn_sum.step(ready)
    output, ready = from_owners([output_blocks], [ready])
    message_low = pl.pallas_call(
        with_ready(partial(last_rows_kernel, slots * part_frames), 1, 1),
        grid=(1,),
        in_specs=[resident(frame_blocks[-1].shape)] + ready_specs(1),
        out_specs=resident((toks, owned, feature)),
        out_shape=jax.ShapeDtypeStruct((toks, owned, feature), BF16),
        cost_estimate=cost(0, toks * feature),
        name="last_rows",
    )(frame_blocks[-1], ready)
    if packed:
        ready = ff_sum.step(message_low)
        ready = attn_sum.step(ready)
    message_low = message_low.reshape(group_frames, feature)
    bit = 1
    while bit < vids:
        message_low = message_low if bit == 1 else after(message_low, ready)
        message_low = jnp.concatenate([message_low, swap(message_low, "vid", vids, bit)])
        bit *= 2
    if packed:
        ready = attn_sum.step(message_low)
    frames_grad, done = from_owners(frame_blocks, [ready])

    place = (vid * toks + tok) * share
    message_grad, msg_in_w_grad, msg_out_w_grad, *msg_vec = pl.pallas_call(
        with_ready(message_backward_kernel, 10, 1),
        grid_spec=pltpu.PrefetchScalarGridSpec(
            num_scalar_prefetch=1,
            grid=(1,),
            in_specs=[
                resident((message_rows, feature)),
                resident((message_rows, message_rows)),
                resident((message_rows, feature)),
                resident((message_rows, 3 * feature)),
                resident((message_rows, feature)),
                row(0),
                row(1),
                resident((feature, 3 * feature)),
                resident((feature, feature)),
            ]
            + ready_specs(1),
            out_specs=[
                resident((message_rows, feature)),
                resident((share, 3 * feature)),
                resident((share, feature)),
                resident((share,)),
                resident((share,)),
                resident((2, share)),
                resident((share,)),
            ],
            scratch_shapes=[
                pltpu.VMEM((message_rows, feature), BF16),
                pltpu.VMEM((message_rows, 3 * feature), BF16),
            ],
        ),
        out_shape=(
            jax.ShapeDtypeStruct((message_rows, feature), BF16),
            jax.ShapeDtypeStruct((share, 3 * feature), F32),
            jax.ShapeDtypeStruct((share, feature), F32),
            jax.ShapeDtypeStruct((share,), F32),
            jax.ShapeDtypeStruct((share,), F32),
            jax.ShapeDtypeStruct((2, share), F32),
            jax.ShapeDtypeStruct((share,), F32),
        ),
        compiler_params=params(40),
        cost_estimate=cost(message_rows * feature, message_rows * feature),
        name="message_backward",
    )(
        place[None].astype(jnp.int32), message_all, allowed, message_low, joined, mixed,
        stacked, stacked, msg_in_w, msg_out_w, done,
    )
    messages_grad = lax.dynamic_slice(message_grad, (0, tok * piece), (group_frames, piece)).reshape(
        messages.shape
    )

    def scatter(grad):
        return lax.psum_scatter(grad, both, scatter_dimension=0, tiled=True)

    if packed:
        shapes = [(1, across * chunks), (1, across), (chunks, across)]
        fc_w_grad, attn_out_w_grad, proj_w_grad = ff_sum.end(shapes, done, messages_grad)
        attn_in_w_grad, in_b_grad, fc_b_grad, *vec_grads = attn_sum.end([(1, 3 * across), None])
    else:
        proj_w_grad = scatter(proj_grads[0])
        fc_w_grad = scatter(fc_grads[0][:chunks].transpose(1, 0, 2).reshape(feature, hidden_units))
        attn_out_w_grad = scatter(fc_grads[0][chunks])
        attn_in_w_grad = scatter(attn_grads[0][:3].transpose(1, 0, 2).reshape(feature, 3 * feature))
        own_vec = scatter(attn_grads[0][3, :, :LANES]).T
        in_b_grad, fc_b_grad, vec_grads = own_vec[:2], own_vec[8 : 8 + chunks], list(own_vec[2:8])
    fc_b_grad = fc_b_grad.reshape(-1)

    return (
        output,
        frames_grad,
        messages_grad,
        msg_vec[0],
        msg_vec[1],
        msg_in_w_grad,
        msg_vec[2],
        msg_out_w_grad,
        msg_vec[3],
        vec_grads[0],
        vec_grads[1],
        attn_in_w_grad,
        in_b_grad,
        attn_out_w_grad,
        vec_grads[4],
        vec_grads[2],
        vec_grads[3],
        fc_w_grad,
        fc_b_grad,
        proj_w_grad,
        vec_grads[5],
    )


def solution(mesh):
    tokens = P("vid", None, "tok", None)
    rows, columns, one = P(("vid", "tok"), None), P(None, ("vid", "tok")), P(("vid", "tok"))
    in_specs = (tokens, P("vid", None, "tok"), P("vid"), tokens) + (P(),) * 18
    out_specs = (
        tokens, tokens, P("vid", None, "tok"),
        one, one, rows, columns, rows, one,
        one, one, rows, columns, rows, one,
        one, one, rows, one, rows, one,
    )
    return jax.shard_map(
        partial(shards, mesh.shape["vid"], mesh.shape["tok"]),
        mesh=mesh,
        in_specs=in_specs,
        out_specs=out_specs,
        check_vma=False,
    )
```
